32 devices in a mesh: group: 2 (over y), tile: 4 (over z), sect: 2 (over x), sub: 2 (over core).
Axes of the slice: x: 2, y: 2, z: 4, core: 2. Of those that a mesh axis runs over, the one named last changes fastest.
Arguments:
- air_state: float32 [4, 80, 64, 256], P(None, ('sect', 'sub'), ('group', 'tile')), parts along dimension 2, may hold values from -3 to 3
- fire_level: float32 [640, 2560], P(('group', 'tile'), ('sect', 'sub')), parts along dimension 0, may hold values from 0.2 to 3
- fuel_left: float32 [640, 2560], P(('group', 'tile'), ('sect', 'sub')), parts along dimension 0, may hold values from 0.3 to 1
- fuel_class: int32 [640, 2560], P(('group', 'tile'), ('sect', 'sub')), parts along dimension 0, may hold values from 0 to 12
- ignition: int32 [640, 2560], P(('group', 'tile'), ('sect', 'sub')), parts along dimension 0, may hold values from 0 to 4, as said below
- plan: int32 [4], replicated, may hold values from 1 to 3
- spread_rate: float32 [13], replicated, may hold values from 0.05 to 0.3
- burn_time: float32 [13], replicated, may hold values from 0.5 to 8
- heat_content: float32 [13], replicated, may hold values from 1 to 10
- moisture_content: float32 [13], replicated, may hold values from 0.1 to 1
Outputs:
- air_out: float32 [4, 80, 64, 256], P(None, ('sect', 'sub'), ('group', 'tile')), parts along dimension 2
- level_out: float32 [640, 2560], P(('group', 'tile'), ('sect', 'sub')), parts along dimension 0
- fuel_out: float32 [640, 2560], P(('group', 'tile'), ('sect', 'sub')), parts along dimension 0
The draws below stay inside these ranges and needn't reach their ends.
There are 2 independent parts, one for each index of `group`. The reference program is written for one: setup_inputs(seed, part) draws one part's arguments, and reference() takes and returns one part's arrays. A program takes and returns all parts, laid end to end along the dimension named above; an argument that names none is the same for every part. Nothing has to cross between parts.
Inputs may be any that keep to these rules, and one draw needn't show every extreme that they name: `ignition`: A cell with value c is ignited at the start of coupling step c; cells with value 4 are not ignited in the window. Ignited cells lie in scattered atmosphere columns. The plan is shared by all scenarios.
All inputs are finite; a program needn't handle non-finite values.
Results may differ from the reference program's by a relative error of at most 0.0001.
Values sent between devices are 32-bit elements; how exact they have to be, the bound alone decides.
A program may use at most 128 MiB of HBM per device.

```python
import math
import jax
import jax.numpy as jnp
import numpy as np
from jax import lax

LEVELS = 80
REFINE = 10
NFUEL = 13
STEPS = 4
SUBSTEPS = 4
NX = 32
NY = 256
FIRE_X = 320
FIRE_Y = 2560


def draw_ignition(key, part):
    first_key, second_key, third_key = jax.random.split(key, 3)
    active = jax.random.randint(first_key, (NX, NY), 0, 8) == 0
    ignite_at = jax.random.randint(second_key, (NX, NY), 0, STEPS)
    coarse_map = jnp.where(active, ignite_at, STEPS)
    fine_map = jnp.repeat(jnp.repeat(coarse_map, REFINE, axis=0), REFINE, axis=1)
    chosen = jax.random.randint(third_key, (FIRE_X, FIRE_Y), 0, 4) == 0
    return jnp.where(chosen, fine_map, STEPS).astype(jnp.int32)


def place_ends(values, rng, smallest, top_value):
    dims = values.shape
    place = [jax.random.randint(jax.random.fold_in(rng, axis), (), 0, dims[axis]) for axis in range(len(dims))]
    values = values.at[tuple(place)].set(smallest)
    longest = dims.index(max(dims))
    place[longest] = (place[longest] + 1) % dims[longest]
    return values.at[tuple(place)].set(top_value)


def levels(own_key, dims, shards, least, largest):
    def one(position, shards_of):
        steps = jax.random.uniform(jax.random.fold_in(jax.random.fold_in(own_key, 6), position), (shards_of,), jnp.float32, least / len(shards), largest / len(shards))
        return jnp.repeat(jnp.exp(steps), dims[position] // shards_of).reshape((-1,) + (1,) * (len(dims) - position - 1))

    loudness = one(*shards[0])
    for cut in shards[1:]:
        loudness = loudness * one(*cut)
    return loudness


def rank_table(count, lean):
    portions = [(1 << 20) // math.isqrt(grade ** lean) + 1 for grade in range(1, count + 1)]
    deviation = 1 + sum(portions) // (1 << 30)
    return np.cumsum(np.array([max(1, weight // deviation) for weight in portions]))


def ranked_ids(rng, dims, amount, lean):
    listing = rank_table(amount, lean)
    ticket = jax.random.randint(jax.random.fold_in(rng, 1), dims, 0, int(listing[amount - 1]))
    standing = jnp.searchsorted(jnp.asarray(listing, jnp.int32), ticket, side="right")
    return jax.random.permutation(jax.random.fold_in(rng, 2), amount)[standing].astype(jnp.int32)


def centred(own_key, extent, deviation, reach, cuts=(), dtype=jnp.bfloat16):
    drawn = deviation * jax.random.normal(own_key, extent, jnp.float32)
    if cuts:
        drawn = drawn * levels(own_key, extent, cuts, -0.22, 0.18)
    return jnp.clip(drawn, -reach, reach).astype(dtype)


def setup_inputs(seed: int = 0, part: int = 0) -> dict:
    arg_keys = jax.random.split(jax.random.key(seed), 11)
    own_keys = jax.random.split(jax.random.fold_in(arg_keys[10], part), 11)
    air_state = centred(own_keys[0], (4, LEVELS, NX, NY), 1.0, 3.0, ((1, 4), (2, 4)), jnp.float32)
    fire_level = jnp.clip(0.2 + 2.8 * jax.random.uniform(own_keys[1], (FIRE_X, FIRE_Y), jnp.float32) ** levels(own_keys[1], (FIRE_X, FIRE_Y), ((0, 4), (1, 4)), -0.2, 0.2), 0.2, 3.0)
    fuel_left = jnp.clip(0.3 + 0.7 * jax.random.uniform(own_keys[2], (FIRE_X, FIRE_Y), jnp.float32) ** levels(own_keys[2], (FIRE_X, FIRE_Y), ((0, 4), (1, 4)), -0.2, 0.2), 0.3, 1.0)
    fuel_class = place_ends(ranked_ids(own_keys[3], (FIRE_X, FIRE_Y), NFUEL, 2), jax.random.fold_in(own_keys[3], 3), 0, NFUEL - 1).astype(jnp.int32)
    ignition = draw_ignition(jax.random.fold_in(jax.random.fold_in(arg_keys[10], part), 71), part)
    plan = place_ends(jax.random.randint(arg_keys[5], (STEPS,), 1, 4), jax.random.fold_in(arg_keys[5], 1), 1, 3).astype(jnp.int32)
    spread_rate = jnp.clip(jnp.exp(jax.random.uniform(arg_keys[6], (NFUEL,), jnp.float32, math.log(0.05), math.log(0.3))), 0.05, 0.3)
    burn_time = jnp.clip(jnp.exp(jax.random.uniform(arg_keys[7], (NFUEL,), jnp.float32, math.log(0.5), math.log(8.0))), 0.5, 8.0)
    heat_content = jnp.clip(jnp.exp(jax.random.uniform(arg_keys[8], (NFUEL,), jnp.float32, math.log(1.0), math.log(10.0))), 1.0, 10.0)
    moisture_content = jnp.clip(jnp.exp(jax.random.uniform(arg_keys[9], (NFUEL,), jnp.float32, math.log(0.1), math.log(1.0))), 0.1, 1.0)
    return dict(air_state=air_state, fire_level=fire_level, fuel_left=fuel_left, fuel_class=fuel_class, ignition=ignition, plan=plan, spread_rate=spread_rate, burn_time=burn_time, heat_content=heat_content, moisture_content=moisture_content)


air_delta = 0.1
diffusion = 0.2
heat_gain = 20.0
vapour_gain = 20.0
lift_gain = 0.3
wind_gain = 0.5
fire_delta = 0.15

def level_weights(layer_count):
    height = jnp.arange(layer_count).astype(jnp.float32)
    profile = jnp.exp(-2.0 * height / layer_count)
    profile = layer_count * profile / jnp.sum(profile)
    column = jnp.exp(-height / layer_count)
    column = column / jnp.sum(column)
    return (profile, column)

def fire_core(padded, fuel_now, energy, vapour, rate_cell, burnout, heat_cell, moist_cell, wind_east, wind_north, fire_step):
    at_centre = padded[1:-1, 1:-1]
    at_west = padded[:-2, 1:-1]
    at_east = padded[2:, 1:-1]
    at_south = padded[1:-1, :-2]
    at_north = padded[1:-1, 2:]
    steepness = jnp.sqrt(jnp.maximum(at_centre - at_west, 0.0) ** 2 + jnp.minimum(at_east - at_centre, 0.0) ** 2 + jnp.maximum(at_centre - at_south, 0.0) ** 2 + jnp.minimum(at_north - at_centre, 0.0) ** 2)
    grad_east = 0.5 * (at_east - at_west)
    grad_north = 0.5 * (at_north - at_south)
    tailwind = (wind_east * grad_east + wind_north * grad_north) / jnp.sqrt(grad_east * grad_east + grad_north * grad_north + 1.0)
    fire_speed = rate_cell * (1.0 + wind_gain * jnp.maximum(tailwind, 0.0))
    level_set = at_centre - fire_step * fire_speed * steepness
    burning = jnp.clip(0.5 - level_set, 0.0, 1.0)
    remain = fuel_now * jnp.exp(-fire_step * burning / burnout)
    consumed = fuel_now - remain
    return (level_set, remain, energy + consumed * heat_cell, vapour + consumed * moist_cell)

def air_core(padded, flux_coarse, profile):
    at_centre = padded[:, 1:-1, 1:-1, 1:-1]
    at_below = padded[:, :-2, 1:-1, 1:-1]
    at_above = padded[:, 2:, 1:-1, 1:-1]
    at_west = padded[:, 1:-1, :-2, 1:-1]
    at_east = padded[:, 1:-1, 2:, 1:-1]
    at_south = padded[:, 1:-1, 1:-1, :-2]
    at_north = padded[:, 1:-1, 1:-1, 2:]
    speed_east = at_centre[2]
    speed_north = at_centre[3]
    advect = jnp.maximum(speed_east, 0.0) * (at_centre - at_west) + jnp.minimum(speed_east, 0.0) * (at_east - at_centre) + jnp.maximum(speed_north, 0.0) * (at_centre - at_south) + jnp.minimum(speed_north, 0.0) * (at_north - at_centre)
    diffused = at_west + at_east + at_south + at_north + at_below + at_above - 6.0 * at_centre
    lift_east = at_east[0] + 0.6 * at_east[1] - (at_west[0] + 0.6 * at_west[1])
    lift_north = at_north[0] + 0.6 * at_north[1] - (at_south[0] + 0.6 * at_south[1])
    heights = profile[:, None, None]
    forcing = jnp.stack([heat_gain * flux_coarse[0][None] * heights, vapour_gain * flux_coarse[1][None] * heights, 0.5 * lift_gain * lift_east, 0.5 * lift_gain * lift_north])
    return at_centre + air_delta * (diffusion * diffused - advect + forcing)

def coarsen(fine_field, refine_by):
    channels, row_count, col_count = fine_field.shape
    blocks = fine_field.reshape(channels, row_count // refine_by, refine_by, col_count // refine_by, refine_by)
    return lax.optimization_barrier(jnp.sum(blocks, axis=(2, 4))) / (refine_by * refine_by)

def reference(air_state, fire_level, fuel_left, fuel_class, ignition, plan, spread_rate, burn_time, heat_content, moisture_content):
    rate_cell = spread_rate[fuel_class]
    burnout = burn_time[fuel_class]
    heat_cell = heat_content[fuel_class]
    moist_cell = moisture_content[fuel_class]
    profile, column = level_weights(LEVELS)
    air_field = air_state
    level_set = fire_level
    fuel_now = fuel_left
    for coupling in range(STEPS):
        wind_coarse = lax.optimization_barrier(jnp.sum(column[None, :, None, None] * air_field[2:4], axis=1))
        wind_fine = jnp.repeat(jnp.repeat(wind_coarse, REFINE, axis=1), REFINE, axis=2)
        fire_step = plan[coupling].astype(jnp.float32) * fire_delta
        level_set = jnp.where(ignition <= coupling, jnp.minimum(level_set, -1.0), level_set)
        energy = jnp.zeros_like(level_set)
        vapour = jnp.zeros_like(level_set)
        for sub_step in range(SUBSTEPS):
            padded = jnp.pad(level_set, 1, mode='edge')
            level_set, fuel_now, energy, vapour = fire_core(padded, fuel_now, energy, vapour, rate_cell, burnout, heat_cell, moist_cell, wind_fine[0], wind_fine[1], fire_step)
        flux_coarse = coarsen(jnp.stack([energy, vapour]), REFINE)
        padded_air = jnp.pad(air_field, ((0, 0), (1, 1), (1, 1), (1, 1)))
        air_field = air_core(padded_air, flux_coarse, profile)
    return (air_field, level_set, fuel_now)
```

```python
import functools
import math

import jax
import jax.numpy as jnp
from jax import lax
from jax.experimental import pallas as pl
from jax.experimental.pallas import tpu as pltpu
from jax.sharding import PartitionSpec as P

LEVELS = 80
REFINE = 10
NFUEL = 13
STEPS = 4
SUBSTEPS = 4
DEEP = 4
SEG = REFINE // 2
MESH = pl.DeviceIdType.MESH
TINY = 1.1754944e-38
f32 = jnp.float32
bf16 = jnp.bfloat16


def split(value, axis, pieces):
    parts = []
    for _ in range(pieces):
        parts.append(value.astype(bf16))
        value = value - parts[-1].astype(f32)
    return jnp.concatenate(parts, axis=axis)


def indicator(mask, value=1.0):
    return jnp.where(mask, value, 0.0).astype(bf16)


def kernel(
    tiles,
    sects,
    subs,
    air_in,
    level_in,
    fuel_in,
    class_in,
    ign_in,
    plan,
    t_rate,
    t_burn,
    t_heat,
    t_moist,
    air_out,
    level_out,
    fuel_out,
    air,
    xh,
    xa,
    xb,
    rate,
    fuel,
    binv,
    heat,
    moist,
    ign,
    bsum,
    stage,
    turned,
    gather,
    spread,
    wmat,
    smat,
    wnd,
    es,
    gs,
    hb,
    er,
    dg,
    wsend,
    wrecv,
    hsend,
    hrecv,
    fsend,
    frecv,
    in_s,
    out_s,
    fire_s,
    fire_r,
    wind_s,
    wind_r,
    flux_s,
    flux_r,
    halo_s,
    halo_r,
):
    bands = sects * subs
    depth = air_in.shape[1]
    width = air_in.shape[3]
    rows, cols = level_in.shape
    coarse = cols // REFINE
    groups = cols // 128
    tile_at = lax.axis_index("tile")
    sect_at = lax.axis_index("sect")
    sub_at = lax.axis_index("sub")
    band = sect_at * subs + sub_at
    not_first = tile_at > 0
    not_final = tile_at < tiles - 1
    band_low = band > 0
    band_high = band < bands - 1

    def device(tile_step, at_band):
        return {
            "tile": tile_at + tile_step,
            "sect": at_band // subs,
            "sub": at_band % subs,
        }

    def both(a, b):
        return jnp.logical_and(a, b)

    pending = []

    def send(condition, src, dst, send_sem, recv_sem, where):
        def make():
            return pltpu.make_async_remote_copy(
                src_ref=src,
                dst_ref=dst,
                send_sem=send_sem,
                recv_sem=recv_sem,
                device_id=where,
                device_id_type=MESH,
            )

        @pl.when(condition)
        def _():
            make().start()

        pending.append((condition, make))

    def drain():
        for condition, make in pending:

            @pl.when(condition)
            def _(make=make):
                make().wait_send()

        pending.clear()

    def receive(condition, dst, recv_sem, send_sem, where):
        @pl.when(condition)
        def _():
            pltpu.make_async_remote_copy(
                src_ref=dst,
                dst_ref=dst,
                send_sem=send_sem,
                recv_sem=recv_sem,
                device_id=where,
                device_id_type=MESH,
            ).wait_recv()

    def iota(shape, dim):
        return lax.broadcasted_iota(jnp.int32, shape, dim)

    def fetch(array, slot):
        return [
            pltpu.make_async_copy(
                array.at[:, pl.ds(128 * v, 128)], stage.at[slot, v], in_s.at[slot, v]
            )
            for v in range(groups)
        ]

    air_copy = pltpu.make_async_copy(air_in, air.at[0, :, pl.ds(1, depth)], in_s.at[0, groups])
    level_copy, fuel_copy = fetch(level_in, 0), fetch(fuel_in, 1)

    def fetch_int(array, slot):
        return [
            pltpu.make_async_copy(
                array.at[:, pl.ds(128 * v, 128)], turned.at[slot, v], in_s.at[2 + slot, v]
            )
            for v in range(groups)
        ]

    class_copy, ign_copy = fetch_int(class_in, 0), fetch_int(ign_in, 1)
    air_copy.start()
    for copies in (level_copy, class_copy, ign_copy, fuel_copy):
        for copy in copies:
            copy.start()

    hrecv[...] = jnp.zeros_like(hrecv)
    hb[...] = jnp.zeros_like(hb)
    er[...] = jnp.zeros_like(er)
    dg[...] = jnp.zeros_like(dg)

    barrier = pltpu.get_barrier_semaphore()
    for tile_step, condition in ((0, None), (-1, not_first), (1, not_final)):
        for j in range(bands):
            ok = (band != j) if condition is None else condition

            @pl.when(ok)
            def _(tile_step=tile_step, j=j):
                pl.semaphore_signal(
                    barrier, inc=1, device_id=device(tile_step, j), device_id_type=MESH
                )

    spot = iota((16, cols), 1)
    spot = SEG * (spot % 128) + spot // 128
    line16 = iota((16, cols), 0)

    def make_gather(i, carry):
        at = pl.ds(pl.multiple_of(i * 16, 16), 16)
        gather[at, :] = indicator(spot == line16 + 16 * i)
        return carry

    lax.fori_loop(0, cols // 16, make_gather, 0, unroll=4)

    column = iota((16, cols), 1)

    def make_spread(i, carry):
        at = pl.ds(pl.multiple_of(i * 16, 16), 16)
        spread[at, :] = indicator(column == SEG * (line16 + 16 * (i % 8)) + i // 8)
        return carry

    source, place = iota((128, 512), 0), iota((128, 512), 1)
    block, place = place // 128, place % 128
    inner = place % 8 < 4
    first = jnp.where(block == 0, 32 + place // 2, jnp.where(inner, 32, 31))
    second = jnp.where(
        block == 2, jnp.where(inner, 96, 95), jnp.where(place < 64, 31, 96)
    )
    pattern = indicator(source == jnp.where(block < 2, first, second), 0.5)
    wmat[:128, :] = pattern
    wmat[128:, :] = pattern
    source, place = iota((128, 128), 0), iota((128, 128), 1)
    pattern = indicator(place == source // 2 + coarse * (band % 2))
    smat[:128, :] = pattern
    smat[128:, :] = pattern

    sub = iota((8, 128), 0)
    lane = iota((8, 128), 1)
    octet = lane // 8
    inner = lane % 8 < 4
    edge_w = sub == jnp.where(not_first, -1, 0)
    edge_e = sub == jnp.where(not_final, -1, 7)
    edge_s = lane == jnp.where(band_low, -1, 0)
    edge_n = lane == jnp.where(band_high, -1, 127)
    strip_w = both(edge_w, octet == 3)
    strip_e = both(edge_e, octet == 12)

    def rolled(value, shift, axis):
        shift = shift % value.shape[axis]
        return pltpu.roll(value, shift, axis) if shift else value

    row8 = iota((8, width), 0)
    total_col = sum(math.exp(-k / LEVELS) for k in range(LEVELS))
    total_prof = sum(math.exp(-2.0 * k / LEVELS) for k in range(LEVELS))
    col_base = f32(0.0)
    prof_base = f32(0.0)
    for j in range(bands):
        here = band == j
        col_base = jnp.where(here, f32(math.exp(-j * depth / LEVELS) / total_col), col_base)
        prof_base = jnp.where(
            here, f32(LEVELS * math.exp(-2.0 * j * depth / LEVELS) / total_prof), prof_base
        )
    col_ratio = math.exp(-1.0 / LEVELS)
    prof_ratio = math.exp(-2.0 / LEVELS)

    air_copy.wait()

    def first_air(i, carry):
        weight, total_u, total_v = carry
        total_u = total_u + weight * air[0, 2, i + 1]
        total_v = total_v + weight * air[0, 3, i + 1]
        return weight * f32(col_ratio), total_u, total_v

    nothing = jnp.zeros((8, width), f32)
    _, total_u, total_v = lax.fori_loop(
        0, depth, first_air, (col_base, nothing, nothing), unroll=4
    )

    expected = (
        bands - 1 + bands * (not_first.astype(jnp.int32) + not_final.astype(jnp.int32))
    )
    pl.semaphore_wait(barrier, expected)

    def send_wind(c, total_u, total_v):
        stacked = jnp.concatenate([total_u, total_v], axis=0)
        for j in range(bands):
            shift = (128 // 4 - coarse * j) % width
            window = (pltpu.roll(stacked, shift, 1) if shift else stacked)[:, :128]
            wsend[c, j] = window
            for k in range(2):
                low = jnp.broadcast_to(window[8 * k : 8 * k + 1], (8, 128))
                high = jnp.broadcast_to(window[8 * k + 7 : 8 * k + 8], (8, 128))
                hsend[c, j, k] = jnp.where(sub < 4, high, low)

            @pl.when(band == j)
            def _(window=window, j=j):
                wrecv[c, j] = window

        for j in range(bands):
            send(
                band != j,
                wsend.at[c, j],
                wrecv.at[c, band],
                wind_s.at[c, 2, j],
                wind_r.at[c, 2, band],
                device(0, j),
            )
        for way, tile_step, ok in ((0, 1, not_final), (1, -1, not_first)):
            part = pl.ds(4 * way, 4)
            for j in range(bands):
                send(
                    ok,
                    hsend.at[c, j, :, part, :],
                    hrecv.at[c, band, :, part, :],
                    wind_s.at[c, way, j],
                    wind_r.at[c, way, band],
                    device(tile_step, j),
                )

    def wait_wind(c):
        for j in range(bands):
            receive(band != j, wrecv.at[c, j], wind_r.at[c, 2, j], wind_s.at[c, 2, j], device(0, j))
        for way, tile_step, ok in ((0, -1, not_first), (1, 1, not_final)):
            part = pl.ds(4 * way, 4)
            for j in range(bands):
                receive(
                    ok,
                    hrecv.at[c, j, :, part, :],
                    wind_r.at[c, way, j],
                    wind_s.at[c, way, j],
                    device(tile_step, j),
                )
        own = wrecv[c, 0]
        beyond = [hrecv[c, 0, 0], hrecv[c, 0, 1]]
        for j in range(1, bands):
            own = own + wrecv[c, j]
            beyond = [beyond[0] + hrecv[c, j, 0], beyond[1] + hrecv[c, j, 1]]
        together = jnp.concatenate([own] + beyond, axis=0)
        wide = jnp.dot(split(together, 1, 2), wmat[...], preferred_element_type=f32)
        for k in range(2):
            own, beyond = wide[8 * k : 8 * k + 8], wide[16 + 8 * k : 24 + 8 * k]
            wnd[k, 0] = own[:, :128]
            wnd[k, 1] = beyond[:, :128]
            for at in (1, 2):
                here = own[:, 128 * at : 128 * at + 128]
                there = beyond[:, 128 * at : 128 * at + 128]
                below = jnp.where(sub == 0, there, pltpu.roll(here, 1, 0))
                above = jnp.where(sub == 7, there, pltpu.roll(here, 7, 0))
                wnd[k, at + 1] = jnp.where(
                    octet < 3, below, jnp.where(octet >= 13, above, here)
                )
            wnd[k, 4] = beyond[:, 384:]

    def send_air(c):
        send(
            not_final,
            air.at[c, :, pl.ds(1, depth), pl.ds(7, 1), :],
            xh.at[c, 0, :, :, pl.ds(7, 1), :],
            halo_s.at[c, 0],
            halo_r.at[c, 0],
            device(1, band),
        )
        send(
            not_first,
            air.at[c, :, pl.ds(1, depth), pl.ds(0, 1), :],
            xh.at[c, 1, :, :, pl.ds(0, 1), :],
            halo_s.at[c, 1],
            halo_r.at[c, 1],
            device(-1, band),
        )
        send(
            band_high,
            air.at[c, :, depth],
            air.at[c, :, 0],
            halo_s.at[c, 2],
            halo_r.at[c, 2],
            device(0, band + 1),
        )
        send(
            band_low,
            air.at[c, :, 1],
            air.at[c, :, depth + 1],
            halo_s.at[c, 3],
            halo_r.at[c, 3],
            device(0, band - 1),
        )

    def wait_air(c):
        receive(
            not_first,
            xh.at[c, 0, :, :, pl.ds(7, 1), :],
            halo_r.at[c, 0],
            halo_s.at[c, 0],
            device(-1, band),
        )
        receive(
            not_final,
            xh.at[c, 1, :, :, pl.ds(0, 1), :],
            halo_r.at[c, 1],
            halo_s.at[c, 1],
            device(1, band),
        )
        receive(band_low, air.at[c, :, 0], halo_r.at[c, 2], halo_s.at[c, 2], device(0, band - 1))
        receive(
            band_high,
            air.at[c, :, depth + 1],
            halo_r.at[c, 3],
            halo_s.at[c, 3],
            device(0, band + 1),
        )

    send_wind(0, total_u, total_v)
    send_air(0)

    def reorder(load):
        return jnp.concatenate(
            [
                jnp.concatenate([load(v, pl.ds(q, 8, stride=REFINE)) for v in range(groups)], axis=1)
                for q in range(REFINE)
            ],
            axis=0,
        )

    for copy in level_copy + class_copy + ign_copy:
        copy.wait()
    kinds = reorder(
        lambda v, at: (turned[0, v, at, :] + 16 * turned[1, v, at, :]).astype(f32)
    ).astype(bf16)
    pieces = split(reorder(lambda v, at: stage[0, v, at, :]), 0, 3)
    found = jnp.dot(
        jnp.concatenate([pieces, kinds], axis=0), gather[...], preferred_element_type=f32
    )
    together = found[:rows] + found[rows : 2 * rows] + found[2 * rows : 3 * rows]
    kinds = found[3 * rows :]
    for q in range(REFINE):
        for p in range(SEG):
            kind = kinds[8 * q : 8 * q + 8, 128 * p : 128 * p + 128]
            when = jnp.floor(kind * (1.0 / 16.0))
            now = together[8 * q : 8 * q + 8, 128 * p : 128 * p + 128]
            ign[q, p] = when
            moist[q, p] = kind - 16.0 * when
            xa[q + 1, p] = jnp.where(when <= 0.0, jnp.minimum(now, -1.0), now)

    def find_rate(q, carry):
        for p in range(SEG):
            kind = moist[q, p]
            value = jnp.full((8, 128), t_rate[0], f32)
            for k in range(1, NFUEL):
                value = jnp.where(kind == float(k), t_rate[k], value)
            rate[q + 1, p] = value
        return carry

    lax.fori_loop(0, REFINE, find_rate, 0)

    def outline(e, ref):
        def edge(q, found):
            x = [ref[q + 1, p] for p in range(SEG)]
            near = pltpu.roll(x[SEG - 1], 1, 1)
            for k in range(1, DEEP):
                near = jnp.where(lane == k, pltpu.roll(x[SEG - 1 - k], k + 1, 1), near)
            for k in range(DEEP):
                near = jnp.where(lane == 127 - k, pltpu.roll(x[k], 127 - k, 1), near)
            return jnp.where(octet == q + 3, pltpu.roll(near, 8 * q + 28, 1), found)

        found = lax.fori_loop(0, REFINE, edge, jnp.zeros((8, 128), f32), unroll=5)
        es[e] = found
        gs[e, SEG] = jnp.where(
            sub < 4,
            jnp.broadcast_to(found[7:8], (8, 128)),
            jnp.broadcast_to(found[0:1], (8, 128)),
        )

        def border(p, carry):
            value = rolled(ref[REFINE, p], 1, 0)
            for k in range(1, DEEP):
                value = jnp.where(sub == k, rolled(ref[REFINE - k, p], k + 1, 0), value)
            for k in range(DEEP):
                value = jnp.where(sub == 4 + k, rolled(ref[DEEP - k, p], 4 + k, 0), value)
            gs[e, p] = value
            return carry

        lax.fori_loop(0, SEG, border, 0, unroll=5)
        for way, tile_step, ok in ((0, 1, not_final), (1, -1, not_first)):
            part = pl.ds(4 * way, 4)
            send(
                ok,
                gs.at[e, :, part, :],
                hb.at[e, :, part, :],
                fire_s.at[e, way],
                fire_r.at[e, way],
                device(tile_step, band),
            )
        for side, band_step, ok in ((0, 1, band_high), (1, -1, band_low)):
            send(
                ok,
                es.at[e],
                er.at[e, side],
                fire_s.at[e, 2 + side],
                fire_r.at[e, 2 + side],
                device(0, band + band_step),
            )
            for way, tile_step, also in ((0, 1, not_final), (1, -1, not_first)):
                send(
                    both(ok, also),
                    es.at[e, pl.ds(7 - 7 * way, 1), :],
                    dg.at[e, side, pl.ds(7 * way, 1), :],
                    fire_s.at[e, 4 + 2 * side + way],
                    fire_r.at[e, 4 + 2 * side + way],
                    device(tile_step, band + band_step),
                )

    def surround(e, ref):
        for way, tile_step, ok in ((0, -1, not_first), (1, 1, not_final)):
            receive(
                ok,
                hb.at[e, :, pl.ds(4 * way, 4), :],
                fire_r.at[e, way],
                fire_s.at[e, way],
                device(tile_step, band),
            )
        for side, band_step, ok in ((0, -1, band_low), (1, 1, band_high)):
            receive(
                ok,
                er.at[e, side],
                fire_r.at[e, 2 + side],
                fire_s.at[e, 2 + side],
                device(0, band + band_step),
            )
            for way, tile_step, also in ((0, -1, not_first), (1, 1, not_final)):
                receive(
                    both(ok, also),
                    dg.at[e, side, pl.ds(7 * way, 1), :],
                    fire_r.at[e, 4 + 2 * side + way],
                    fire_s.at[e, 4 + 2 * side + way],
                    device(tile_step, band + band_step),
                )
        for p in range(SEG):
            ref[12, p] = hb[e, p]
        mine, beyond = es[e], hb[e, SEG]

        def strip(here, there):
            below = jnp.where(sub == 0, there, pltpu.roll(here, 1, 0))
            above = jnp.where(sub == 7, there, pltpu.roll(here, 7, 0))
            return jnp.where(
                octet < 3,
                pltpu.roll(below, 48, 1),
                jnp.where(octet >= 13, pltpu.roll(above, 80, 1), here),
            )

        low = strip(jnp.where(inner, mine, er[e, 0]), jnp.where(inner, beyond, dg[e, 0]))
        high = strip(jnp.where(inner, er[e, 1], mine), jnp.where(inner, dg[e, 1], beyond))
        mixed = jnp.where(inner, high, low)
        corner = mixed
        for k in range(3):
            corner = jnp.where(sub == k, rolled(rolled(mixed, 108 + 8 * k, 1), k, 0), corner)
            corner = jnp.where(sub == 7 - k, rolled(rolled(mixed, 20 - 8 * k, 1), -k, 0), corner)
        ref[13, 0] = low
        ref[13, 1] = high
        ref[13, 2] = corner

    outline(0, rate)
    outline(1, xa)

    @pl.when(jnp.logical_not(not_first))
    def _():
        def zero(i, carry):
            for c in range(STEPS):
                for f in range(4):
                    xh[c, 0, f, i] = jnp.zeros((8, width), f32)
            return carry

        lax.fori_loop(0, depth, zero, 0)

    @pl.when(jnp.logical_not(not_final))
    def _():
        def zero(i, carry):
            for c in range(STEPS):
                for f in range(4):
                    xh[c, 1, f, i] = jnp.zeros((8, width), f32)
            return carry

        lax.fori_loop(0, depth, zero, 0)

    @pl.when(jnp.logical_not(band_low))
    def _():
        for c in range(STEPS):
            air[c, :, 0] = jnp.zeros((4, 8, width), f32)

    @pl.when(jnp.logical_not(band_high))
    def _():
        for c in range(STEPS):
            air[c, :, depth + 1] = jnp.zeros((4, 8, width), f32)

    def lookup(q, carry):
        for p in range(SEG):
            kind = moist[q, p]
            burn = jnp.full((8, 128), t_burn[0], f32)
            hot = jnp.full((8, 128), t_heat[0], f32)
            wet = jnp.full((8, 128), t_moist[0], f32)
            for k in range(1, NFUEL):
                same = kind == float(k)
                burn = jnp.where(same, t_burn[k], burn)
                hot = jnp.where(same, t_heat[k], hot)
                wet = jnp.where(same, t_moist[k], wet)
            binv[q, p] = 1.0 / burn
            heat[q, p] = hot
            moist[q, p] = wet
            bsum[q, p] = jnp.zeros((8, 128), f32)
        return carry

    lax.fori_loop(0, REFINE, lookup, 0)
    for copy in fuel_copy:
        copy.wait()
    pieces = split(reorder(lambda v, at: stage[1, v, at, :]), 0, 3)
    found = jnp.dot(pieces, gather[...], preferred_element_type=f32)
    together = found[:rows] + found[rows : 2 * rows] + found[2 * rows :]
    for q in range(REFINE):
        for p in range(SEG):
            fuel[q, p] = together[8 * q : 8 * q + 8, 128 * p : 128 * p + 128]
    lax.fori_loop(0, cols // 16, make_spread, 0, unroll=4)

    def uphill(d):
        return jnp.maximum(d, 0.0) * d

    def downhill(d):
        return jnp.minimum(d, 0.0) * d

    def moved(here, dw, de, ds, dn, speed, wu, wv):
        square = (uphill(dw) + downhill(de)) + (uphill(ds) + downhill(dn))
        steep = square * lax.rsqrt(jnp.maximum(square, TINY))
        gx, gy = dw + de, ds + dn
        tail = (wu * gx + wv * gy) * lax.rsqrt(gx * gx + gy * gy + 4.0)
        return here - (speed * (1.0 + jnp.maximum(tail, 0.0))) * steep

    def substep(src, dst, fire_step):
        low, high, corner = src[13, 0], src[13, 1], src[13, 2]
        mixed = jnp.where(inner, high, low)
        top, border, bottom = [], [], []
        for p in range(SEG):
            first, final, beyond = src[1, p], src[REFINE, p], src[12, p]
            border.append(beyond)
            top.append(
                jnp.where(
                    edge_w, first, jnp.where(sub == 0, beyond, pltpu.roll(final, 1, 0))
                )
            )
            src[11, p] = jnp.where(
                edge_e, final, jnp.where(sub == 7, beyond, pltpu.roll(first, 7, 0))
            )

        def across(x, outer):
            south = jnp.where(lane == 0, outer, pltpu.roll(x[SEG - 1], 1, 1))
            north = jnp.where(lane == 127, outer, pltpu.roll(x[0], 127, 1))
            south = jnp.where(edge_s, x[0], south)
            north = jnp.where(edge_n, x[SEG - 1], north)
            line = [south] + x + [north]
            return [line[k + 1] - line[k] for k in range(SEG + 1)]

        wu, wv = wnd[0, 0], wnd[1, 0]

        def line(q, carry):
            x, dw = carry
            after = [src[q + 2, p] for p in range(SEG)]
            dh = across(x, pltpu.roll(mixed, 100 - 8 * q, 1))
            de = []
            for p in range(SEG):
                de.append(after[p] - x[p])
                new = moved(
                    x[p], dw[p], de[p], dh[p], dh[p + 1], fire_step * rate[q + 1, p], wu, wv
                )
                dst[q + 1, p] = new
                bsum[q, p] = bsum[q, p] + jnp.clip(new, -0.5, 0.5)
            return after, de

        x = [src[1, p] for p in range(SEG)]
        lax.fori_loop(0, REFINE, line, (x, [x[p] - top[p] for p in range(SEG)]), unroll=10)

        wu, wv = wnd[0, 1], wnd[1, 1]
        dh = across(border, corner)
        for p in range(SEG):
            here = border[p]
            west = jnp.where(sub == 7, src[REFINE, p], pltpu.roll(here, 7, 0))
            east = jnp.where(sub == 0, src[1, p], pltpu.roll(here, 1, 0))
            dst[12, p] = moved(
                here, here - west, east - here, dh[p], dh[p + 1], fire_step * rate[12, p], wu, wv
            )
        for k, here in enumerate((low, high)):
            west = jnp.where(strip_w, here, pltpu.roll(here, 8, 1))
            east = jnp.where(strip_e, here, pltpu.roll(here, 120, 1))
            south, north = pltpu.roll(here, 127, 1), pltpu.roll(here, 1, 1)
            dst[13, k] = moved(
                here,
                here - west,
                east - here,
                here - south,
                north - here,
                fire_step * rate[13, k],
                wnd[0, 2 + k],
                wnd[1, 2 + k],
            )
        west = jnp.where(sub == 7, pltpu.roll(mixed, 28, 1), pltpu.roll(corner, 7, 0))
        east = jnp.where(sub == 0, pltpu.roll(mixed, 100, 1), pltpu.roll(corner, 1, 0))
        south = jnp.where(lane == 127, border[SEG - 1], pltpu.roll(corner, 127, 1))
        north = jnp.where(lane == 0, border[0], pltpu.roll(corner, 1, 1))
        dst[13, 2] = moved(
            corner,
            corner - west,
            east - corner,
            corner - south,
            north - corner,
            fire_step * rate[13, 2],
            wnd[0, 4],
            wnd[1, 4],
        )

    lane_a = lax.broadcasted_iota(jnp.int32, (8, width), 1)

    def write(c, f, i, value):
        if c == STEPS - 1:
            air_out[f, i] = value
        else:
            air[c + 1, f, i + 1] = value

    def move_air(c):
        wait_air(c)
        final = c == STEPS - 1

        def update(i, carry):
            weight, total_u, total_v = carry
            u, v = air[c, 2, i + 1], air[c, 3, i + 1]
            u_up, u_dn = jnp.maximum(u, 0.0), jnp.minimum(u, 0.0)
            v_up, v_dn = jnp.maximum(v, 0.0), jnp.minimum(v, 0.0)
            lift_x = lift_y = None
            for f in range(4):
                here = air[c, f, i + 1]
                west = pltpu.roll(jnp.where(row8 == 7, xh[c, 0, f, i], here), 1, 0)
                east = pltpu.roll(jnp.where(row8 == 0, xh[c, 1, f, i], here), 7, 0)
                south = jnp.where(lane_a == 0, 0.0, pltpu.roll(here, 1, 1))
                north = jnp.where(lane_a == width - 1, 0.0, pltpu.roll(here, width - 1, 1))
                dw, de, ds, dn = here - west, east - here, here - south, north - here
                advect = u_up * dw + u_dn * de + v_up * ds + v_dn * dn
                lap = (de - dw) + (dn - ds) + (
                    (air[c, f, i] + air[c, f, i + 2]) - 2.0 * here
                )
                new = here + 0.1 * (0.2 * lap - advect)
                if f == 0:
                    lift_x, lift_y = east - west, north - south
                elif f == 1:
                    lift_x = lift_x + 0.6 * (east - west)
                    lift_y = lift_y + 0.6 * (north - south)
                elif f == 2:
                    new = new + 0.015 * lift_x
                    total_u = total_u + weight * new
                else:
                    new = new + 0.015 * lift_y
                    total_v = total_v + weight * new
                write(c, f, i, new)
            return weight * f32(col_ratio), total_u, total_v

        _, total_u, total_v = lax.fori_loop(0, depth, update, (col_base, nothing, nothing), unroll=2)
        if not final:
            send_wind(c + 1, total_u, total_v)

    def finish_air(c):
        final = c == STEPS - 1
        for j in range(bands):
            receive(band != j, frecv.at[c, j], flux_r.at[c, j], flux_s.at[c, j], device(0, j))
        parts = [
            frecv[c, 2 * k] + frecv[c, 2 * k + 1] for k in range(width // 128)
        ]
        whole = jnp.concatenate(parts, axis=1)
        heat_in, moist_in = whole[:8], whole[8:]

        def force(i, weight):
            for f, flux in ((0, heat_in), (1, moist_in)):
                now = air_out[f, i] if final else air[c + 1, f, i + 1]
                write(c, f, i, now + weight * flux)
            return weight * f32(prof_ratio)

        lax.fori_loop(0, depth, force, prof_base * f32(2.0), unroll=2)

    def burn_fire(c, fire_step):
        def burn(q, carry):
            hot, wet = carry
            for p in range(SEG):
                now = fuel[q, p]
                spent = (float(SUBSTEPS) * 0.5 - bsum[q, p]) * binv[q, p]
                remain = now * jnp.exp(-fire_step * spent)
                used = now - remain
                fuel[q, p] = remain
                bsum[q, p] = jnp.zeros((8, 128), f32)
                hot = hot + used * heat[q, p]
                wet = wet + used * moist[q, p]
            return hot, wet

        zero = jnp.zeros((8, 128), f32)
        hot, wet = lax.fori_loop(0, REFINE, burn, (zero, zero), unroll=2)
        flux = jnp.dot(
            split(jnp.concatenate([hot, wet], axis=0), 1, 2),
            smat[...],
            preferred_element_type=f32,
        ) * f32(1.0 / (REFINE * REFINE))
        fsend[c] = flux
        for j in range(bands):

            @pl.when(band == j)
            def _(j=j):
                frecv[c, j] = flux

            send(
                band != j,
                fsend.at[c],
                frecv.at[c, band],
                flux_s.at[c, j],
                flux_r.at[c, band],
                device(0, j),
            )

    def burn_window(c):
        fire_step = plan[c].astype(f32) * f32(0.15)
        if c == 0:
            surround(0, rate)
        surround(1 + c, xa)
        wait_wind(c)

        def pair(i, carry):
            substep(xa, xb, fire_step)
            substep(xb, xa, fire_step)
            return carry

        lax.fori_loop(0, SUBSTEPS // 2, pair, 0)
        if c < STEPS - 1:

            def ignite(q, carry):
                for p in range(SEG):
                    now = xa[q + 1, p]
                    xa[q + 1, p] = jnp.where(
                        ign[q, p] <= float(c + 1), jnp.minimum(now, -1.0), now
                    )
                return carry

            lax.fori_loop(0, REFINE, ignite, 0, unroll=2)
            outline(2 + c, xa)
        burn_fire(c, fire_step)

    def give(load, slot, array):
        values = jnp.concatenate(
            [
                jnp.concatenate([load(q, p) for p in range(SEG)], axis=1)
                for q in range(REFINE)
            ],
            axis=0,
        )
        found = jnp.dot(split(values, 0, 3), spread[...], preferred_element_type=f32)
        found = found[:rows] + found[rows : 2 * rows] + found[2 * rows :]
        for q in range(REFINE):
            for v in range(groups):
                stage[slot, v, pl.ds(q, 8, stride=REFINE), :] = found[
                    8 * q : 8 * q + 8, 128 * v : 128 * v + 128
                ]
        copies = [
            pltpu.make_async_copy(
                stage.at[slot, v], array.at[:, pl.ds(128 * v, 128)], out_s.at[slot, v]
            )
            for v in range(groups)
        ]
        for copy in copies:
            copy.start()
        return copies

    move_air(0)
    burn_window(0)
    finish_air(0)
    send_air(1)
    burn_window(1)
    move_air(1)
    finish_air(1)
    send_air(2)
    burn_window(2)
    move_air(2)
    finish_air(2)
    send_air(3)
    burn_window(3)
    copies = give(lambda q, p: xa[q + 1, p], 0, level_out)
    move_air(3)
    copies += give(lambda q, p: fuel[q, p], 1, fuel_out)
    drain()
    finish_air(3)
    for copy in copies:
        copy.wait()


def solution(mesh):
    tiles, sects, subs = (mesh.shape[name] for name in ("tile", "sect", "sub"))
    bands = sects * subs
    air_spec = P(None, ("sect", "sub"), ("group", "tile"), None)
    fire_spec = P(("group", "tile"), ("sect", "sub"))

    def local(air_state, fire_level, *rest):
        depth, width = air_state.shape[1], air_state.shape[3]
        rows, cols = fire_level.shape
        groups = cols // 128
        assert air_state.shape[2] == 8 and cols == 64 * REFINE and rows == 8 * REFINE
        vmem = pl.BlockSpec(memory_space=pltpu.VMEM)
        smem = pl.BlockSpec(memory_space=pltpu.SMEM)
        hbm = pl.BlockSpec(memory_space=pltpu.HBM)
        dma = pltpu.SemaphoreType.DMA

        def blocks(*lead):
            return pltpu.VMEM((*lead, 8, 128), f32)

        return pl.pallas_call(
            functools.partial(kernel, tiles, sects, subs),
            out_shape=(
                jax.ShapeDtypeStruct(air_state.shape, f32),
                jax.ShapeDtypeStruct(fire_level.shape, f32),
                jax.ShapeDtypeStruct(fire_level.shape, f32),
            ),
            in_specs=[hbm] * 5 + [smem] * 5,
            out_specs=(vmem, hbm, hbm),
            scratch_shapes=[
                pltpu.VMEM((STEPS, 4, depth + 2, 8, width), f32),
                pltpu.VMEM((STEPS, 2, 4, depth, 8, width), f32),
                blocks(14, SEG),
                blocks(14, SEG),
                blocks(14, SEG),
                blocks(REFINE, SEG),
                blocks(REFINE, SEG),
                blocks(REFINE, SEG),
                blocks(REFINE, SEG),
                blocks(REFINE, SEG),
                blocks(REFINE, SEG),
                pltpu.VMEM((2, groups, rows, 128), f32),
                pltpu.VMEM((2, groups, rows, 128), jnp.int32),
                pltpu.VMEM((cols, cols), bf16),
                pltpu.VMEM((cols, cols), bf16),
                pltpu.VMEM((256, 512), bf16),
                pltpu.VMEM((256, 128), bf16),
                blocks(2, 5),
                blocks(STEPS + 1),
                blocks(STEPS + 1, SEG + 1),
                blocks(STEPS + 1, SEG + 1),
                blocks(STEPS + 1, 2),
                blocks(STEPS + 1, 2),
                pltpu.VMEM((STEPS, bands, 16, 128), f32),
                pltpu.VMEM((STEPS, bands, 16, 128), f32),
                blocks(STEPS, bands, 2),
                blocks(STEPS, bands, 2),
                pltpu.VMEM((STEPS, 16, 128), f32),
                pltpu.VMEM((STEPS, bands, 16, 128), f32),
                dma((4, groups + 1)),
                dma((2, groups)),
                dma((STEPS + 1, 8)),
                dma((STEPS + 1, 8)),
                dma((STEPS, 3, bands)),
                dma((STEPS, 3, bands)),
                dma((STEPS, bands)),
                dma((STEPS, bands)),
                dma((STEPS, 4)),
                dma((STEPS, 4)),
            ],
            compiler_params=pltpu.CompilerParams(
                collective_id=0, has_side_effects=True, vmem_limit_bytes=56 * 1024 * 1024
            ),
        )(air_state, fire_level, *rest)

    return jax.shard_map(
        local,
        mesh=mesh,
        in_specs=(air_spec, fire_spec, fire_spec, fire_spec, fire_spec) + (P(),) * 5,
        out_specs=(air_spec, fire_spec, fire_spec),
        check_vma=False,
    )
```

```python
import functools
import math

import jax
import jax.numpy as jnp
from jax import lax
from jax.experimental import pallas as pl
from jax.experimental.pallas import tpu as pltpu
from jax.sharding import PartitionSpec as P

LEVELS = 80
REFINE = 10
NFUEL = 13
STEPS = 4
SUBSTEPS = 4
DEEP = 4
SEG = REFINE // 2
MESH = pl.DeviceIdType.MESH
TINY = 1.1754944e-38
f32 = jnp.float32
bf16 = jnp.bfloat16


def split(value, axis, pieces):
    parts = []
    for _ in range(pieces):
        parts.append(value.astype(bf16))
        value = value - parts[-1].astype(f32)
    return jnp.concatenate(parts, axis=axis)


def indicator(mask, value=1.0):
    return jnp.where(mask, value, 0.0).astype(bf16)


def kernel(
    tiles,
    sects,
    subs,
    air_in,
    level_in,
    fuel_in,
    class_in,
    ign_in,
    plan,
    t_rate,
    t_burn,
    t_heat,
    t_moist,
    air_out,
    level_out,
    fuel_out,
    air,
    xh,
    xa,
    xb,
    rate,
    fuel,
    binv,
    heat,
    moist,
    ign,
    bsum,
    stage,
    turned,
    gather,
    spread,
    wmat,
    smat,
    wnd,
    es,
    gs,
    hb,
    er,
    dg,
    wsend,
    wrecv,
    hsend,
    hrecv,
    fsend,
    frecv,
    gsend,
    grecv,
    in_s,
    fire_s,
    fire_r,
    wind_s,
    wind_r,
    flux_s,
    flux_r,
    rim_s,
    rim_r,
    halo_s,
    halo_r,
):
    bands = sects * subs
    depth = air_in.shape[1]
    width = air_in.shape[3]
    rows, cols = level_in.shape
    coarse = cols // REFINE
    groups = cols // 128
    tile_at = lax.axis_index("tile")
    sect_at = lax.axis_index("sect")
    sub_at = lax.axis_index("sub")
    band = sect_at * subs + sub_at
    not_first = tile_at > 0
    not_final = tile_at < tiles - 1
    band_low = band > 0
    band_high = band < bands - 1

    def device(tile_step, at_band):
        return {
            "tile": tile_at + tile_step,
            "sect": at_band // subs,
            "sub": at_band % subs,
        }

    def both(a, b):
        return jnp.logical_and(a, b)

    pending = []

    def send(condition, src, dst, send_sem, recv_sem, where):
        def make():
            return pltpu.make_async_remote_copy(
                src_ref=src,
                dst_ref=dst,
                send_sem=send_sem,
                recv_sem=recv_sem,
                device_id=where,
                device_id_type=MESH,
            )

        @pl.when(condition)
        def _():
            make().start()

        pending.append((condition, make))

    def drain(pending):
        for condition, make in pending:

            @pl.when(condition)
            def _(make=make):
                make().wait_send()

        pending.clear()

    def send_group(condition, parts, whole, send_sem, recv_sem, wheres):
        def make(src, dst, where):
            return pltpu.make_async_remote_copy(
                src_ref=src,
                dst_ref=dst,
                send_sem=send_sem,
                recv_sem=recv_sem,
                device_id=where,
                device_id_type=MESH,
            )

        @pl.when(condition)
        def _():
            for (src, dst), where in zip(parts, wheres):
                make(src, dst, where).start()

        pending.append((condition, lambda: make(whole, whole, wheres[0])))

    def receive(condition, dst, recv_sem, send_sem, where):
        @pl.when(condition)
        def _():
            pltpu.make_async_remote_copy(
                src_ref=dst,
                dst_ref=dst,
                send_sem=send_sem,
                recv_sem=recv_sem,
                device_id=where,
                device_id_type=MESH,
            ).wait_recv()

    def iota(shape, dim):
        return lax.broadcasted_iota(jnp.int32, shape, dim)

    barrier = pltpu.get_barrier_semaphore()
    for tile_step, condition in ((0, None), (-1, not_first), (1, not_final)):
        for j in range(bands):
            ok = (band != j) if condition is None else condition

            @pl.when(ok)
            def _(tile_step=tile_step, j=j):
                pl.semaphore_signal(
                    barrier, inc=1, device_id=device(tile_step, j), device_id_type=MESH
                )

    def fetch(array, slot):
        return [
            pltpu.make_async_copy(
                array.at[:, pl.ds(128 * v, 128)], stage.at[slot, v], in_s.at[slot, v]
            )
            for v in range(groups)
        ]

    air_copy = pltpu.make_async_copy(air_in, air.at[0, :, pl.ds(1, depth)], in_s.at[0, groups])
    level_copy, fuel_copy = fetch(level_in, 0), fetch(fuel_in, 1)

    def fetch_int(array, slot):
        return [
            pltpu.make_async_copy(
                array.at[:, pl.ds(128 * v, 128)], turned.at[slot, v], in_s.at[2 + slot, v]
            )
            for v in range(groups)
        ]

    class_copy, ign_copy = fetch_int(class_in, 0), fetch_int(ign_in, 1)
    air_copy.start()
    for copies in (level_copy, class_copy, ign_copy, fuel_copy):
        for copy in copies:
            copy.start()

    spot = iota((16, cols), 1)
    spot = SEG * (spot % 128) + spot // 128
    line16 = iota((16, cols), 0)

    def make_gather(i, carry):
        at = pl.ds(pl.multiple_of(i * 16, 16), 16)
        gather[at, :] = indicator(spot == line16 + 16 * i)
        return carry

    lax.fori_loop(0, cols // 16, make_gather, 0, unroll=4)

    column = iota((16, cols), 1)

    def make_spread(i, carry):
        at = pl.ds(pl.multiple_of(i * 16, 16), 16)
        spread[at, :] = indicator(column == SEG * (line16 + 16 * (i % 8)) + i // 8)
        return carry

    source, place = iota((128, 512), 0), iota((128, 512), 1)
    block, place = place // 128, place % 128
    inner = place % 8 < 4
    first = jnp.where(block == 0, 32 + place // 2, jnp.where(inner, 32, 31))
    second = jnp.where(
        block == 2, jnp.where(inner, 96, 95), jnp.where(place < 64, 31, 96)
    )
    pattern = indicator(source == jnp.where(block < 2, first, second), 0.5)
    wmat[:128, :] = pattern
    wmat[128:, :] = pattern
    source, place = iota((128, 128), 0), iota((128, 128), 1)
    pattern = indicator(place == source // 2 + coarse * (band % 2))
    smat[:128, :] = pattern
    smat[128:, :] = pattern

    sub = iota((8, 128), 0)
    lane = iota((8, 128), 1)
    octet = lane // 8
    inner = lane % 8 < 4
    edge_w = sub == jnp.where(not_first, -1, 0)
    edge_e = sub == jnp.where(not_final, -1, 7)
    edge_s = lane == jnp.where(band_low, -1, 0)
    edge_n = lane == jnp.where(band_high, -1, 127)
    strip_w = both(edge_w, octet == 3)
    strip_e = both(edge_e, octet == 12)

    def rolled(value, shift, axis):
        shift = shift % value.shape[axis]
        return pltpu.roll(value, shift, axis) if shift else value

    row8 = iota((8, width), 0)
    total_col = sum(math.exp(-k / LEVELS) for k in range(LEVELS))
    total_prof = sum(math.exp(-2.0 * k / LEVELS) for k in range(LEVELS))
    col_base = f32(0.0)
    prof_base = f32(0.0)
    for j in range(bands):
        here = band == j
        col_base = jnp.where(here, f32(math.exp(-j * depth / LEVELS) / total_col), col_base)
        prof_base = jnp.where(
            here, f32(LEVELS * math.exp(-2.0 * j * depth / LEVELS) / total_prof), prof_base
        )
    col_ratio = math.exp(-1.0 / LEVELS)
    prof_ratio = math.exp(-2.0 / LEVELS)

    air_copy.wait()

    def first_air(i, carry):
        weight, total_u, total_v = carry
        total_u = total_u + weight * air[0, 2, i + 1]
        total_v = total_v + weight * air[0, 3, i + 1]
        return weight * f32(col_ratio), total_u, total_v

    nothing = jnp.zeros((8, width), f32)
    _, total_u, total_v = lax.fori_loop(
        0, depth, first_air, (col_base, nothing, nothing), unroll=4
    )

    def send_wind(c, total_u, total_v):
        stacked = jnp.concatenate([total_u, total_v], axis=0)
        for j in range(bands):
            shift = (128 // 4 - coarse * j) % width
            window = (pltpu.roll(stacked, shift, 1) if shift else stacked)[:, :128]
            wsend[c, j] = window
            for k in range(2):
                low = jnp.broadcast_to(window[8 * k : 8 * k + 1], (8, 128))
                high = jnp.broadcast_to(window[8 * k + 7 : 8 * k + 8], (8, 128))
                hsend[c, j, k] = jnp.where(sub < 4, high, low)

            @pl.when(band == j)
            def _(window=window, j=j):
                wrecv[c, j] = window

        for j in range(bands):
            send(
                band != j,
                wsend.at[c, j],
                wrecv.at[c, band],
                wind_s.at[c, j],
                wind_r.at[c, band],
                device(0, j),
            )
        for way, tile_step, ok in ((0, 1, not_final), (1, -1, not_first)):
            part = pl.ds(4 * way, 4)
            send_group(
                ok,
                [
                    (hsend.at[c, j, :, part, :], hrecv.at[c, band, :, part, :])
                    for j in range(bands)
                ],
                hsend.at[c, :, :, part, :],
                rim_s.at[c, way],
                rim_r.at[c, way],
                [device(tile_step, j) for j in range(bands)],
            )

    def wait_wind(c):
        for j in range(bands):
            receive(band != j, wrecv.at[c, j], wind_r.at[c, j], wind_s.at[c, j], device(0, j))
        for way, tile_step, ok in ((0, -1, not_first), (1, 1, not_final)):
            part = pl.ds(4 * way, 4)
            receive(
                ok,
                hrecv.at[c, :, :, part, :],
                rim_r.at[c, way],
                rim_s.at[c, way],
                device(tile_step, 0),
            )
        own = wrecv[c, 0]
        beyond = [hrecv[c, 0, 0], hrecv[c, 0, 1]]
        for j in range(1, bands):
            own = own + wrecv[c, j]
            beyond = [beyond[0] + hrecv[c, j, 0], beyond[1] + hrecv[c, j, 1]]
        together = jnp.concatenate([own] + beyond, axis=0)
        wide = jnp.dot(split(together, 1, 2), wmat[...], preferred_element_type=f32)
        for k in range(2):
            own, beyond = wide[8 * k : 8 * k + 8], wide[16 + 8 * k : 24 + 8 * k]
            wnd[k, 0] = own[:, :128]
            wnd[k, 1] = beyond[:, :128]
            for at in (1, 2):
                here = own[:, 128 * at : 128 * at + 128]
                there = beyond[:, 128 * at : 128 * at + 128]
                below = jnp.where(sub == 0, there, pltpu.roll(here, 1, 0))
                above = jnp.where(sub == 7, there, pltpu.roll(here, 7, 0))
                wnd[k, at + 1] = jnp.where(
                    octet < 3, below, jnp.where(octet >= 13, above, here)
                )
            wnd[k, 4] = beyond[:, 384:]

    def send_air(c):
        before = len(pending)
        send(
            not_final,
            air.at[c, :, pl.ds(1, depth), pl.ds(7, 1), :],
            xh.at[c, 0, :, :, pl.ds(7, 1), :],
            halo_s.at[c, 0],
            halo_r.at[c, 0],
            device(1, band),
        )
        send(
            not_first,
            air.at[c, :, pl.ds(1, depth), pl.ds(0, 1), :],
            xh.at[c, 1, :, :, pl.ds(0, 1), :],
            halo_s.at[c, 1],
            halo_r.at[c, 1],
            device(-1, band),
        )
        send(
            band_high,
            air.at[c, :, depth],
            air.at[c, :, 0],
            halo_s.at[c, 2],
            halo_r.at[c, 2],
            device(0, band + 1),
        )
        send(
            band_low,
            air.at[c, :, 1],
            air.at[c, :, depth + 1],
            halo_s.at[c, 3],
            halo_r.at[c, 3],
            device(0, band - 1),
        )
        leaving[c] = pending[before:]
        del pending[before:]

    leaving = {}

    def wait_air(c):
        receive(
            not_first,
            xh.at[c, 0, :, :, pl.ds(7, 1), :],
            halo_r.at[c, 0],
            halo_s.at[c, 0],
            device(-1, band),
        )
        receive(
            not_final,
            xh.at[c, 1, :, :, pl.ds(0, 1), :],
            halo_r.at[c, 1],
            halo_s.at[c, 1],
            device(1, band),
        )
        receive(band_low, air.at[c, :, 0], halo_r.at[c, 2], halo_s.at[c, 2], device(0, band - 1))
        receive(
            band_high,
            air.at[c, :, depth + 1],
            halo_r.at[c, 3],
            halo_s.at[c, 3],
            device(0, band + 1),
        )

    def reorder(load):
        return jnp.concatenate(
            [
                jnp.concatenate([load(v, pl.ds(q, 8, stride=REFINE)) for v in range(groups)], axis=1)
                for q in range(REFINE)
            ],
            axis=0,
        )

    for copy in level_copy + class_copy + ign_copy:
        copy.wait()
    kinds = reorder(
        lambda v, at: (turned[0, v, at, :] + 16 * turned[1, v, at, :]).astype(f32)
    ).astype(bf16)
    pieces = split(reorder(lambda v, at: stage[0, v, at, :]), 0, 3)
    found = jnp.dot(
        jnp.concatenate([pieces, kinds], axis=0), gather[...], preferred_element_type=f32
    )
    together = found[:rows] + found[rows : 2 * rows] + found[2 * rows : 3 * rows]
    kinds = found[3 * rows :]
    for q in range(REFINE):
        for p in range(SEG):
            kind = kinds[8 * q : 8 * q + 8, 128 * p : 128 * p + 128]
            when = jnp.floor(kind * (1.0 / 16.0))
            now = together[8 * q : 8 * q + 8, 128 * p : 128 * p + 128]
            ign[q, p] = when
            moist[q, p] = kind - 16.0 * when
            xa[q + 1, p] = jnp.where(when <= 0.0, jnp.minimum(now, -1.0), now)

    def find_rate(q, carry):
        for p in range(SEG):
            kind = moist[q, p]
            value = jnp.full((8, 128), t_rate[0], f32)
            for k in range(1, NFUEL):
                value = jnp.where(kind == float(k), t_rate[k], value)
            rate[q + 1, p] = value
        return carry

    lax.fori_loop(0, REFINE, find_rate, 0)

    def outline(e, ref):
        def edge(q, found):
            x = [ref[q + 1, p] for p in range(SEG)]
            near = pltpu.roll(x[SEG - 1], 1, 1)
            for k in range(1, DEEP):
                near = jnp.where(lane == k, pltpu.roll(x[SEG - 1 - k], k + 1, 1), near)
            for k in range(DEEP):
                near = jnp.where(lane == 127 - k, pltpu.roll(x[k], 127 - k, 1), near)
            return jnp.where(octet == q + 3, pltpu.roll(near, 8 * q + 28, 1), found)

        found = lax.fori_loop(0, REFINE, edge, jnp.zeros((8, 128), f32), unroll=10)
        es[e] = found
        gs[e, SEG] = jnp.where(
            sub < 4,
            jnp.broadcast_to(found[7:8], (8, 128)),
            jnp.broadcast_to(found[0:1], (8, 128)),
        )

        def border(p, carry):
            value = rolled(ref[REFINE, p], 1, 0)
            for k in range(1, DEEP):
                value = jnp.where(sub == k, rolled(ref[REFINE - k, p], k + 1, 0), value)
            for k in range(DEEP):
                value = jnp.where(sub == 4 + k, rolled(ref[DEEP - k, p], 4 + k, 0), value)
            gs[e, p] = value
            return carry

        lax.fori_loop(0, SEG, border, 0, unroll=5)

    def send_outline(e):
        for way, tile_step, ok in ((0, 1, not_final), (1, -1, not_first)):
            part = pl.ds(4 * way, 4)
            send(
                ok,
                gs.at[e, :, part, :],
                hb.at[e, :, part, :],
                fire_s.at[e, way],
                fire_r.at[e, way],
                device(tile_step, band),
            )
        for side, band_step, ok in ((0, 1, band_high), (1, -1, band_low)):
            send(
                ok,
                es.at[e],
                er.at[e, side],
                fire_s.at[e, 2 + side],
                fire_r.at[e, 2 + side],
                device(0, band + band_step),
            )
            for way, tile_step, also in ((0, 1, not_final), (1, -1, not_first)):
                send(
                    both(ok, also),
                    es.at[e, pl.ds(7 - 7 * way, 1), :],
                    dg.at[e, side, pl.ds(7 * way, 1), :],
                    fire_s.at[e, 4 + 2 * side + way],
                    fire_r.at[e, 4 + 2 * side + way],
                    device(tile_step, band + band_step),
                )

    def surround(e, ref):
        for way, tile_step, ok in ((0, -1, not_first), (1, 1, not_final)):
            receive(
                ok,
                hb.at[e, :, pl.ds(4 * way, 4), :],
                fire_r.at[e, way],
                fire_s.at[e, way],
                device(tile_step, band),
            )
        for side, band_step, ok in ((0, -1, band_low), (1, 1, band_high)):
            receive(
                ok,
                er.at[e, side],
                fire_r.at[e, 2 + side],
                fire_s.at[e, 2 + side],
                device(0, band + band_step),
            )
            for way, tile_step, also in ((0, -1, not_first), (1, 1, not_final)):
                receive(
                    both(ok, also),
                    dg.at[e, side, pl.ds(7 * way, 1), :],
                    fire_r.at[e, 4 + 2 * side + way],
                    fire_s.at[e, 4 + 2 * side + way],
                    device(tile_step, band + band_step),
                )
        for p in range(SEG):
            ref[12, p] = hb[e, p]
        mine, beyond = es[e], hb[e, SEG]

        def strip(here, there):
            below = jnp.where(sub == 0, there, pltpu.roll(here, 1, 0))
            above = jnp.where(sub == 7, there, pltpu.roll(here, 7, 0))
            return jnp.where(
                octet < 3,
                pltpu.roll(below, 48, 1),
                jnp.where(octet >= 13, pltpu.roll(above, 80, 1), here),
            )

        low = strip(jnp.where(inner, mine, er[e, 0]), jnp.where(inner, beyond, dg[e, 0]))
        high = strip(jnp.where(inner, er[e, 1], mine), jnp.where(inner, dg[e, 1], beyond))
        mixed = jnp.where(inner, high, low)
        corner = mixed
        for k in range(3):
            corner = jnp.where(sub == k, rolled(rolled(mixed, 108 + 8 * k, 1), k, 0), corner)
            corner = jnp.where(sub == 7 - k, rolled(rolled(mixed, 20 - 8 * k, 1), -k, 0), corner)
        ref[13, 0] = low
        ref[13, 1] = high
        ref[13, 2] = corner

    outline(0, rate)
    outline(1, xa)
    expected = (
        bands - 1 + bands * (not_first.astype(jnp.int32) + not_final.astype(jnp.int32))
    )
    pl.semaphore_wait(barrier, expected)

    send_air(0)
    send_wind(0, total_u, total_v)
    send_outline(0)
    send_outline(1)

    @pl.when(jnp.logical_not(not_first))
    def _():
        def zero(i, carry):
            for c in range(STEPS):
                for f in range(4):
                    xh[c, 0, f, i] = jnp.zeros((8, width), f32)
            return carry

        lax.fori_loop(0, depth, zero, 0)
        grecv[:, :, :, 4:] = jnp.zeros((STEPS - 1, bands, 2, 4, 128), f32)

    @pl.when(jnp.logical_not(not_final))
    def _():
        grecv[:, :, :, :4] = jnp.zeros((STEPS - 1, bands, 2, 4, 128), f32)

        def zero(i, carry):
            for c in range(STEPS):
                for f in range(4):
                    xh[c, 1, f, i] = jnp.zeros((8, width), f32)
            return carry

        lax.fori_loop(0, depth, zero, 0)

    @pl.when(jnp.logical_not(band_low))
    def _():
        for c in range(STEPS):
            air[c, :, 0] = jnp.zeros((4, 8, width), f32)

    @pl.when(jnp.logical_not(band_high))
    def _():
        for c in range(STEPS):
            air[c, :, depth + 1] = jnp.zeros((4, 8, width), f32)

    def lookup(q, carry):
        for p in range(SEG):
            kind = moist[q, p]
            burn = jnp.full((8, 128), t_burn[0], f32)
            hot = jnp.full((8, 128), t_heat[0], f32)
            wet = jnp.full((8, 128), t_moist[0], f32)
            for k in range(1, NFUEL):
                same = kind == float(k)
                burn = jnp.where(same, t_burn[k], burn)
                hot = jnp.where(same, t_heat[k], hot)
                wet = jnp.where(same, t_moist[k], wet)
            binv[q, p] = 1.0 / burn
            heat[q, p] = hot
            moist[q, p] = wet
            bsum[q, p] = jnp.zeros((8, 128), f32)
        return carry

    lax.fori_loop(0, REFINE, lookup, 0)
    for copy in fuel_copy:
        copy.wait()
    pieces = split(reorder(lambda v, at: stage[1, v, at, :]), 0, 3)
    found = jnp.dot(pieces, gather[...], preferred_element_type=f32)
    together = found[:rows] + found[rows : 2 * rows] + found[2 * rows :]
    for q in range(REFINE):
        for p in range(SEG):
            fuel[q, p] = together[8 * q : 8 * q + 8, 128 * p : 128 * p + 128]
    lax.fori_loop(0, cols // 16, make_spread, 0, unroll=4)

    def uphill(d):
        return jnp.maximum(d, 0.0) * d

    def downhill(d):
        return jnp.minimum(d, 0.0) * d

    def moved(here, dw, de, ds, dn, speed, wu, wv):
        square = (uphill(dw) + downhill(de)) + (uphill(ds) + downhill(dn))
        steep = square * lax.rsqrt(jnp.maximum(square, TINY))
        gx, gy = dw + de, ds + dn
        tail = (wu * gx + wv * gy) * lax.rsqrt(gx * gx + gy * gy + 4.0)
        return here - (speed * (1.0 + jnp.maximum(tail, 0.0))) * steep

    def substep(src, dst, fire_step):
        low, high, corner = src[13, 0], src[13, 1], src[13, 2]
        mixed = jnp.where(inner, high, low)
        top, border, bottom = [], [], []
        for p in range(SEG):
            first, final, beyond = src[1, p], src[REFINE, p], src[12, p]
            border.append(beyond)
            top.append(
                jnp.where(
                    edge_w, first, jnp.where(sub == 0, beyond, pltpu.roll(final, 1, 0))
                )
            )
            src[11, p] = jnp.where(
                edge_e, final, jnp.where(sub == 7, beyond, pltpu.roll(first, 7, 0))
            )

        def across(x, outer):
            south = jnp.where(lane == 0, outer, pltpu.roll(x[SEG - 1], 1, 1))
            north = jnp.where(lane == 127, outer, pltpu.roll(x[0], 127, 1))
            south = jnp.where(edge_s, x[0], south)
            north = jnp.where(edge_n, x[SEG - 1], north)
            line = [south] + x + [north]
            return [line[k + 1] - line[k] for k in range(SEG + 1)]

        wu, wv = wnd[0, 0], wnd[1, 0]

        def line(q, carry):
            x, dw = carry
            after = [src[q + 2, p] for p in range(SEG)]
            dh = across(x, pltpu.roll(mixed, 100 - 8 * q, 1))
            de = []
            for p in range(SEG):
                de.append(after[p] - x[p])
                new = moved(
                    x[p], dw[p], de[p], dh[p], dh[p + 1], fire_step * rate[q + 1, p], wu, wv
                )
                dst[q + 1, p] = new
                bsum[q, p] = bsum[q, p] + jnp.clip(new, -0.5, 0.5)
            return after, de

        x = [src[1, p] for p in range(SEG)]
        lax.fori_loop(0, REFINE, line, (x, [x[p] - top[p] for p in range(SEG)]), unroll=10)

        wu, wv = wnd[0, 1], wnd[1, 1]
        dh = across(border, corner)
        for p in range(SEG):
            here = border[p]
            west = jnp.where(sub == 7, src[REFINE, p], pltpu.roll(here, 7, 0))
            east = jnp.where(sub == 0, src[1, p], pltpu.roll(here, 1, 0))
            dst[12, p] = moved(
                here, here - west, east - here, dh[p], dh[p + 1], fire_step * rate[12, p], wu, wv
            )
        for k, here in enumerate((low, high)):
            west = jnp.where(strip_w, here, pltpu.roll(here, 8, 1))
            east = jnp.where(strip_e, here, pltpu.roll(here, 120, 1))
            south, north = pltpu.roll(here, 127, 1), pltpu.roll(here, 1, 1)
            dst[13, k] = moved(
                here,
                here - west,
                east - here,
                here - south,
                north - here,
                fire_step * rate[13, k],
                wnd[0, 2 + k],
                wnd[1, 2 + k],
            )
        west = jnp.where(sub == 7, pltpu.roll(mixed, 28, 1), pltpu.roll(corner, 7, 0))
        east = jnp.where(sub == 0, pltpu.roll(mixed, 100, 1), pltpu.roll(corner, 1, 0))
        south = jnp.where(lane == 127, border[SEG - 1], pltpu.roll(corner, 127, 1))
        north = jnp.where(lane == 0, border[0], pltpu.roll(corner, 1, 1))
        dst[13, 2] = moved(
            corner,
            corner - west,
            east - corner,
            corner - south,
            north - corner,
            fire_step * rate[13, 2],
            wnd[0, 4],
            wnd[1, 4],
        )

    lane_a = lax.broadcasted_iota(jnp.int32, (8, width), 1)

    def write(c, f, i, value):
        if c == STEPS - 1:
            air_out[f, i] = value
        else:
            air[c + 1, f, i + 1] = value

    def wait_flux(c):
        for j in range(bands):
            receive(band != j, frecv.at[c, j], flux_r.at[c, j], flux_s.at[c, j], device(0, j))
        whole = jnp.concatenate(
            [frecv[c, 2 * k] + frecv[c, 2 * k + 1] for k in range(width // 128)], axis=1
        )
        return whole[:8], whole[8:]

    def wait_rim(c):
        for way, tile_step, ok in ((0, -1, not_first), (1, 1, not_final)):
            part = pl.ds(4 - 4 * way, 4)
            receive(
                ok,
                grecv.at[c, :, :, part, :],
                rim_r.at[STEPS + c, way],
                rim_s.at[STEPS + c, way],
                device(tile_step, 0),
            )
        return [
            jnp.concatenate(
                [grecv[c, 2 * k, f] + grecv[c, 2 * k + 1, f] for k in range(width // 128)],
                axis=1,
            )
            for f in range(2)
        ]

    def force_air(c, flux):
        def force(i, weight):
            for f in range(2):
                now = air_out[f, i] if c == STEPS - 1 else air[c + 1, f, i + 1]
                write(c, f, i, now + weight * flux[f])
            return weight * f32(prof_ratio)

        lax.fori_loop(0, depth, force, prof_base * f32(2.0), unroll=4)

    def move_air(c):
        rim = None
        if c > 0:
            drain(leaving[c])
            flux = wait_flux(c - 1)
            force_air(c - 1, flux)
        wait_air(c)
        if c > 0:
            low = jnp.where(band_low, prof_base * f32(2.0 / prof_ratio), 0.0)
            high = jnp.where(band_high, prof_base * f32(2.0 * prof_ratio**depth), 0.0)
            for f in range(2):
                air[c, f, 0] = air[c, f, 0] + low * flux[f]
                air[c, f, depth + 1] = air[c, f, depth + 1] + high * flux[f]
            rim = wait_rim(c - 1)
        final = c == STEPS - 1

        def update(i, carry):
            weight, share, total_u, total_v = carry
            u, v = air[c, 2, i + 1], air[c, 3, i + 1]
            u_up, u_dn = jnp.maximum(u, 0.0), jnp.minimum(u, 0.0)
            v_up, v_dn = jnp.maximum(v, 0.0), jnp.minimum(v, 0.0)
            lift_x = lift_y = None
            for f in range(4):
                here = air[c, f, i + 1]
                west, east = xh[c, 0, f, i], xh[c, 1, f, i]
                if c > 0 and f < 2:
                    west, east = west + share * rim[f], east + share * rim[f]
                west = pltpu.roll(jnp.where(row8 == 7, west, here), 1, 0)
                east = pltpu.roll(jnp.where(row8 == 0, east, here), 7, 0)
                south = jnp.where(lane_a == 0, 0.0, pltpu.roll(here, 1, 1))
                north = jnp.where(lane_a == width - 1, 0.0, pltpu.roll(here, width - 1, 1))
                dw, de, ds, dn = here - west, east - here, here - south, north - here
                advect = u_up * dw + u_dn * de + v_up * ds + v_dn * dn
                lap = (de - dw) + (dn - ds) + (
                    (air[c, f, i] + air[c, f, i + 2]) - 2.0 * here
                )
                new = here + 0.1 * (0.2 * lap - advect)
                if f == 0:
                    lift_x, lift_y = east - west, north - south
                elif f == 1:
                    lift_x = lift_x + 0.6 * (east - west)
                    lift_y = lift_y + 0.6 * (north - south)
                elif f == 2:
                    new = new + 0.015 * lift_x
                    total_u = total_u + weight * new
                else:
                    new = new + 0.015 * lift_y
                    total_v = total_v + weight * new
                write(c, f, i, new)
            return weight * f32(col_ratio), share * f32(prof_ratio), total_u, total_v

        carry = (col_base, prof_base * f32(2.0), nothing, nothing)
        _, _, total_u, total_v = lax.fori_loop(0, depth, update, carry, unroll=2)
        if not final:
            send_wind(c + 1, total_u, total_v)
            send_air(c + 1)

    def burn_fire(c, fire_step):
        def burn(q, carry):
            hot, wet = carry
            for p in range(SEG):
                now = fuel[q, p]
                spent = (float(SUBSTEPS) * 0.5 - bsum[q, p]) * binv[q, p]
                remain = now * jnp.exp(-fire_step * spent)
                used = now - remain
                fuel[q, p] = remain
                bsum[q, p] = jnp.zeros((8, 128), f32)
                hot = hot + used * heat[q, p]
                wet = wet + used * moist[q, p]
            return hot, wet

        zero = jnp.zeros((8, 128), f32)
        hot, wet = lax.fori_loop(0, REFINE, burn, (zero, zero), unroll=2)
        flux = jnp.dot(
            split(jnp.concatenate([hot, wet], axis=0), 1, 2),
            smat[...],
            preferred_element_type=f32,
        ) * f32(1.0 / (REFINE * REFINE))
        fsend[c] = flux
        for j in range(bands):

            @pl.when(band == j)
            def _(j=j):
                frecv[c, j] = flux

            send(
                band != j,
                fsend.at[c],
                frecv.at[c, band],
                flux_s.at[c, j],
                flux_r.at[c, band],
                device(0, j),
            )
        if c == STEPS - 1:
            return
        for k in range(2):
            low = jnp.broadcast_to(flux[8 * k : 8 * k + 1], (8, 128))
            high = jnp.broadcast_to(flux[8 * k + 7 : 8 * k + 8], (8, 128))
            for j in range(bands):
                gsend[c, j, k] = jnp.where(sub < 4, low, high)
        for way, tile_step, ok in ((0, 1, not_final), (1, -1, not_first)):
            part = pl.ds(4 - 4 * way, 4)
            send_group(
                ok,
                [
                    (gsend.at[c, j, :, part, :], grecv.at[c, band, :, part, :])
                    for j in range(bands)
                ],
                gsend.at[c, :, :, part, :],
                rim_s.at[STEPS + c, way],
                rim_r.at[STEPS + c, way],
                [device(tile_step, j) for j in range(bands)],
            )

    def burn_window(c):
        fire_step = plan[c].astype(f32) * f32(0.15)
        if c == 0:
            surround(0, rate)
        wait_wind(c)
        surround(1 + c, xa)

        def pair(i, carry):
            substep(xa, xb, fire_step)
            substep(xb, xa, fire_step)
            return carry

        lax.fori_loop(0, SUBSTEPS // 2, pair, 0)
        burn_fire(c, fire_step)
        if c < STEPS - 1:

            def ignite(q, carry):
                for p in range(SEG):
                    now = xa[q + 1, p]
                    xa[q + 1, p] = jnp.where(
                        ign[q, p] <= float(c + 1), jnp.minimum(now, -1.0), now
                    )
                return carry

            lax.fori_loop(0, REFINE, ignite, 0, unroll=2)
            outline(2 + c, xa)
            send_outline(2 + c)

    def give(load, array):
        values = jnp.concatenate(
            [
                jnp.concatenate([load(q, p) for p in range(SEG)], axis=1)
                for q in range(REFINE)
            ],
            axis=0,
        )
        found = jnp.dot(split(values, 0, 3), spread[...], preferred_element_type=f32)
        found = found[:rows] + found[rows : 2 * rows] + found[2 * rows :]
        for q in range(REFINE):
            for v in range(groups):
                array[v, pl.ds(q, 8, stride=REFINE), :] = found[
                    8 * q : 8 * q + 8, 128 * v : 128 * v + 128
                ]

    for c in range(STEPS - 1):
        move_air(c)
        burn_window(c)
    burn_window(STEPS - 1)
    give(lambda q, p: xa[q + 1, p], level_out)
    move_air(STEPS - 1)
    give(lambda q, p: fuel[q, p], fuel_out)
    drain(pending)
    drain(leaving[0])
    force_air(STEPS - 1, wait_flux(STEPS - 1))


def release(air, level, fuel, air_out, level_out, fuel_out, sems):
    copies = [pltpu.make_async_copy(air, air_out, sems.at[0, 0])]
    for k, (held, out) in enumerate(((level, level_out), (fuel, fuel_out))):
        for v in range(held.shape[0]):
            copies.append(
                pltpu.make_async_copy(
                    held.at[v], out.at[:, pl.ds(128 * v, 128)], sems.at[1 + k, v]
                )
            )
    for copy in copies:
        copy.start()
    for copy in copies:
        copy.wait()


def solution(mesh):
    tiles, sects, subs = (mesh.shape[name] for name in ("tile", "sect", "sub"))
    bands = sects * subs
    air_spec = P(None, ("sect", "sub"), ("group", "tile"), None)
    fire_spec = P(("group", "tile"), ("sect", "sub"))

    def local(air_state, fire_level, *rest):
        depth, width = air_state.shape[1], air_state.shape[3]
        rows, cols = fire_level.shape
        groups = cols // 128
        assert air_state.shape[2] == 8 and cols == 64 * REFINE and rows == 8 * REFINE
        vmem = pl.BlockSpec(memory_space=pltpu.VMEM)
        smem = pl.BlockSpec(memory_space=pltpu.SMEM)
        hbm = pl.BlockSpec(memory_space=pltpu.HBM)
        dma = pltpu.SemaphoreType.DMA

        def blocks(*lead):
            return pltpu.VMEM((*lead, 8, 128), f32)

        held = pl.pallas_call(
            functools.partial(kernel, tiles, sects, subs),
            out_shape=(
                pltpu.VMEM(air_state.shape, f32),
                pltpu.VMEM((groups, rows, 128), f32),
                pltpu.VMEM((groups, rows, 128), f32),
            ),
            in_specs=[hbm] * 5 + [smem] * 5,
            out_specs=(vmem, vmem, vmem),
            scratch_shapes=[
                pltpu.VMEM((STEPS, 4, depth + 2, 8, width), f32),
                pltpu.VMEM((STEPS, 2, 4, depth, 8, width), f32),
                blocks(14, SEG),
                blocks(14, SEG),
                blocks(14, SEG),
                blocks(REFINE, SEG),
                blocks(REFINE, SEG),
                blocks(REFINE, SEG),
                blocks(REFINE, SEG),
                blocks(REFINE, SEG),
                blocks(REFINE, SEG),
                pltpu.VMEM((2, groups, rows, 128), f32),
                pltpu.VMEM((2, groups, rows, 128), jnp.int32),
                pltpu.VMEM((cols, cols), bf16),
                pltpu.VMEM((cols, cols), bf16),
                pltpu.VMEM((256, 512), bf16),
                pltpu.VMEM((256, 128), bf16),
                blocks(2, 5),
                blocks(STEPS + 1),
                blocks(STEPS + 1, SEG + 1),
                blocks(STEPS + 1, SEG + 1),
                blocks(STEPS + 1, 2),
                blocks(STEPS + 1, 2),
                pltpu.VMEM((STEPS, bands, 16, 128), f32),
                pltpu.VMEM((STEPS, bands, 16, 128), f32),
                blocks(STEPS, bands, 2),
                blocks(STEPS, bands, 2),
                pltpu.VMEM((STEPS, 16, 128), f32),
                pltpu.VMEM((STEPS, bands, 16, 128), f32),
                blocks(STEPS - 1, bands, 2),
                blocks(STEPS - 1, bands, 2),
                dma((4, groups + 1)),
                dma((STEPS + 1, 8)),
                dma((STEPS + 1, 8)),
                dma((STEPS, bands)),
                dma((STEPS, bands)),
                dma((STEPS, bands)),
                dma((STEPS, bands)),
                dma((2 * STEPS - 1, 2)),
                dma((2 * STEPS - 1, 2)),
                dma((STEPS, 4)),
                dma((STEPS, 4)),
            ],
            compiler_params=pltpu.CompilerParams(
                collective_id=0, has_side_effects=True, vmem_limit_bytes=56 * 1024 * 1024
            ),
        )(air_state, fire_level, *rest)
        held = [pltpu.with_memory_space_constraint(x, pltpu.VMEM) for x in held]
        return pl.pallas_call(
            release,
            out_shape=(
                jax.ShapeDtypeStruct(air_state.shape, f32),
                jax.ShapeDtypeStruct(fire_level.shape, f32),
                jax.ShapeDtypeStruct(fire_level.shape, f32),
            ),
            in_specs=[vmem] * 3,
            out_specs=(hbm, hbm, hbm),
            scratch_shapes=[dma((3, groups))],
        )(*held)

    return jax.shard_map(
        local,
        mesh=mesh,
        in_specs=(air_spec, fire_spec, fire_spec, fire_spec, fire_spec) + (P(),) * 5,
        out_specs=(air_spec, fire_spec, fire_spec),
        check_vma=False,
    )
```

```python
import functools
import math

import jax
import jax.numpy as jnp
from jax import lax
from jax.experimental import pallas as pl
from jax.experimental.pallas import tpu as pltpu
from jax.sharding import PartitionSpec as P

LEVELS = 80
REFINE = 10
NFUEL = 13
STEPS = 4
SUBSTEPS = 4
DEEP = 4
SEG = REFINE // 2
MESH = pl.DeviceIdType.MESH
TINY = 1.1754944e-38
f32 = jnp.float32
bf16 = jnp.bfloat16


def split(value, axis, pieces):
    parts = []
    for _ in range(pieces):
        parts.append(value.astype(bf16))
        value = value - parts[-1].astype(f32)
    return jnp.concatenate(parts, axis=axis)


def indicator(mask, value=1.0):
    return jnp.where(mask, value, 0.0).astype(bf16)


def kernel(
    tiles,
    sects,
    subs,
    air_in,
    level_in,
    fuel_in,
    class_in,
    ign_in,
    plan_in,
    rate_in,
    burn_in,
    heat_in,
    moist_in,
    air_out,
    level_out,
    fuel_out,
    air_0,
    air_1,
    air_2,
    air_3,
    xh,
    xa,
    xb,
    rate,
    fuel,
    binv,
    heat,
    moist,
    ign,
    bsum,
    stage,
    turned,
    gather,
    spread,
    wmat,
    smat,
    wnd,
    es,
    gs,
    hb,
    er,
    dg,
    wsend,
    wrecv,
    hsend,
    hrecv,
    fsend,
    frecv,
    gsend,
    grecv,
    plan,
    t_rate,
    t_burn,
    t_heat,
    t_moist,
    in_s,
    table_s,
    fire_s,
    fire_r,
    wind_s,
    wind_r,
    flux_s,
    flux_r,
    rim_s,
    rim_r,
    halo_s,
    halo_r,
):
    air = (air_0, air_1, air_2, air_3)
    bands = sects * subs
    depth = air_in.shape[1]
    width = air_in.shape[3]
    rows, cols = level_in.shape
    coarse = cols // REFINE
    groups = cols // 128
    tile_at = lax.axis_index("tile")
    sect_at = lax.axis_index("sect")
    sub_at = lax.axis_index("sub")
    band = sect_at * subs + sub_at
    not_first = tile_at > 0
    not_final = tile_at < tiles - 1
    band_low = band > 0
    band_high = band < bands - 1

    def device(tile_step, at_band):
        return {
            "tile": tile_at + tile_step,
            "sect": at_band // subs,
            "sub": at_band % subs,
        }

    def both(a, b):
        return jnp.logical_and(a, b)

    pending = []

    def send(condition, src, dst, send_sem, recv_sem, where):
        def make():
            return pltpu.make_async_remote_copy(
                src_ref=src,
                dst_ref=dst,
                send_sem=send_sem,
                recv_sem=recv_sem,
                device_id=where,
                device_id_type=MESH,
            )

        @pl.when(condition)
        def _():
            make().start()

        pending.append((condition, make))

    def drain():
        for condition, make in pending:

            @pl.when(condition)
            def _(make=make):
                make().wait_send()

        pending.clear()

    def send_group(condition, parts, whole, send_sem, recv_sem, wheres):
        def make(src, dst, where):
            return pltpu.make_async_remote_copy(
                src_ref=src,
                dst_ref=dst,
                send_sem=send_sem,
                recv_sem=recv_sem,
                device_id=where,
                device_id_type=MESH,
            )

        @pl.when(condition)
        def _():
            for (src, dst), where in zip(parts, wheres):
                make(src, dst, where).start()

        pending.append((condition, lambda: make(whole, whole, wheres[0])))

    def receive(condition, dst, recv_sem, send_sem, where):
        @pl.when(condition)
        def _():
            pltpu.make_async_remote_copy(
                src_ref=dst,
                dst_ref=dst,
                send_sem=send_sem,
                recv_sem=recv_sem,
                device_id=where,
                device_id_type=MESH,
            ).wait_recv()

    def iota(shape, dim):
        return lax.broadcasted_iota(jnp.int32, shape, dim)

    barrier = pltpu.get_barrier_semaphore()
    for tile_step, condition in ((0, None), (-1, not_first), (1, not_final)):
        for j in range(bands):
            ok = (band != j) if condition is None else condition

            @pl.when(ok)
            def _(tile_step=tile_step, j=j):
                pl.semaphore_signal(
                    barrier, inc=1, device_id=device(tile_step, j), device_id_type=MESH
                )

    def fetch(array, held, slot):
        for v in range(groups):
            pltpu.make_async_copy(
                array.at[:, pl.ds(128 * v, 128)], held.at[v], in_s.at[slot]
            ).start()
        return pltpu.make_async_copy(held, held, in_s.at[slot])

    fire_copies = [
        fetch(class_in, turned.at[0], 0),
        fetch(ign_in, turned.at[1], 1),
        fetch(level_in, stage.at[0], 2),
    ]
    tables = [
        pltpu.make_async_copy(src, dst, table_s.at[k])
        for k, (src, dst) in enumerate(
            (
                (rate_in, t_rate),
                (plan_in, plan),
                (burn_in, t_burn),
                (heat_in, t_heat),
                (moist_in, t_moist),
            )
        )
    ]
    for copy in tables:
        copy.start()
    air_copy = pltpu.make_async_copy(air_in, air[0].at[:, pl.ds(1, depth)], in_s.at[3])
    air_copy.start()
    fuel_copy = fetch(fuel_in, stage.at[1], 4)

    spot = iota((16, cols), 1)
    spot = SEG * (spot % 128) + spot // 128
    line16 = iota((16, cols), 0)

    def make_gather(i, carry):
        at = pl.ds(pl.multiple_of(i * 16, 16), 16)
        gather[at, :] = indicator(spot == line16 + 16 * i)
        return carry

    lax.fori_loop(0, cols // 16, make_gather, 0, unroll=4)

    sub = iota((8, 128), 0)
    lane = iota((8, 128), 1)
    octet = lane // 8
    inner = lane % 8 < 4
    edge_w = sub == jnp.where(not_first, -1, 0)
    edge_e = sub == jnp.where(not_final, -1, 7)
    edge_s = lane == jnp.where(band_low, -1, 0)
    edge_n = lane == jnp.where(band_high, -1, 127)
    strip_w = both(edge_w, octet == 3)
    strip_e = both(edge_e, octet == 12)

    def rolled(value, shift, axis):
        shift = shift % value.shape[axis]
        return pltpu.roll(value, shift, axis) if shift else value

    row8 = iota((8, width), 0)
    total_col = sum(math.exp(-k / LEVELS) for k in range(LEVELS))
    total_prof = sum(math.exp(-2.0 * k / LEVELS) for k in range(LEVELS))
    col_base = f32(0.0)
    prof_base = f32(0.0)
    for j in range(bands):
        here = band == j
        col_base = jnp.where(here, f32(math.exp(-j * depth / LEVELS) / total_col), col_base)
        prof_base = jnp.where(
            here, f32(LEVELS * math.exp(-2.0 * j * depth / LEVELS) / total_prof), prof_base
        )
    col_ratio = math.exp(-1.0 / LEVELS)
    prof_ratio = math.exp(-2.0 / LEVELS)

    def send_wind(c, total_u, total_v):
        stacked = jnp.concatenate([total_u, total_v], axis=0)
        for j in range(bands):
            shift = (128 // 4 - coarse * j) % width
            window = (pltpu.roll(stacked, shift, 1) if shift else stacked)[:, :128]
            wsend[c, j] = window
            for k in range(2):
                low = jnp.broadcast_to(window[8 * k : 8 * k + 1], (8, 128))
                high = jnp.broadcast_to(window[8 * k + 7 : 8 * k + 8], (8, 128))
                hsend[c, j, k] = jnp.where(sub < 4, high, low)

            @pl.when(band == j)
            def _(window=window, j=j):
                wrecv[c, j] = window

        for j in range(bands):
            send(
                band != j,
                wsend.at[c, j],
                wrecv.at[c, band],
                wind_s.at[j],
                wind_r.at[c % 2, band],
                device(0, j),
            )
        for way, tile_step, ok in ((0, 1, not_final), (1, -1, not_first)):
            part = pl.ds(4 * way, 4)
            send_group(
                ok,
                [
                    (hsend.at[c, j, :, part, :], hrecv.at[c, band, :, part, :])
                    for j in range(bands)
                ],
                hsend.at[c, :, :, part, :],
                rim_s.at[0, way],
                rim_r.at[c % 2, way],
                [device(tile_step, j) for j in range(bands)],
            )

    def wait_wind(c):
        for j in range(bands):
            receive(band != j, wrecv.at[c, j], wind_r.at[c % 2, j], wind_s.at[j], device(0, j))
        for way, tile_step, ok in ((0, -1, not_first), (1, 1, not_final)):
            part = pl.ds(4 * way, 4)
            receive(
                ok,
                hrecv.at[c, :, :, part, :],
                rim_r.at[c % 2, way],
                rim_s.at[0, way],
                device(tile_step, 0),
            )
        own = wrecv[c, 0]
        beyond = [hrecv[c, 0, 0], hrecv[c, 0, 1]]
        for j in range(1, bands):
            own = own + wrecv[c, j]
            beyond = [beyond[0] + hrecv[c, j, 0], beyond[1] + hrecv[c, j, 1]]
        together = jnp.concatenate([own] + beyond, axis=0)
        wide = jnp.dot(split(together, 1, 2), wmat[...], preferred_element_type=f32)
        for k in range(2):
            own, beyond = wide[8 * k : 8 * k + 8], wide[16 + 8 * k : 24 + 8 * k]
            wnd[k, 0] = own[:, :128]
            wnd[k, 1] = beyond[:, :128]
            for at in (1, 2):
                here = own[:, 128 * at : 128 * at + 128]
                there = beyond[:, 128 * at : 128 * at + 128]
                below = jnp.where(sub == 0, there, pltpu.roll(here, 1, 0))
                above = jnp.where(sub == 7, there, pltpu.roll(here, 7, 0))
                wnd[k, at + 1] = jnp.where(
                    octet < 3, below, jnp.where(octet >= 13, above, here)
                )
            wnd[k, 4] = beyond[:, 384:]

    def send_air(c):
        send(
            not_final,
            air[c].at[:, pl.ds(1, depth), pl.ds(7, 1), :],
            xh.at[c, 0, :, :, pl.ds(7, 1), :],
            halo_s.at[0],
            halo_r.at[c % 2, 0],
            device(1, band),
        )
        send(
            not_first,
            air[c].at[:, pl.ds(1, depth), pl.ds(0, 1), :],
            xh.at[c, 1, :, :, pl.ds(0, 1), :],
            halo_s.at[1],
            halo_r.at[c % 2, 1],
            device(-1, band),
        )
        send(
            band_high,
            air[c].at[:, depth],
            air[c].at[:, 0],
            halo_s.at[2],
            halo_r.at[c % 2, 2],
            device(0, band + 1),
        )
        send(
            band_low,
            air[c].at[:, 1],
            air[c].at[:, depth + 1],
            halo_s.at[3],
            halo_r.at[c % 2, 3],
            device(0, band - 1),
        )

    def wait_air(c):
        receive(
            not_first,
            xh.at[c, 0, :, :, pl.ds(7, 1), :],
            halo_r.at[c % 2, 0],
            halo_s.at[0],
            device(-1, band),
        )
        receive(
            not_final,
            xh.at[c, 1, :, :, pl.ds(0, 1), :],
            halo_r.at[c % 2, 1],
            halo_s.at[1],
            device(1, band),
        )
        receive(band_low, air[c].at[:, 0], halo_r.at[c % 2, 2], halo_s.at[2], device(0, band - 1))
        receive(
            band_high,
            air[c].at[:, depth + 1],
            halo_r.at[c % 2, 3],
            halo_s.at[3],
            device(0, band + 1),
        )

    def reorder(load):
        return jnp.concatenate(
            [
                jnp.concatenate([load(v, pl.ds(q, 8, stride=REFINE)) for v in range(groups)], axis=1)
                for q in range(REFINE)
            ],
            axis=0,
        )

    for copy in fire_copies:
        copy.wait()
    tables[0].wait()
    kinds = reorder(
        lambda v, at: (turned[0, v, at, :] + 16 * turned[1, v, at, :]).astype(f32)
    ).astype(bf16)
    pieces = split(reorder(lambda v, at: stage[0, v, at, :]), 0, 3)
    found = jnp.dot(
        jnp.concatenate([pieces, kinds], axis=0), gather[...], preferred_element_type=f32
    )
    together = found[:rows] + found[rows : 2 * rows] + found[2 * rows : 3 * rows]
    kinds = found[3 * rows :]
    for q in range(REFINE):
        for p in range(SEG):
            kind = kinds[8 * q : 8 * q + 8, 128 * p : 128 * p + 128]
            when = jnp.floor(kind * (1.0 / 16.0))
            now = together[8 * q : 8 * q + 8, 128 * p : 128 * p + 128]
            ign[q, p] = when
            moist[q, p] = kind - 16.0 * when
            xa[q + 1, p] = jnp.where(when <= 0.0, jnp.minimum(now, -1.0), now)

    def find_rate(q, carry):
        for p in range(SEG):
            kind = moist[q, p]
            value = jnp.full((8, 128), t_rate[0], f32)
            for k in range(1, NFUEL):
                value = jnp.where(kind == float(k), t_rate[k], value)
            rate[q + 1, p] = value
        return carry

    lax.fori_loop(0, REFINE, find_rate, 0, unroll=2)

    def outline(e, ref):
        def edge(q, found):
            x = [ref[q + 1, p] for p in range(SEG)]
            near = pltpu.roll(x[SEG - 1], 1, 1)
            for k in range(1, DEEP):
                near = jnp.where(lane == k, pltpu.roll(x[SEG - 1 - k], k + 1, 1), near)
            for k in range(DEEP):
                near = jnp.where(lane == 127 - k, pltpu.roll(x[k], 127 - k, 1), near)
            return jnp.where(octet == q + 3, pltpu.roll(near, 8 * q + 28, 1), found)

        found = lax.fori_loop(0, REFINE, edge, jnp.zeros((8, 128), f32), unroll=10)
        es[e] = found
        gs[e, SEG] = jnp.where(
            sub < 4,
            jnp.broadcast_to(found[7:8], (8, 128)),
            jnp.broadcast_to(found[0:1], (8, 128)),
        )

        def border(p, carry):
            value = rolled(ref[REFINE, p], 1, 0)
            for k in range(1, DEEP):
                value = jnp.where(sub == k, rolled(ref[REFINE - k, p], k + 1, 0), value)
            for k in range(DEEP):
                value = jnp.where(sub == 4 + k, rolled(ref[DEEP - k, p], 4 + k, 0), value)
            gs[e, p] = value
            return carry

        lax.fori_loop(0, SEG, border, 0, unroll=5)

    def fields(c):
        return pl.ds(0, 2) if c == 0 else pl.ds(1 + c, 1)

    def send_outline(c):
        at = fields(c)
        for way, tile_step, ok in ((0, 1, not_final), (1, -1, not_first)):
            part = pl.ds(4 * way, 4)
            send(
                ok,
                gs.at[at, :, part, :],
                hb.at[at, :, part, :],
                fire_s.at[way],
                fire_r.at[c % 2, way],
                device(tile_step, band),
            )
        for side, band_step, ok in ((0, 1, band_high), (1, -1, band_low)):
            send(
                ok,
                es.at[at],
                er.at[at, side],
                fire_s.at[2 + side],
                fire_r.at[c % 2, 2 + side],
                device(0, band + band_step),
            )
            for way, tile_step, also in ((0, 1, not_final), (1, -1, not_first)):
                send(
                    both(ok, also),
                    es.at[at, pl.ds(7 - 7 * way, 1), :],
                    dg.at[at, side, pl.ds(7 * way, 1), :],
                    fire_s.at[4 + 2 * side + way],
                    fire_r.at[c % 2, 4 + 2 * side + way],
                    device(tile_step, band + band_step),
                )

    def wait_outline(c):
        at = fields(c)
        for way, tile_step, ok in ((0, -1, not_first), (1, 1, not_final)):
            receive(
                ok,
                hb.at[at, :, pl.ds(4 * way, 4), :],
                fire_r.at[c % 2, way],
                fire_s.at[way],
                device(tile_step, band),
            )
        for side, band_step, ok in ((0, -1, band_low), (1, 1, band_high)):
            receive(
                ok,
                er.at[at, side],
                fire_r.at[c % 2, 2 + side],
                fire_s.at[2 + side],
                device(0, band + band_step),
            )
            for way, tile_step, also in ((0, -1, not_first), (1, 1, not_final)):
                receive(
                    both(ok, also),
                    dg.at[at, side, pl.ds(7 * way, 1), :],
                    fire_r.at[c % 2, 4 + 2 * side + way],
                    fire_s.at[4 + 2 * side + way],
                    device(tile_step, band + band_step),
                )

    def surround(e, ref):
        for p in range(SEG):
            ref[12, p] = hb[e, p]
        mine, beyond = es[e], hb[e, SEG]

        def strip(here, there):
            below = jnp.where(sub == 0, there, pltpu.roll(here, 1, 0))
            above = jnp.where(sub == 7, there, pltpu.roll(here, 7, 0))
            return jnp.where(
                octet < 3,
                pltpu.roll(below, 48, 1),
                jnp.where(octet >= 13, pltpu.roll(above, 80, 1), here),
            )

        low = strip(jnp.where(inner, mine, er[e, 0]), jnp.where(inner, beyond, dg[e, 0]))
        high = strip(jnp.where(inner, er[e, 1], mine), jnp.where(inner, dg[e, 1], beyond))
        mixed = jnp.where(inner, high, low)
        corner = mixed
        for k in range(3):
            corner = jnp.where(sub == k, rolled(rolled(mixed, 108 + 8 * k, 1), k, 0), corner)
            corner = jnp.where(sub == 7 - k, rolled(rolled(mixed, 20 - 8 * k, 1), -k, 0), corner)
        ref[13, 0] = low
        ref[13, 1] = high
        ref[13, 2] = corner

    outline(0, rate)
    outline(1, xa)
    nothing = jnp.zeros((8, width), f32)
    air_copy.wait()

    def first_air(i, carry):
        weight, total_u, total_v = carry
        total_u = total_u + weight * air[0][2, i + 1]
        total_v = total_v + weight * air[0][3, i + 1]
        return weight * f32(col_ratio), total_u, total_v

    _, total_u, total_v = lax.fori_loop(
        0, depth, first_air, (col_base, nothing, nothing), unroll=4
    )

    expected = (
        bands - 1 + bands * (not_first.astype(jnp.int32) + not_final.astype(jnp.int32))
    )
    pl.semaphore_wait(barrier, expected)

    send_air(0)
    send_wind(0, total_u, total_v)
    send_outline(0)

    @pl.when(jnp.logical_not(not_first))
    def _():
        def zero(i, carry):
            for c in range(STEPS):
                for f in range(4):
                    xh[c, 0, f, i] = jnp.zeros((8, width), f32)
            return carry

        lax.fori_loop(0, depth, zero, 0)
        grecv[:, :, :, 4:] = jnp.zeros((STEPS - 1, bands, 2, 4, 128), f32)

    @pl.when(jnp.logical_not(not_final))
    def _():
        grecv[:, :, :, :4] = jnp.zeros((STEPS - 1, bands, 2, 4, 128), f32)

        def zero(i, carry):
            for c in range(STEPS):
                for f in range(4):
                    xh[c, 1, f, i] = jnp.zeros((8, width), f32)
            return carry

        lax.fori_loop(0, depth, zero, 0)

    @pl.when(jnp.logical_not(band_low))
    def _():
        for c in range(STEPS):
            air[c][:, 0] = jnp.zeros((4, 8, width), f32)

    @pl.when(jnp.logical_not(band_high))
    def _():
        for c in range(STEPS):
            air[c][:, depth + 1] = jnp.zeros((4, 8, width), f32)

    column = iota((16, cols), 1)

    def make_spread(i, carry):
        at = pl.ds(pl.multiple_of(i * 16, 16), 16)
        spread[at, :] = indicator(column == SEG * (line16 + 16 * (i % 8)) + i // 8)
        return carry

    source, place = iota((128, 512), 0), iota((128, 512), 1)
    block, place = place // 128, place % 128
    near = place % 8 < 4
    first = jnp.where(block == 0, 32 + place // 2, jnp.where(near, 32, 31))
    second = jnp.where(
        block == 2, jnp.where(near, 96, 95), jnp.where(place < 64, 31, 96)
    )
    pattern = indicator(source == jnp.where(block < 2, first, second), 0.5)
    wmat[:128, :] = pattern
    wmat[128:, :] = pattern
    source, place = iota((128, 128), 0), iota((128, 128), 1)
    pattern = indicator(place == source // 2 + coarse * (band % 2))
    smat[:128, :] = pattern
    smat[128:, :] = pattern

    for copy in tables[1:]:
        copy.wait()

    def lookup(q, carry):
        for p in range(SEG):
            kind = moist[q, p]
            burn = jnp.full((8, 128), t_burn[0], f32)
            hot = jnp.full((8, 128), t_heat[0], f32)
            wet = jnp.full((8, 128), t_moist[0], f32)
            for k in range(1, NFUEL):
                same = kind == float(k)
                burn = jnp.where(same, t_burn[k], burn)
                hot = jnp.where(same, t_heat[k], hot)
                wet = jnp.where(same, t_moist[k], wet)
            binv[q, p] = 1.0 / burn
            heat[q, p] = hot
            moist[q, p] = wet
            bsum[q, p] = jnp.zeros((8, 128), f32)
        return carry

    lax.fori_loop(0, REFINE, lookup, 0)
    fuel_copy.wait()
    pieces = split(reorder(lambda v, at: stage[1, v, at, :]), 0, 3)
    found = jnp.dot(pieces, gather[...], preferred_element_type=f32)
    together = found[:rows] + found[rows : 2 * rows] + found[2 * rows :]
    for q in range(REFINE):
        for p in range(SEG):
            fuel[q, p] = together[8 * q : 8 * q + 8, 128 * p : 128 * p + 128]
    lax.fori_loop(0, cols // 16, make_spread, 0, unroll=4)

    def uphill(d):
        return jnp.maximum(d, 0.0) * d

    def downhill(d):
        return jnp.minimum(d, 0.0) * d

    def moved(here, dw, de, ds, dn, speed, wu, wv):
        square = (uphill(dw) + downhill(de)) + (uphill(ds) + downhill(dn))
        steep = square * lax.rsqrt(jnp.maximum(square, TINY))
        gx, gy = dw + de, ds + dn
        tail = (wu * gx + wv * gy) * lax.rsqrt(gx * gx + gy * gy + 4.0)
        return here - (speed * (1.0 + jnp.maximum(tail, 0.0))) * steep

    def substep(src, dst, fire_step):
        low, high, corner = src[13, 0], src[13, 1], src[13, 2]
        mixed = jnp.where(inner, high, low)
        top, border, bottom = [], [], []
        for p in range(SEG):
            first, final, beyond = src[1, p], src[REFINE, p], src[12, p]
            border.append(beyond)
            top.append(
                jnp.where(
                    edge_w, first, jnp.where(sub == 0, beyond, pltpu.roll(final, 1, 0))
                )
            )
            src[11, p] = jnp.where(
                edge_e, final, jnp.where(sub == 7, beyond, pltpu.roll(first, 7, 0))
            )

        def across(x, outer):
            south = jnp.where(lane == 0, outer, pltpu.roll(x[SEG - 1], 1, 1))
            north = jnp.where(lane == 127, outer, pltpu.roll(x[0], 127, 1))
            south = jnp.where(edge_s, x[0], south)
            north = jnp.where(edge_n, x[SEG - 1], north)
            line = [south] + x + [north]
            return [line[k + 1] - line[k] for k in range(SEG + 1)]

        wu, wv = wnd[0, 0], wnd[1, 0]

        def line(q, carry):
            x, dw = carry
            after = [src[q + 2, p] for p in range(SEG)]
            dh = across(x, pltpu.roll(mixed, 100 - 8 * q, 1))
            de = []
            for p in range(SEG):
                de.append(after[p] - x[p])
                new = moved(
                    x[p], dw[p], de[p], dh[p], dh[p + 1], fire_step * rate[q + 1, p], wu, wv
                )
                dst[q + 1, p] = new
                bsum[q, p] = bsum[q, p] + jnp.clip(new, -0.5, 0.5)
            return after, de

        x = [src[1, p] for p in range(SEG)]
        lax.fori_loop(0, REFINE, line, (x, [x[p] - top[p] for p in range(SEG)]), unroll=10)

        wu, wv = wnd[0, 1], wnd[1, 1]
        dh = across(border, corner)
        for p in range(SEG):
            here = border[p]
            west = jnp.where(sub == 7, src[REFINE, p], pltpu.roll(here, 7, 0))
            east = jnp.where(sub == 0, src[1, p], pltpu.roll(here, 1, 0))
            dst[12, p] = moved(
                here, here - west, east - here, dh[p], dh[p + 1], fire_step * rate[12, p], wu, wv
            )
        for k, here in enumerate((low, high)):
            west = jnp.where(strip_w, here, pltpu.roll(here, 8, 1))
            east = jnp.where(strip_e, here, pltpu.roll(here, 120, 1))
            south, north = pltpu.roll(here, 127, 1), pltpu.roll(here, 1, 1)
            dst[13, k] = moved(
                here,
                here - west,
                east - here,
                here - south,
                north - here,
                fire_step * rate[13, k],
                wnd[0, 2 + k],
                wnd[1, 2 + k],
            )
        west = jnp.where(sub == 7, pltpu.roll(mixed, 28, 1), pltpu.roll(corner, 7, 0))
        east = jnp.where(sub == 0, pltpu.roll(mixed, 100, 1), pltpu.roll(corner, 1, 0))
        south = jnp.where(lane == 127, border[SEG - 1], pltpu.roll(corner, 127, 1))
        north = jnp.where(lane == 0, border[0], pltpu.roll(corner, 1, 1))
        dst[13, 2] = moved(
            corner,
            corner - west,
            east - corner,
            corner - south,
            north - corner,
            fire_step * rate[13, 2],
            wnd[0, 4],
            wnd[1, 4],
        )

    lane_a = lax.broadcasted_iota(jnp.int32, (8, width), 1)

    def write(c, f, i, value):
        if c == STEPS - 1:
            air_out[f, i] = value
        else:
            air[c + 1][f, i + 1] = value

    def wait_flux(c):
        for j in range(bands):
            receive(band != j, frecv.at[c, j], flux_r.at[c % 2, j], flux_s.at[j], device(0, j))
        whole = jnp.concatenate(
            [frecv[c, 2 * k] + frecv[c, 2 * k + 1] for k in range(width // 128)], axis=1
        )
        return whole[:8], whole[8:]

    def wait_rim(c):
        for way, tile_step, ok in ((0, -1, not_first), (1, 1, not_final)):
            part = pl.ds(4 - 4 * way, 4)
            receive(
                ok,
                grecv.at[c, :, :, part, :],
                rim_r.at[2 + c % 2, way],
                rim_s.at[1, way],
                device(tile_step, 0),
            )
        return [
            jnp.concatenate(
                [grecv[c, 2 * k, f] + grecv[c, 2 * k + 1, f] for k in range(width // 128)],
                axis=1,
            )
            for f in range(2)
        ]

    def force_air(c, flux):
        def force(i, weight):
            for f in range(2):
                now = air_out[f, i] if c == STEPS - 1 else air[c + 1][f, i + 1]
                write(c, f, i, now + weight * flux[f])
            return weight * f32(prof_ratio)

        lax.fori_loop(0, depth, force, prof_base * f32(2.0), unroll=4)

    def move_air(c):
        rim = None
        drain()
        if c > 0:
            flux = wait_flux(c - 1)
            force_air(c - 1, flux)
        wait_air(c)
        if c > 0:
            low = jnp.where(band_low, prof_base * f32(2.0 / prof_ratio), 0.0)
            high = jnp.where(band_high, prof_base * f32(2.0 * prof_ratio**depth), 0.0)
            for f in range(2):
                air[c][f, 0] = air[c][f, 0] + low * flux[f]
                air[c][f, depth + 1] = air[c][f, depth + 1] + high * flux[f]
            rim = wait_rim(c - 1)
        final = c == STEPS - 1

        def update(i, carry):
            weight, share, total_u, total_v = carry
            u, v = air[c][2, i + 1], air[c][3, i + 1]
            to_w = 0.02 + 0.1 * jnp.maximum(u, 0.0)
            to_e = 0.02 - 0.1 * jnp.minimum(u, 0.0)
            to_s = 0.02 + 0.1 * jnp.maximum(v, 0.0)
            to_n = 0.02 - 0.1 * jnp.minimum(v, 0.0)
            to_here = 0.96 - ((to_w + to_e) + (to_s + to_n))
            to_s = jnp.where(lane_a == 0, 0.0, to_s)
            to_n = jnp.where(lane_a == width - 1, 0.0, to_n)
            lift_x = lift_s = lift_n = None
            for f in range(4):
                here = air[c][f, i + 1]
                west, east = xh[c, 0, f, i], xh[c, 1, f, i]
                if c > 0 and f < 2:
                    west, east = west + share * rim[f], east + share * rim[f]
                west = pltpu.roll(jnp.where(row8 == 7, west, here), 1, 0)
                east = pltpu.roll(jnp.where(row8 == 0, east, here), 7, 0)
                south, north = pltpu.roll(here, 1, 1), pltpu.roll(here, width - 1, 1)
                new = (to_here * here + (to_w * west + to_e * east)) + (
                    (to_s * south + to_n * north) + 0.02 * (air[c][f, i] + air[c][f, i + 2])
                )
                if f == 0:
                    lift_x, lift_s, lift_n = east - west, south, north
                elif f == 1:
                    lift_x = lift_x + 0.6 * (east - west)
                    lift_s = jnp.where(lane_a == 0, 0.0, lift_s + 0.6 * south)
                    lift_n = jnp.where(lane_a == width - 1, 0.0, lift_n + 0.6 * north)
                elif f == 2:
                    new = new + 0.015 * lift_x
                    total_u = total_u + weight * new
                else:
                    new = new + 0.015 * (lift_n - lift_s)
                    total_v = total_v + weight * new
                write(c, f, i, new)
            return weight * f32(col_ratio), share * f32(prof_ratio), total_u, total_v

        carry = (col_base, prof_base * f32(2.0), nothing, nothing)
        _, _, total_u, total_v = lax.fori_loop(0, depth, update, carry, unroll=10)
        if not final:
            send_wind(c + 1, total_u, total_v)
            send_air(c + 1)

    def burn_fire(c, fire_step):
        def burn(q, carry):
            hot, wet = carry
            for p in range(SEG):
                now = fuel[q, p]
                spent = (float(SUBSTEPS) * 0.5 - bsum[q, p]) * binv[q, p]
                remain = now * jnp.exp(-fire_step * spent)
                used = now - remain
                fuel[q, p] = remain
                bsum[q, p] = jnp.zeros((8, 128), f32)
                hot = hot + used * heat[q, p]
                wet = wet + used * moist[q, p]
            return hot, wet

        zero = jnp.zeros((8, 128), f32)
        hot, wet = lax.fori_loop(0, REFINE, burn, (zero, zero), unroll=10)
        flux = jnp.dot(
            split(jnp.concatenate([hot, wet], axis=0), 1, 2),
            smat[...],
            preferred_element_type=f32,
        ) * f32(1.0 / (REFINE * REFINE))
        fsend[c] = flux
        for j in range(bands):

            @pl.when(band == j)
            def _(j=j):
                frecv[c, j] = flux

            send(
                band != j,
                fsend.at[c],
                frecv.at[c, band],
                flux_s.at[j],
                flux_r.at[c % 2, band],
                device(0, j),
            )
        if c == STEPS - 1:
            return
        for k in range(2):
            low = jnp.broadcast_to(flux[8 * k : 8 * k + 1], (8, 128))
            high = jnp.broadcast_to(flux[8 * k + 7 : 8 * k + 8], (8, 128))
            for j in range(bands):
                gsend[c, j, k] = jnp.where(sub < 4, low, high)
        for way, tile_step, ok in ((0, 1, not_final), (1, -1, not_first)):
            part = pl.ds(4 - 4 * way, 4)
            send_group(
                ok,
                [
                    (gsend.at[c, j, :, part, :], grecv.at[c, band, :, part, :])
                    for j in range(bands)
                ],
                gsend.at[c, :, :, part, :],
                rim_s.at[1, way],
                rim_r.at[2 + c % 2, way],
                [device(tile_step, j) for j in range(bands)],
            )

    def burn_window(c):
        fire_step = plan[c].astype(f32) * f32(0.15)
        if c == STEPS - 1:
            drain()
        wait_wind(c)
        wait_outline(c)
        if c == 0:
            surround(0, rate)
        surround(1 + c, xa)

        def pair(i, carry):
            substep(xa, xb, fire_step)
            substep(xb, xa, fire_step)
            return carry

        lax.fori_loop(0, SUBSTEPS // 2, pair, 0)
        burn_fire(c, fire_step)
        if c < STEPS - 1:

            def ignite(q, carry):
                for p in range(SEG):
                    now = xa[q + 1, p]
                    xa[q + 1, p] = jnp.where(
                        ign[q, p] <= float(c + 1), jnp.minimum(now, -1.0), now
                    )
                return carry

            lax.fori_loop(0, REFINE, ignite, 0, unroll=10)
            outline(2 + c, xa)
            send_outline(1 + c)

    def give(load, array):
        values = jnp.concatenate(
            [
                jnp.concatenate([load(q, p) for p in range(SEG)], axis=1)
                for q in range(REFINE)
            ],
            axis=0,
        )
        found = jnp.dot(split(values, 0, 3), spread[...], preferred_element_type=f32)
        found = found[:rows] + found[rows : 2 * rows] + found[2 * rows :]
        for q in range(REFINE):
            for v in range(groups):
                array[v, pl.ds(q, 8, stride=REFINE), :] = found[
                    8 * q : 8 * q + 8, 128 * v : 128 * v + 128
                ]

    for c in range(STEPS - 1):
        move_air(c)
        burn_window(c)
    burn_window(STEPS - 1)
    give(lambda q, p: xa[q + 1, p], level_out)
    move_air(STEPS - 1)
    give(lambda q, p: fuel[q, p], fuel_out)
    drain()
    force_air(STEPS - 1, wait_flux(STEPS - 1))


def release(air, level, fuel, air_out, level_out, fuel_out, sems):
    copies = [pltpu.make_async_copy(air, air_out, sems.at[0])]
    copies[0].start()
    for k, (held, out) in enumerate(((level, level_out), (fuel, fuel_out))):
        for v in range(held.shape[0]):
            pltpu.make_async_copy(
                held.at[v], out.at[:, pl.ds(128 * v, 128)], sems.at[1 + k]
            ).start()
        copies.append(pltpu.make_async_copy(held, held, sems.at[1 + k]))
    for copy in copies:
        copy.wait()


def solution(mesh):
    tiles, sects, subs = (mesh.shape[name] for name in ("tile", "sect", "sub"))
    bands = sects * subs
    air_spec = P(None, ("sect", "sub"), ("group", "tile"), None)
    fire_spec = P(("group", "tile"), ("sect", "sub"))

    def local(air_state, fire_level, *rest):
        depth, width = air_state.shape[1], air_state.shape[3]
        rows, cols = fire_level.shape
        groups = cols // 128
        assert air_state.shape[2] == 8 and cols == 64 * REFINE and rows == 8 * REFINE
        vmem = pl.BlockSpec(memory_space=pltpu.VMEM)
        hbm = pl.BlockSpec(memory_space=pltpu.HBM)
        dma = pltpu.SemaphoreType.DMA

        def blocks(*lead):
            return pltpu.VMEM((*lead, 8, 128), f32)

        held = pl.pallas_call(
            functools.partial(kernel, tiles, sects, subs),
            out_shape=(
                pltpu.VMEM(air_state.shape, f32),
                pltpu.VMEM((groups, rows, 128), f32),
                pltpu.VMEM((groups, rows, 128), f32),
            ),
            in_specs=[hbm] * 10,
            out_specs=(vmem, vmem, vmem),
            scratch_shapes=[
                pltpu.VMEM((4, depth + 2, 8, width), f32),
                pltpu.VMEM((4, depth + 2, 8, width), f32),
                pltpu.VMEM((4, depth + 2, 8, width), f32),
                pltpu.VMEM((4, depth + 2, 8, width), f32),
                pltpu.VMEM((STEPS, 2, 4, depth, 8, width), f32),
                blocks(14, SEG),
                blocks(14, SEG),
                blocks(14, SEG),
                blocks(REFINE, SEG),
                blocks(REFINE, SEG),
                blocks(REFINE, SEG),
                blocks(REFINE, SEG),
                blocks(REFINE, SEG),
                blocks(REFINE, SEG),
                pltpu.VMEM((2, groups, rows, 128), f32),
                pltpu.VMEM((2, groups, rows, 128), jnp.int32),
                pltpu.VMEM((cols, cols), bf16),
                pltpu.VMEM((cols, cols), bf16),
                pltpu.VMEM((256, 512), bf16),
                pltpu.VMEM((256, 128), bf16),
                blocks(2, 5),
                blocks(STEPS + 1),
                blocks(STEPS + 1, SEG + 1),
                blocks(STEPS + 1, SEG + 1),
                blocks(STEPS + 1, 2),
                blocks(STEPS + 1, 2),
                pltpu.VMEM((STEPS, bands, 16, 128), f32),
                pltpu.VMEM((STEPS, bands, 16, 128), f32),
                blocks(STEPS, bands, 2),
                blocks(STEPS, bands, 2),
                pltpu.VMEM((STEPS, 16, 128), f32),
                pltpu.VMEM((STEPS, bands, 16, 128), f32),
                blocks(STEPS - 1, bands, 2),
                blocks(STEPS - 1, bands, 2),
                pltpu.SMEM((STEPS,), jnp.int32),
                pltpu.SMEM((NFUEL,), f32),
                pltpu.SMEM((NFUEL,), f32),
                pltpu.SMEM((NFUEL,), f32),
                pltpu.SMEM((NFUEL,), f32),
                dma((5,)),
                dma((5,)),
                dma((8,)),
                dma((2, 8)),
                dma((bands,)),
                dma((2, bands)),
                dma((bands,)),
                dma((2, bands)),
                dma((2, 2)),
                dma((4, 2)),
                dma((4,)),
                dma((2, 4)),
            ],
            compiler_params=pltpu.CompilerParams(
                collective_id=0, has_side_effects=True, vmem_limit_bytes=56 * 1024 * 1024
            ),
        )(air_state, fire_level, *rest)
        held = [pltpu.with_memory_space_constraint(x, pltpu.VMEM) for x in held]
        return pl.pallas_call(
            release,
            out_shape=(
                jax.ShapeDtypeStruct(air_state.shape, f32),
                jax.ShapeDtypeStruct(fire_level.shape, f32),
                jax.ShapeDtypeStruct(fire_level.shape, f32),
            ),
            in_specs=[vmem] * 3,
            out_specs=(hbm, hbm, hbm),
            scratch_shapes=[dma((3,))],
        )(*held)

    return jax.shard_map(
        local,
        mesh=mesh,
        in_specs=(air_spec, fire_spec, fire_spec, fire_spec, fire_spec) + (P(),) * 5,
        out_specs=(air_spec, fire_spec, fire_spec),
        check_vma=False,
    )
```

```python
import functools
import math

import jax
import jax.numpy as jnp
from jax import lax
from jax.experimental import pallas as pl
from jax.experimental.pallas import tpu as pltpu
from jax.sharding import PartitionSpec as P

LEVELS = 80
REFINE = 10
NFUEL = 13
STEPS = 4
SUBSTEPS = 4
DEEP = 4
SEG = REFINE // 2
MESH = pl.DeviceIdType.MESH
TINY = 1.1754944e-38
f32 = jnp.float32
bf16 = jnp.bfloat16


def split(value, axis, pieces):
    parts = []
    for _ in range(pieces):
        parts.append(value.astype(bf16))
        value = value - parts[-1].astype(f32)
    return jnp.concatenate(parts, axis=axis)


def indicator(mask, value=1.0):
    return jnp.where(mask, value, 0.0).astype(bf16)


def kernel(
    tiles,
    sects,
    subs,
    air_in,
    level_in,
    fuel_in,
    class_in,
    ign_in,
    plan_in,
    rate_in,
    burn_in,
    heat_in,
    moist_in,
    air_out,
    level_out,
    fuel_out,
    air_0,
    air_1,
    air_2,
    air_3,
    xh,
    xa,
    xb,
    rate,
    fuel,
    binv,
    heat,
    moist,
    ign,
    bsum,
    stage,
    turned,
    gather,
    spread,
    wmat,
    smat,
    wnd,
    es,
    gs,
    hb,
    er,
    dg,
    wsend,
    wrecv,
    hsend,
    hrecv,
    fsend,
    frecv,
    gsend,
    grecv,
    plan,
    t_rate,
    t_burn,
    t_heat,
    t_moist,
    in_s,
    table_s,
    fire_s,
    fire_r,
    wind_s,
    wind_r,
    flux_s,
    flux_r,
    rim_s,
    rim_r,
    halo_s,
    halo_r,
):
    air = (air_0, air_1, air_2, air_3)
    bands = sects * subs
    depth = air_in.shape[1]
    width = air_in.shape[3]
    rows, cols = level_in.shape
    coarse = cols // REFINE
    groups = cols // 128
    tile_at = lax.axis_index("tile")
    sect_at = lax.axis_index("sect")
    sub_at = lax.axis_index("sub")
    band = sect_at * subs + sub_at
    not_first = tile_at > 0
    not_final = tile_at < tiles - 1
    band_low = band > 0
    band_high = band < bands - 1

    def device(tile_step, at_band):
        return {
            "tile": tile_at + tile_step,
            "sect": at_band // subs,
            "sub": at_band % subs,
        }

    def both(a, b):
        return jnp.logical_and(a, b)

    pending = []

    def send(condition, src, dst, send_sem, recv_sem, where):
        def make():
            return pltpu.make_async_remote_copy(
                src_ref=src,
                dst_ref=dst,
                send_sem=send_sem,
                recv_sem=recv_sem,
                device_id=where,
                device_id_type=MESH,
            )

        @pl.when(condition)
        def _():
            make().start()

        pending.append((condition, make))

    def drain():
        for condition, make in pending:
            if condition is None:
                make().wait_send()
                continue

            @pl.when(condition)
            def _(make=make):
                make().wait_send()

        pending.clear()

    def send_group(condition, parts, whole, send_sem, recv_sem, wheres):
        def make(src, dst, where):
            return pltpu.make_async_remote_copy(
                src_ref=src,
                dst_ref=dst,
                send_sem=send_sem,
                recv_sem=recv_sem,
                device_id=where,
                device_id_type=MESH,
            )

        @pl.when(condition)
        def _():
            for (src, dst), where in zip(parts, wheres):
                make(src, dst, where).start()

        pending.append((condition, lambda: make(whole, whole, wheres[0])))

    def send_tile(parts, whole, send_sem, recv_sem):
        def make(src, dst, j):
            return pltpu.make_async_remote_copy(
                src_ref=src,
                dst_ref=dst,
                send_sem=send_sem,
                recv_sem=recv_sem,
                device_id=device(0, j),
                device_id_type=MESH,
            )

        for j, (src, dst) in enumerate(parts):

            @pl.when(band != j)
            def _(src=src, dst=dst, j=j):
                make(src, dst, j).start()

        pending.append((None, lambda: make(whole, whole, 0)))

    def receive_tile(whole, recv_sem, send_sem):
        pltpu.make_async_remote_copy(
            src_ref=whole,
            dst_ref=whole,
            send_sem=send_sem,
            recv_sem=recv_sem,
            device_id=device(0, 0),
            device_id_type=MESH,
        ).wait_recv()

    def receive(condition, dst, recv_sem, send_sem, where):
        @pl.when(condition)
        def _():
            pltpu.make_async_remote_copy(
                src_ref=dst,
                dst_ref=dst,
                send_sem=send_sem,
                recv_sem=recv_sem,
                device_id=where,
                device_id_type=MESH,
            ).wait_recv()

    def iota(shape, dim):
        return lax.broadcasted_iota(jnp.int32, shape, dim)

    barrier = pltpu.get_barrier_semaphore()
    for tile_step, condition in ((0, None), (-1, not_first), (1, not_final)):
        for j in range(bands):
            ok = (band != j) if condition is None else condition

            @pl.when(ok)
            def _(tile_step=tile_step, j=j):
                pl.semaphore_signal(
                    barrier, inc=1, device_id=device(tile_step, j), device_id_type=MESH
                )

    def fetch(array, held, slot):
        for v in range(groups):
            pltpu.make_async_copy(
                array.at[:, pl.ds(128 * v, 128)], held.at[v], in_s.at[slot]
            ).start()
        return pltpu.make_async_copy(held, held, in_s.at[slot])

    air_copy = pltpu.make_async_copy(air_in, air[0].at[:, pl.ds(1, depth)], in_s.at[3])
    air_copy.start()
    fire_copies = [
        fetch(class_in, turned.at[0], 0),
        fetch(ign_in, turned.at[1], 1),
        fetch(level_in, stage.at[0], 2),
    ]
    tables = [
        pltpu.make_async_copy(src, dst, table_s.at[k])
        for k, (src, dst) in enumerate(
            (
                (rate_in, t_rate),
                (plan_in, plan),
                (burn_in, t_burn),
                (heat_in, t_heat),
                (moist_in, t_moist),
            )
        )
    ]
    for copy in tables:
        copy.start()
    fuel_copy = fetch(fuel_in, stage.at[1], 4)

    spot = iota((16, cols), 1)
    spot = SEG * (spot % 128) + spot // 128
    line16 = iota((16, cols), 0)

    def make_gather(i, carry):
        at = pl.ds(pl.multiple_of(i * 16, 16), 16)
        gather[at, :] = indicator(spot == line16 + 16 * i)
        return carry

    lax.fori_loop(0, cols // 16, make_gather, 0, unroll=4)

    sub = iota((8, 128), 0)
    lane = iota((8, 128), 1)
    octet = lane // 8
    inner = lane % 8 < 4
    edge_w = sub == jnp.where(not_first, -1, 0)
    edge_e = sub == jnp.where(not_final, -1, 7)
    edge_s = lane == jnp.where(band_low, -1, 0)
    edge_n = lane == jnp.where(band_high, -1, 127)
    strip_w = both(edge_w, octet == 3)
    strip_e = both(edge_e, octet == 12)

    def rolled(value, shift, axis):
        shift = shift % value.shape[axis]
        return pltpu.roll(value, shift, axis) if shift else value

    row8 = iota((8, width), 0)
    total_col = sum(math.exp(-k / LEVELS) for k in range(LEVELS))
    total_prof = sum(math.exp(-2.0 * k / LEVELS) for k in range(LEVELS))
    col_base = f32(0.0)
    prof_base = f32(0.0)
    for j in range(bands):
        here = band == j
        col_base = jnp.where(here, f32(math.exp(-j * depth / LEVELS) / total_col), col_base)
        prof_base = jnp.where(
            here, f32(LEVELS * math.exp(-2.0 * j * depth / LEVELS) / total_prof), prof_base
        )
    col_ratio = math.exp(-1.0 / LEVELS)
    prof_ratio = math.exp(-2.0 / LEVELS)

    def send_wind(c, total_u, total_v):
        stacked = jnp.concatenate([total_u, total_v], axis=0)
        for j in range(bands):
            shift = (128 // 4 - coarse * j) % width
            window = (pltpu.roll(stacked, shift, 1) if shift else stacked)[:, :128]
            wsend[c, j] = window
            for k in range(2):
                low = jnp.broadcast_to(window[8 * k : 8 * k + 1], (8, 128))
                high = jnp.broadcast_to(window[8 * k + 7 : 8 * k + 8], (8, 128))
                hsend[c, j, k] = jnp.where(sub < 4, high, low)

            @pl.when(band == j)
            def _(window=window, j=j):
                wrecv[c, j] = window

        send_tile(
            [(wsend.at[c, j], wrecv.at[c, band]) for j in range(bands)],
            wsend.at[c, pl.ds(0, bands - 1)],
            wind_s.at[0],
            wind_r.at[c % 2],
        )
        for way, tile_step, ok in ((0, 1, not_final), (1, -1, not_first)):
            part = pl.ds(4 * way, 4)
            send_group(
                ok,
                [
                    (hsend.at[c, j, :, part, :], hrecv.at[c, band, :, part, :])
                    for j in range(bands)
                ],
                hsend.at[c, :, :, part, :],
                rim_s.at[0, way],
                rim_r.at[c % 2, way],
                [device(tile_step, j) for j in range(bands)],
            )

    def wait_wind(c):
        receive_tile(wrecv.at[c, pl.ds(0, bands - 1)], wind_r.at[c % 2], wind_s.at[0])
        for way, tile_step, ok in ((0, -1, not_first), (1, 1, not_final)):
            part = pl.ds(4 * way, 4)
            receive(
                ok,
                hrecv.at[c, :, :, part, :],
                rim_r.at[c % 2, way],
                rim_s.at[0, way],
                device(tile_step, 0),
            )
        own = wrecv[c, 0]
        beyond = [hrecv[c, 0, 0], hrecv[c, 0, 1]]
        for j in range(1, bands):
            own = own + wrecv[c, j]
            beyond = [beyond[0] + hrecv[c, j, 0], beyond[1] + hrecv[c, j, 1]]
        together = jnp.concatenate([own] + beyond, axis=0)
        wide = jnp.dot(split(together, 1, 2), wmat[...], preferred_element_type=f32)
        for k in range(2):
            own, beyond = wide[8 * k : 8 * k + 8], wide[16 + 8 * k : 24 + 8 * k]
            wnd[k, 0] = own[:, :128]
            wnd[k, 1] = beyond[:, :128]
            for at in (1, 2):
                here = own[:, 128 * at : 128 * at + 128]
                there = beyond[:, 128 * at : 128 * at + 128]
                below = jnp.where(sub == 0, there, pltpu.roll(here, 1, 0))
                above = jnp.where(sub == 7, there, pltpu.roll(here, 7, 0))
                wnd[k, at + 1] = jnp.where(
                    octet < 3, below, jnp.where(octet >= 13, above, here)
                )
            wnd[k, 4] = beyond[:, 384:]

    def send_air(c):
        send(
            not_final,
            air[c].at[:, pl.ds(1, depth), pl.ds(7, 1), :],
            xh.at[c, 0, :, :, pl.ds(7, 1), :],
            halo_s.at[0],
            halo_r.at[c % 2, 0],
            device(1, band),
        )
        send(
            not_first,
            air[c].at[:, pl.ds(1, depth), pl.ds(0, 1), :],
            xh.at[c, 1, :, :, pl.ds(0, 1), :],
            halo_s.at[1],
            halo_r.at[c % 2, 1],
            device(-1, band),
        )
        send(
            band_high,
            air[c].at[:, depth],
            air[c].at[:, 0],
            halo_s.at[2],
            halo_r.at[c % 2, 2],
            device(0, band + 1),
        )
        send(
            band_low,
            air[c].at[:, 1],
            air[c].at[:, depth + 1],
            halo_s.at[3],
            halo_r.at[c % 2, 3],
            device(0, band - 1),
        )

    def wait_air(c):
        receive(
            not_first,
            xh.at[c, 0, :, :, pl.ds(7, 1), :],
            halo_r.at[c % 2, 0],
            halo_s.at[0],
            device(-1, band),
        )
        receive(
            not_final,
            xh.at[c, 1, :, :, pl.ds(0, 1), :],
            halo_r.at[c % 2, 1],
            halo_s.at[1],
            device(1, band),
        )
        receive(band_low, air[c].at[:, 0], halo_r.at[c % 2, 2], halo_s.at[2], device(0, band - 1))
        receive(
            band_high,
            air[c].at[:, depth + 1],
            halo_r.at[c % 2, 3],
            halo_s.at[3],
            device(0, band + 1),
        )

    nothing = jnp.zeros((8, width), f32)
    air_copy.wait()

    def first_air(i, carry):
        weight, total_u, total_v = carry
        total_u = total_u + weight * air[0][2, i + 1]
        total_v = total_v + weight * air[0][3, i + 1]
        return weight * f32(col_ratio), total_u, total_v

    _, total_u, total_v = lax.fori_loop(
        0, depth, first_air, (col_base, nothing, nothing), unroll=4
    )

    expected = (
        bands - 1 + bands * (not_first.astype(jnp.int32) + not_final.astype(jnp.int32))
    )
    pl.semaphore_wait(barrier, expected)

    send_air(0)
    send_wind(0, total_u, total_v)

    def reorder(load):
        return jnp.concatenate(
            [
                jnp.concatenate([load(v, pl.ds(q, 8, stride=REFINE)) for v in range(groups)], axis=1)
                for q in range(REFINE)
            ],
            axis=0,
        )

    for copy in fire_copies:
        copy.wait()
    tables[0].wait()
    kinds = reorder(
        lambda v, at: (turned[0, v, at, :] + 16 * turned[1, v, at, :]).astype(f32)
    ).astype(bf16)
    pieces = split(reorder(lambda v, at: stage[0, v, at, :]), 0, 3)
    found = jnp.dot(
        jnp.concatenate([pieces, kinds], axis=0), gather[...], preferred_element_type=f32
    )
    together = found[:rows] + found[rows : 2 * rows] + found[2 * rows : 3 * rows]
    kinds = found[3 * rows :]
    for q in range(REFINE):
        for p in range(SEG):
            kind = kinds[8 * q : 8 * q + 8, 128 * p : 128 * p + 128]
            when = jnp.floor(kind * (1.0 / 16.0))
            now = together[8 * q : 8 * q + 8, 128 * p : 128 * p + 128]
            ign[q, p] = when
            moist[q, p] = kind - 16.0 * when
            xa[q + 1, p] = jnp.where(when <= 0.0, jnp.minimum(now, -1.0), now)

    def find_rate(q, carry):
        for p in range(SEG):
            kind = moist[q, p]
            value = jnp.full((8, 128), t_rate[0], f32)
            for k in range(1, NFUEL):
                value = jnp.where(kind == float(k), t_rate[k], value)
            rate[q + 1, p] = value
        return carry

    lax.fori_loop(0, REFINE, find_rate, 0, unroll=2)

    def outline(e, ref):
        def edge(q, found):
            x = [ref[q + 1, p] for p in range(SEG)]
            near = pltpu.roll(x[SEG - 1], 1, 1)
            for k in range(1, DEEP):
                near = jnp.where(lane == k, pltpu.roll(x[SEG - 1 - k], k + 1, 1), near)
            for k in range(DEEP):
                near = jnp.where(lane == 127 - k, pltpu.roll(x[k], 127 - k, 1), near)
            return jnp.where(octet == q + 3, pltpu.roll(near, 8 * q + 28, 1), found)

        found = lax.fori_loop(0, REFINE, edge, jnp.zeros((8, 128), f32), unroll=10)
        es[e] = found
        gs[e, SEG] = jnp.where(
            sub < 4,
            jnp.broadcast_to(found[7:8], (8, 128)),
            jnp.broadcast_to(found[0:1], (8, 128)),
        )

        def border(p, carry):
            value = rolled(ref[REFINE, p], 1, 0)
            for k in range(1, DEEP):
                value = jnp.where(sub == k, rolled(ref[REFINE - k, p], k + 1, 0), value)
            for k in range(DEEP):
                value = jnp.where(sub == 4 + k, rolled(ref[DEEP - k, p], 4 + k, 0), value)
            gs[e, p] = value
            return carry

        lax.fori_loop(0, SEG, border, 0, unroll=5)

    def fields(c):
        return pl.ds(0, 2) if c == 0 else pl.ds(1 + c, 1)

    def send_outline(c):
        at = fields(c)
        for way, tile_step, ok in ((0, 1, not_final), (1, -1, not_first)):
            part = pl.ds(4 * way, 4)
            send(
                ok,
                gs.at[at, :, part, :],
                hb.at[at, :, part, :],
                fire_s.at[way],
                fire_r.at[c % 2, way],
                device(tile_step, band),
            )
        for side, band_step, ok in ((0, 1, band_high), (1, -1, band_low)):
            send(
                ok,
                es.at[at],
                er.at[at, side],
                fire_s.at[2 + side],
                fire_r.at[c % 2, 2 + side],
                device(0, band + band_step),
            )
            for way, tile_step, also in ((0, 1, not_final), (1, -1, not_first)):
                send(
                    both(ok, also),
                    es.at[at, pl.ds(7 - 7 * way, 1), :],
                    dg.at[at, side, pl.ds(7 * way, 1), :],
                    fire_s.at[4 + 2 * side + way],
                    fire_r.at[c % 2, 4 + 2 * side + way],
                    device(tile_step, band + band_step),
                )

    def wait_outline(c):
        at = fields(c)
        for way, tile_step, ok in ((0, -1, not_first), (1, 1, not_final)):
            receive(
                ok,
                hb.at[at, :, pl.ds(4 * way, 4), :],
                fire_r.at[c % 2, way],
                fire_s.at[way],
                device(tile_step, band),
            )
        for side, band_step, ok in ((0, -1, band_low), (1, 1, band_high)):
            receive(
                ok,
                er.at[at, side],
                fire_r.at[c % 2, 2 + side],
                fire_s.at[2 + side],
                device(0, band + band_step),
            )
            for way, tile_step, also in ((0, -1, not_first), (1, 1, not_final)):
                receive(
                    both(ok, also),
                    dg.at[at, side, pl.ds(7 * way, 1), :],
                    fire_r.at[c % 2, 4 + 2 * side + way],
                    fire_s.at[4 + 2 * side + way],
                    device(tile_step, band + band_step),
                )

    def surround(e, ref):
        for p in range(SEG):
            ref[12, p] = hb[e, p]
        mine, beyond = es[e], hb[e, SEG]

        def strip(here, there):
            below = jnp.where(sub == 0, there, pltpu.roll(here, 1, 0))
            above = jnp.where(sub == 7, there, pltpu.roll(here, 7, 0))
            return jnp.where(
                octet < 3,
                pltpu.roll(below, 48, 1),
                jnp.where(octet >= 13, pltpu.roll(above, 80, 1), here),
            )

        low = strip(jnp.where(inner, mine, er[e, 0]), jnp.where(inner, beyond, dg[e, 0]))
        high = strip(jnp.where(inner, er[e, 1], mine), jnp.where(inner, dg[e, 1], beyond))
        mixed = jnp.where(inner, high, low)
        corner = mixed
        for k in range(3):
            corner = jnp.where(sub == k, rolled(rolled(mixed, 108 + 8 * k, 1), k, 0), corner)
            corner = jnp.where(sub == 7 - k, rolled(rolled(mixed, 20 - 8 * k, 1), -k, 0), corner)
        ref[13, 0] = low
        ref[13, 1] = high
        ref[13, 2] = corner

    outline(0, rate)
    outline(1, xa)
    send_outline(0)

    @pl.when(jnp.logical_not(not_first))
    def _():
        def zero(i, carry):
            for c in range(STEPS):
                for f in range(4):
                    xh[c, 0, f, i] = jnp.zeros((8, width), f32)
            return carry

        lax.fori_loop(0, depth, zero, 0)
        grecv[:, :, :, 4:] = jnp.zeros((STEPS - 1, bands, 2, 4, 128), f32)

    @pl.when(jnp.logical_not(not_final))
    def _():
        grecv[:, :, :, :4] = jnp.zeros((STEPS - 1, bands, 2, 4, 128), f32)

        def zero(i, carry):
            for c in range(STEPS):
                for f in range(4):
                    xh[c, 1, f, i] = jnp.zeros((8, width), f32)
            return carry

        lax.fori_loop(0, depth, zero, 0)

    @pl.when(jnp.logical_not(band_low))
    def _():
        for c in range(STEPS):
            air[c][:, 0] = jnp.zeros((4, 8, width), f32)

    @pl.when(jnp.logical_not(band_high))
    def _():
        for c in range(STEPS):
            air[c][:, depth + 1] = jnp.zeros((4, 8, width), f32)

    column = iota((16, cols), 1)

    def make_spread(i, carry):
        at = pl.ds(pl.multiple_of(i * 16, 16), 16)
        spread[at, :] = indicator(column == SEG * (line16 + 16 * (i % 8)) + i // 8)
        return carry

    source, place = iota((128, 512), 0), iota((128, 512), 1)
    block, place = place // 128, place % 128
    near = place % 8 < 4
    first = jnp.where(block == 0, 32 + place // 2, jnp.where(near, 32, 31))
    second = jnp.where(
        block == 2, jnp.where(near, 96, 95), jnp.where(place < 64, 31, 96)
    )
    pattern = indicator(source == jnp.where(block < 2, first, second), 0.5)
    wmat[:128, :] = pattern
    wmat[128:, :] = pattern
    source, place = iota((128, 128), 0), iota((128, 128), 1)
    pattern = indicator(place == source // 2 + coarse * (band % 2))
    smat[:128, :] = pattern
    smat[128:, :] = pattern

    for copy in tables[1:]:
        copy.wait()

    def lookup(q, carry):
        for p in range(SEG):
            kind = moist[q, p]
            burn = jnp.full((8, 128), t_burn[0], f32)
            hot = jnp.full((8, 128), t_heat[0], f32)
            wet = jnp.full((8, 128), t_moist[0], f32)
            for k in range(1, NFUEL):
                same = kind == float(k)
                burn = jnp.where(same, t_burn[k], burn)
                hot = jnp.where(same, t_heat[k], hot)
                wet = jnp.where(same, t_moist[k], wet)
            binv[q, p] = 1.0 / burn
            heat[q, p] = hot
            moist[q, p] = wet
            bsum[q, p] = jnp.zeros((8, 128), f32)
        return carry

    lax.fori_loop(0, REFINE, lookup, 0)
    fuel_copy.wait()
    pieces = split(reorder(lambda v, at: stage[1, v, at, :]), 0, 3)
    found = jnp.dot(pieces, gather[...], preferred_element_type=f32)
    together = found[:rows] + found[rows : 2 * rows] + found[2 * rows :]
    for q in range(REFINE):
        for p in range(SEG):
            fuel[q, p] = together[8 * q : 8 * q + 8, 128 * p : 128 * p + 128]
    lax.fori_loop(0, cols // 16, make_spread, 0, unroll=4)

    def uphill(d):
        return jnp.maximum(d, 0.0) * d

    def downhill(d):
        return jnp.minimum(d, 0.0) * d

    def moved(here, dw, de, ds, dn, speed, wu, wv):
        square = (uphill(dw) + downhill(de)) + (uphill(ds) + downhill(dn))
        steep = square * lax.rsqrt(jnp.maximum(square, TINY))
        gx, gy = dw + de, ds + dn
        tail = (wu * gx + wv * gy) * lax.rsqrt(gx * gx + gy * gy + 4.0)
        return here - (speed * (1.0 + jnp.maximum(tail, 0.0))) * steep

    def substep(src, dst, fire_step):
        low, high, corner = src[13, 0], src[13, 1], src[13, 2]
        mixed = jnp.where(inner, high, low)
        top, border, bottom = [], [], []
        for p in range(SEG):
            first, final, beyond = src[1, p], src[REFINE, p], src[12, p]
            border.append(beyond)
            top.append(
                jnp.where(
                    edge_w, first, jnp.where(sub == 0, beyond, pltpu.roll(final, 1, 0))
                )
            )
            src[11, p] = jnp.where(
                edge_e, final, jnp.where(sub == 7, beyond, pltpu.roll(first, 7, 0))
            )

        def across(x, outer):
            south = jnp.where(lane == 0, outer, pltpu.roll(x[SEG - 1], 1, 1))
            north = jnp.where(lane == 127, outer, pltpu.roll(x[0], 127, 1))
            south = jnp.where(edge_s, x[0], south)
            north = jnp.where(edge_n, x[SEG - 1], north)
            line = [south] + x + [north]
            return [line[k + 1] - line[k] for k in range(SEG + 1)]

        wu, wv = wnd[0, 0], wnd[1, 0]

        def line(q, carry):
            x, dw = carry
            after = [src[q + 2, p] for p in range(SEG)]
            dh = across(x, pltpu.roll(mixed, 100 - 8 * q, 1))
            de = []
            for p in range(SEG):
                de.append(after[p] - x[p])
                new = moved(
                    x[p], dw[p], de[p], dh[p], dh[p + 1], fire_step * rate[q + 1, p], wu, wv
                )
                dst[q + 1, p] = new
                bsum[q, p] = bsum[q, p] + jnp.clip(new, -0.5, 0.5)
            return after, de

        x = [src[1, p] for p in range(SEG)]
        lax.fori_loop(0, REFINE, line, (x, [x[p] - top[p] for p in range(SEG)]), unroll=10)

        wu, wv = wnd[0, 1], wnd[1, 1]
        dh = across(border, corner)
        for p in range(SEG):
            here = border[p]
            west = jnp.where(sub == 7, src[REFINE, p], pltpu.roll(here, 7, 0))
            east = jnp.where(sub == 0, src[1, p], pltpu.roll(here, 1, 0))
            dst[12, p] = moved(
                here, here - west, east - here, dh[p], dh[p + 1], fire_step * rate[12, p], wu, wv
            )
        for k, here in enumerate((low, high)):
            west = jnp.where(strip_w, here, pltpu.roll(here, 8, 1))
            east = jnp.where(strip_e, here, pltpu.roll(here, 120, 1))
            south, north = pltpu.roll(here, 127, 1), pltpu.roll(here, 1, 1)
            dst[13, k] = moved(
                here,
                here - west,
                east - here,
                here - south,
                north - here,
                fire_step * rate[13, k],
                wnd[0, 2 + k],
                wnd[1, 2 + k],
            )
        west = jnp.where(sub == 7, pltpu.roll(mixed, 28, 1), pltpu.roll(corner, 7, 0))
        east = jnp.where(sub == 0, pltpu.roll(mixed, 100, 1), pltpu.roll(corner, 1, 0))
        south = jnp.where(lane == 127, border[SEG - 1], pltpu.roll(corner, 127, 1))
        north = jnp.where(lane == 0, border[0], pltpu.roll(corner, 1, 1))
        dst[13, 2] = moved(
            corner,
            corner - west,
            east - corner,
            corner - south,
            north - corner,
            fire_step * rate[13, 2],
            wnd[0, 4],
            wnd[1, 4],
        )

    lane_a = lax.broadcasted_iota(jnp.int32, (8, width), 1)

    def write(c, f, i, value):
        if c == STEPS - 1:
            air_out[f, i] = value
        else:
            air[c + 1][f, i + 1] = value

    def wait_flux(c):
        receive_tile(frecv.at[c, pl.ds(0, bands - 1)], flux_r.at[c % 2], flux_s.at[0])
        whole = jnp.concatenate(
            [frecv[c, 2 * k] + frecv[c, 2 * k + 1] for k in range(width // 128)], axis=1
        )
        return whole[:8], whole[8:]

    def wait_rim(c):
        for way, tile_step, ok in ((0, -1, not_first), (1, 1, not_final)):
            part = pl.ds(4 - 4 * way, 4)
            receive(
                ok,
                grecv.at[c, :, :, part, :],
                rim_r.at[2 + c % 2, way],
                rim_s.at[1, way],
                device(tile_step, 0),
            )
        return [
            jnp.concatenate(
                [grecv[c, 2 * k, f] + grecv[c, 2 * k + 1, f] for k in range(width // 128)],
                axis=1,
            )
            for f in range(2)
        ]

    def force_air(c, flux):
        def force(i, weight):
            for f in range(2):
                now = air_out[f, i] if c == STEPS - 1 else air[c + 1][f, i + 1]
                write(c, f, i, now + weight * flux[f])
            return weight * f32(prof_ratio)

        lax.fori_loop(0, depth, force, prof_base * f32(2.0), unroll=4)

    def move_air(c):
        if c < STEPS - 1:
            drain()
        if c > 0:
            flux = wait_flux(c - 1)
            force_air(c - 1, flux)
        wait_air(c)
        if c > 0:
            low = jnp.where(band_low, prof_base * f32(2.0 / prof_ratio), 0.0)
            high = jnp.where(band_high, prof_base * f32(2.0 * prof_ratio**depth), 0.0)
            for f in range(2):
                air[c][f, 0] = air[c][f, 0] + low * flux[f]
                air[c][f, depth + 1] = air[c][f, depth + 1] + high * flux[f]
        final = c == STEPS - 1

        def update(i, carry):
            weight, total_u, total_v = carry
            u, v = air[c][2, i + 1], air[c][3, i + 1]
            to_w = 0.02 + 0.1 * jnp.maximum(u, 0.0)
            to_e = 0.02 - 0.1 * jnp.minimum(u, 0.0)
            to_s = 0.02 + 0.1 * jnp.maximum(v, 0.0)
            to_n = 0.02 - 0.1 * jnp.minimum(v, 0.0)
            to_here = 0.96 - ((to_w + to_e) + (to_s + to_n))
            to_s = jnp.where(lane_a == 0, 0.0, to_s)
            to_n = jnp.where(lane_a == width - 1, 0.0, to_n)
            lift_x = lift_s = lift_n = None
            for f in range(4):
                here = air[c][f, i + 1]
                west, east = xh[c, 0, f, i], xh[c, 1, f, i]
                west = pltpu.roll(jnp.where(row8 == 7, west, here), 1, 0)
                east = pltpu.roll(jnp.where(row8 == 0, east, here), 7, 0)
                south, north = pltpu.roll(here, 1, 1), pltpu.roll(here, width - 1, 1)
                new = (to_here * here + (to_w * west + to_e * east)) + (
                    (to_s * south + to_n * north) + 0.02 * (air[c][f, i] + air[c][f, i + 2])
                )
                if f == 0:
                    lift_x, lift_s, lift_n = east - west, south, north
                elif f == 1:
                    lift_x = lift_x + 0.6 * (east - west)
                    lift_s = jnp.where(lane_a == 0, 0.0, lift_s + 0.6 * south)
                    lift_n = jnp.where(lane_a == width - 1, 0.0, lift_n + 0.6 * north)
                elif f == 2:
                    new = new + 0.015 * lift_x
                    total_u = total_u + weight * new
                else:
                    new = new + 0.015 * (lift_n - lift_s)
                    total_v = total_v + weight * new
                write(c, f, i, new)
            return weight * f32(col_ratio), total_u, total_v

        carry = (col_base, nothing, nothing)
        _, total_u, total_v = lax.fori_loop(0, depth, update, carry, unroll=10)
        if c > 0:
            rim = wait_rim(c - 1)
            west = [jnp.where(row8 == 0, pltpu.roll(rim[f], 1, 0), 0.0) for f in range(2)]
            east = [jnp.where(row8 == 7, pltpu.roll(rim[f], 7, 0), 0.0) for f in range(2)]
            push = 0.015 * ((east[0] - west[0]) + 0.6 * (east[1] - west[1]))

            def border(i, carry):
                weight, share, total_u = carry
                u = air[c][2, i + 1]
                to_w = share * (0.02 + 0.1 * jnp.maximum(u, 0.0))
                to_e = share * (0.02 - 0.1 * jnp.minimum(u, 0.0))
                for f in range(2):
                    now = air_out[f, i] if final else air[c + 1][f, i + 1]
                    write(c, f, i, now + (to_w * west[f] + to_e * east[f]))
                more = share * push
                now = air_out[2, i] if final else air[c + 1][2, i + 1]
                write(c, 2, i, now + more)
                return weight * f32(col_ratio), share * f32(prof_ratio), total_u + weight * more

            _, _, total_u = lax.fori_loop(
                0, depth, border, (col_base, prof_base * f32(2.0), total_u), unroll=5
            )
        if not final:
            send_wind(c + 1, total_u, total_v)
            send_air(c + 1)

    def send_rim(c, flux):
        for k in range(2):
            low = jnp.broadcast_to(flux[8 * k : 8 * k + 1], (8, 128))
            high = jnp.broadcast_to(flux[8 * k + 7 : 8 * k + 8], (8, 128))
            for j in range(bands):
                gsend[c, j, k] = jnp.where(sub < 4, low, high)
        for way, tile_step, ok in ((0, 1, not_final), (1, -1, not_first)):
            part = pl.ds(4 - 4 * way, 4)
            send_group(
                ok,
                [
                    (gsend.at[c, j, :, part, :], grecv.at[c, band, :, part, :])
                    for j in range(bands)
                ],
                gsend.at[c, :, :, part, :],
                rim_s.at[1, way],
                rim_r.at[2 + c % 2, way],
                [device(tile_step, j) for j in range(bands)],
            )

    def burn_fire(c, fire_step):
        def burn(q, carry):
            hot, wet = carry
            for p in range(SEG):
                now = fuel[q, p]
                spent = (float(SUBSTEPS) * 0.5 - bsum[q, p]) * binv[q, p]
                remain = now * jnp.exp(-fire_step * spent)
                used = now - remain
                fuel[q, p] = remain
                bsum[q, p] = jnp.zeros((8, 128), f32)
                hot = hot + used * heat[q, p]
                wet = wet + used * moist[q, p]
            return hot, wet

        zero = jnp.zeros((8, 128), f32)
        hot, wet = lax.fori_loop(0, REFINE, burn, (zero, zero), unroll=10)
        flux = jnp.dot(
            split(jnp.concatenate([hot, wet], axis=0), 1, 2),
            smat[...],
            preferred_element_type=f32,
        ) * f32(1.0 / (REFINE * REFINE))
        if c < STEPS - 1:
            send_rim(c, flux)
        fsend[c] = flux
        for j in range(bands):

            @pl.when(band == j)
            def _(j=j):
                frecv[c, j] = flux

        send_tile(
            [(fsend.at[c], frecv.at[c, band]) for j in range(bands)],
            frecv.at[c, pl.ds(0, bands - 1)],
            flux_s.at[0],
            flux_r.at[c % 2],
        )

    def burn_window(c):
        fire_step = plan[c].astype(f32) * f32(0.15)
        if c == STEPS - 1:
            drain()
        wait_outline(c)
        if c == 0:
            surround(0, rate)
        surround(1 + c, xa)

        def pair(i, carry):
            substep(xa, xb, fire_step)
            substep(xb, xa, fire_step)
            return carry

        lax.fori_loop(0, SUBSTEPS // 2, pair, 0)
        burn_fire(c, fire_step)
        if c < STEPS - 1:

            def ignite(q, carry):
                for p in range(SEG):
                    now = xa[q + 1, p]
                    xa[q + 1, p] = jnp.where(
                        ign[q, p] <= float(c + 1), jnp.minimum(now, -1.0), now
                    )
                return carry

            lax.fori_loop(0, REFINE, ignite, 0, unroll=10)
            outline(2 + c, xa)
            send_outline(1 + c)
            wait_wind(c + 1)

    def give(load, array):
        values = jnp.concatenate(
            [
                jnp.concatenate([load(q, p) for p in range(SEG)], axis=1)
                for q in range(REFINE)
            ],
            axis=0,
        )
        found = jnp.dot(split(values, 0, 3), spread[...], preferred_element_type=f32)
        found = found[:rows] + found[rows : 2 * rows] + found[2 * rows :]
        for q in range(REFINE):
            for v in range(groups):
                array[v, pl.ds(q, 8, stride=REFINE), :] = found[
                    8 * q : 8 * q + 8, 128 * v : 128 * v + 128
                ]

    move_air(0)
    wait_wind(0)
    burn_window(0)
    for c in range(1, STEPS - 1):
        move_air(c)
        burn_window(c)
    burn_window(STEPS - 1)
    give(lambda q, p: xa[q + 1, p], level_out)
    move_air(STEPS - 1)
    give(lambda q, p: fuel[q, p], fuel_out)
    drain()
    force_air(STEPS - 1, wait_flux(STEPS - 1))


def release(air, level, fuel, air_out, level_out, fuel_out, sems):
    copies = [pltpu.make_async_copy(air, air_out, sems.at[0])]
    copies[0].start()
    for k, (held, out) in enumerate(((level, level_out), (fuel, fuel_out))):
        for v in range(held.shape[0]):
            pltpu.make_async_copy(
                held.at[v], out.at[:, pl.ds(128 * v, 128)], sems.at[1 + k]
            ).start()
        copies.append(pltpu.make_async_copy(held, held, sems.at[1 + k]))
    for copy in copies:
        copy.wait()


def solution(mesh):
    tiles, sects, subs = (mesh.shape[name] for name in ("tile", "sect", "sub"))
    bands = sects * subs
    air_spec = P(None, ("sect", "sub"), ("group", "tile"), None)
    fire_spec = P(("group", "tile"), ("sect", "sub"))

    def local(air_state, fire_level, *rest):
        depth, width = air_state.shape[1], air_state.shape[3]
        rows, cols = fire_level.shape
        groups = cols // 128
        assert air_state.shape[2] == 8 and cols == 64 * REFINE and rows == 8 * REFINE
        vmem = pl.BlockSpec(memory_space=pltpu.VMEM)
        hbm = pl.BlockSpec(memory_space=pltpu.HBM)
        dma = pltpu.SemaphoreType.DMA

        def blocks(*lead):
            return pltpu.VMEM((*lead, 8, 128), f32)

        held = pl.pallas_call(
            functools.partial(kernel, tiles, sects, subs),
            out_shape=(
                pltpu.VMEM(air_state.shape, f32),
                pltpu.VMEM((groups, rows, 128), f32),
                pltpu.VMEM((groups, rows, 128), f32),
            ),
            in_specs=[hbm] * 10,
            out_specs=(vmem, vmem, vmem),
            scratch_shapes=[
                pltpu.VMEM((4, depth + 2, 8, width), f32),
                pltpu.VMEM((4, depth + 2, 8, width), f32),
                pltpu.VMEM((4, depth + 2, 8, width), f32),
                pltpu.VMEM((4, depth + 2, 8, width), f32),
                pltpu.VMEM((STEPS, 2, 4, depth, 8, width), f32),
                blocks(14, SEG),
                blocks(14, SEG),
                blocks(14, SEG),
                blocks(REFINE, SEG),
                blocks(REFINE, SEG),
                blocks(REFINE, SEG),
                blocks(REFINE, SEG),
                blocks(REFINE, SEG),
                blocks(REFINE, SEG),
                pltpu.VMEM((2, groups, rows, 128), f32),
                pltpu.VMEM((2, groups, rows, 128), jnp.int32),
                pltpu.VMEM((cols, cols), bf16),
                pltpu.VMEM((cols, cols), bf16),
                pltpu.VMEM((256, 512), bf16),
                pltpu.VMEM((256, 128), bf16),
                blocks(2, 5),
                blocks(STEPS + 1),
                blocks(STEPS + 1, SEG + 1),
                blocks(STEPS + 1, SEG + 1),
                blocks(STEPS + 1, 2),
                blocks(STEPS + 1, 2),
                pltpu.VMEM((STEPS, bands, 16, 128), f32),
                pltpu.VMEM((STEPS, bands, 16, 128), f32),
                blocks(STEPS, bands, 2),
                blocks(STEPS, bands, 2),
                pltpu.VMEM((STEPS, 16, 128), f32),
                pltpu.VMEM((STEPS, bands, 16, 128), f32),
                blocks(STEPS - 1, bands, 2),
                blocks(STEPS - 1, bands, 2),
                pltpu.SMEM((STEPS,), jnp.int32),
                pltpu.SMEM((NFUEL,), f32),
                pltpu.SMEM((NFUEL,), f32),
                pltpu.SMEM((NFUEL,), f32),
                pltpu.SMEM((NFUEL,), f32),
                dma((5,)),
                dma((5,)),
                dma((8,)),
                dma((2, 8)),
                dma((1,)),
                dma((2,)),
                dma((1,)),
                dma((2,)),
                dma((2, 2)),
                dma((4, 2)),
                dma((4,)),
                dma((2, 4)),
            ],
            compiler_params=pltpu.CompilerParams(
                collective_id=0, has_side_effects=True, vmem_limit_bytes=56 * 1024 * 1024
            ),
        )(air_state, fire_level, *rest)
        held = [pltpu.with_memory_space_constraint(x, pltpu.VMEM) for x in held]
        return pl.pallas_call(
            release,
            out_shape=(
                jax.ShapeDtypeStruct(air_state.shape, f32),
                jax.ShapeDtypeStruct(fire_level.shape, f32),
                jax.ShapeDtypeStruct(fire_level.shape, f32),
            ),
            in_specs=[vmem] * 3,
            out_specs=(hbm, hbm, hbm),
            scratch_shapes=[dma((3,))],
        )(*held)

    return jax.shard_map(
        local,
        mesh=mesh,
        in_specs=(air_spec, fire_spec, fire_spec, fire_spec, fire_spec) + (P(),) * 5,
        out_specs=(air_spec, fire_spec, fire_spec),
        check_vma=False,
    )
```

```python
import functools
import math

import jax
import jax.numpy as jnp
from jax import lax
from jax.experimental import pallas as pl
from jax.experimental.pallas import tpu as pltpu
from jax.sharding import PartitionSpec as P

LEVELS = 80
REFINE = 10
NFUEL = 13
STEPS = 4
SUBSTEPS = 4
DEEP = 4
SEG = REFINE // 2
MESH = pl.DeviceIdType.MESH
TINY = 1.1754944e-38
f32 = jnp.float32
bf16 = jnp.bfloat16


def split(value, axis, pieces):
    parts = []
    for _ in range(pieces):
        parts.append(value.astype(bf16))
        value = value - parts[-1].astype(f32)
    return jnp.concatenate(parts, axis=axis)


def indicator(mask, value=1.0):
    return jnp.where(mask, value, 0.0).astype(bf16)


def kernel(
    tiles,
    sects,
    subs,
    air_in,
    level_in,
    fuel_in,
    class_in,
    ign_in,
    plan_in,
    rate_in,
    burn_in,
    heat_in,
    moist_in,
    air_out,
    level_out,
    fuel_out,
    air_0,
    air_1,
    air_2,
    air_3,
    xh,
    xa,
    xb,
    rate,
    fuel,
    binv,
    heat,
    moist,
    ign,
    bsum,
    stage,
    turned,
    gather,
    spread,
    wmat,
    smat,
    wnd,
    es,
    gs,
    hb,
    er,
    dg,
    wsend,
    wrecv,
    hrecv,
    fsend,
    frecv,
    grecv,
    plan,
    t_rate,
    t_burn,
    t_heat,
    t_moist,
    in_s,
    table_s,
    fire_s,
    fire_r,
    wind_s,
    wind_r,
    flux_s,
    flux_r,
    rim_s,
    rim_r,
    halo_s,
    halo_r,
):
    air = (air_0, air_1, air_2, air_3)
    bands = sects * subs
    depth = air_in.shape[1]
    width = air_in.shape[3]
    rows, cols = level_in.shape
    coarse = cols // REFINE
    groups = cols // 128
    tile_at = lax.axis_index("tile")
    sect_at = lax.axis_index("sect")
    sub_at = lax.axis_index("sub")
    band = sect_at * subs + sub_at
    not_first = tile_at > 0
    not_final = tile_at < tiles - 1
    band_low = band > 0
    band_high = band < bands - 1

    def device(tile_step, at_band):
        return {
            "tile": tile_at + tile_step,
            "sect": at_band // subs,
            "sub": at_band % subs,
        }

    def both(a, b):
        return jnp.logical_and(a, b)

    pending = []

    def send(condition, src, dst, send_sem, recv_sem, where):
        def make():
            return pltpu.make_async_remote_copy(
                src_ref=src,
                dst_ref=dst,
                send_sem=send_sem,
                recv_sem=recv_sem,
                device_id=where,
                device_id_type=MESH,
            )

        @pl.when(condition)
        def _():
            make().start()

        pending.append((condition, make))

    def drain():
        for condition, make in pending:
            if condition is None:
                make().wait_send()
                continue

            @pl.when(condition)
            def _(make=make):
                make().wait_send()

        pending.clear()

    def send_group(condition, parts, whole, send_sem, recv_sem, wheres):
        def make(src, dst, where):
            return pltpu.make_async_remote_copy(
                src_ref=src,
                dst_ref=dst,
                send_sem=send_sem,
                recv_sem=recv_sem,
                device_id=where,
                device_id_type=MESH,
            )

        @pl.when(condition)
        def _():
            for (src, dst), where in zip(parts, wheres):
                make(src, dst, where).start()

        pending.append((condition, lambda: make(whole, whole, wheres[0])))

    def send_tile(parts, whole, send_sem, recv_sem):
        def make(src, dst, j):
            return pltpu.make_async_remote_copy(
                src_ref=src,
                dst_ref=dst,
                send_sem=send_sem,
                recv_sem=recv_sem,
                device_id=device(0, j),
                device_id_type=MESH,
            )

        for j, (src, dst) in enumerate(parts):

            @pl.when(band != j)
            def _(src=src, dst=dst, j=j):
                make(src, dst, j).start()

        pending.append((None, lambda: make(whole, whole, 0)))

    def receive_tile(whole, recv_sem, send_sem):
        pltpu.make_async_remote_copy(
            src_ref=whole,
            dst_ref=whole,
            send_sem=send_sem,
            recv_sem=recv_sem,
            device_id=device(0, 0),
            device_id_type=MESH,
        ).wait_recv()

    def receive(condition, dst, recv_sem, send_sem, where):
        @pl.when(condition)
        def _():
            pltpu.make_async_remote_copy(
                src_ref=dst,
                dst_ref=dst,
                send_sem=send_sem,
                recv_sem=recv_sem,
                device_id=where,
                device_id_type=MESH,
            ).wait_recv()

    def iota(shape, dim):
        return lax.broadcasted_iota(jnp.int32, shape, dim)

    barrier = pltpu.get_barrier_semaphore()
    for tile_step, condition in ((0, None), (-1, not_first), (1, not_final)):
        for j in range(bands):
            ok = (band != j) if condition is None else condition

            @pl.when(ok)
            def _(tile_step=tile_step, j=j):
                pl.semaphore_signal(
                    barrier, inc=1, device_id=device(tile_step, j), device_id_type=MESH
                )

    def fetch(array, held, slot):
        for v in range(groups):
            pltpu.make_async_copy(
                array.at[:, pl.ds(128 * v, 128)], held.at[v], in_s.at[slot]
            ).start()
        return pltpu.make_async_copy(held, held, in_s.at[slot])

    air_copy = pltpu.make_async_copy(air_in, air[0].at[:, pl.ds(1, depth)], in_s.at[3])
    air_copy.start()
    fire_copies = [
        fetch(class_in, turned.at[0], 0),
        fetch(ign_in, turned.at[1], 1),
        fetch(level_in, stage.at[0], 2),
    ]
    tables = [
        pltpu.make_async_copy(src, dst, table_s.at[k])
        for k, (src, dst) in enumerate(
            (
                (rate_in, t_rate),
                (plan_in, plan),
                (burn_in, t_burn),
                (heat_in, t_heat),
                (moist_in, t_moist),
            )
        )
    ]
    for copy in tables:
        copy.start()
    fuel_copy = fetch(fuel_in, stage.at[1], 4)

    spot = iota((16, cols), 1)
    spot = SEG * (spot % 128) + spot // 128
    line16 = iota((16, cols), 0)

    def make_gather(i, carry):
        at = pl.ds(pl.multiple_of(i * 16, 16), 16)
        gather[at, :] = indicator(spot == line16 + 16 * i)
        return carry

    lax.fori_loop(0, cols // 16, make_gather, 0, unroll=4)

    sub = iota((8, 128), 0)
    lane = iota((8, 128), 1)
    octet = lane // 8
    inner = lane % 8 < 4
    edge_w = sub == jnp.where(not_first, -1, 0)
    edge_e = sub == jnp.where(not_final, -1, 7)
    edge_s = lane == jnp.where(band_low, -1, 0)
    edge_n = lane == jnp.where(band_high, -1, 127)
    strip_w = both(edge_w, octet == 3)
    strip_e = both(edge_e, octet == 12)

    def rolled(value, shift, axis):
        shift = shift % value.shape[axis]
        return pltpu.roll(value, shift, axis) if shift else value

    row8 = iota((8, width), 0)
    total_col = sum(math.exp(-k / LEVELS) for k in range(LEVELS))
    total_prof = sum(math.exp(-2.0 * k / LEVELS) for k in range(LEVELS))
    col_base = f32(0.0)
    prof_base = f32(0.0)
    for j in range(bands):
        here = band == j
        col_base = jnp.where(here, f32(math.exp(-j * depth / LEVELS) / total_col), col_base)
        prof_base = jnp.where(
            here, f32(LEVELS * math.exp(-2.0 * j * depth / LEVELS) / total_prof), prof_base
        )
    col_ratio = math.exp(-1.0 / LEVELS)
    prof_ratio = math.exp(-2.0 / LEVELS)

    def send_wind(c, total_u, total_v):
        stacked = jnp.concatenate([total_u, total_v], axis=0)
        for j in range(bands):
            shift = (128 // 4 - coarse * j) % width
            window = (pltpu.roll(stacked, shift, 1) if shift else stacked)[:, :128]
            wsend[c, j, 0] = window[:8]
            wsend[c, j, 1] = window[8:]

            @pl.when(band == j)
            def _(window=window, j=j):
                wrecv[c, j, 0] = window[:8]
                wrecv[c, j, 1] = window[8:]

        send_tile(
            [(wsend.at[c, j], wrecv.at[c, band]) for j in range(bands)],
            wsend.at[c, pl.ds(0, bands - 1)],
            wind_s.at[0],
            wind_r.at[c % 2],
        )
        for way, tile_step, ok in ((0, 1, not_final), (1, -1, not_first)):
            row, there = pl.ds(7 - 7 * way, 1), pl.ds(7 * way, 1)
            send_group(
                ok,
                [
                    (wsend.at[c, j, :, row, :], hrecv.at[c, band, :, there, :])
                    for j in range(bands)
                ],
                hrecv.at[c, :, :, there, :],
                rim_s.at[0, way],
                rim_r.at[c % 2, way],
                [device(tile_step, j) for j in range(bands)],
            )

    def wait_wind(c):
        receive_tile(wrecv.at[c, pl.ds(0, bands - 1)], wind_r.at[c % 2], wind_s.at[0])
        for way, tile_step, ok in ((0, -1, not_first), (1, 1, not_final)):
            receive(
                ok,
                hrecv.at[c, :, :, pl.ds(7 * way, 1), :],
                rim_r.at[c % 2, way],
                rim_s.at[0, way],
                device(tile_step, 0),
            )
        own, beyond = [], []
        for k in range(2):
            here, there = wrecv[c, 0, k], hrecv[c, 0, k]
            for j in range(1, bands):
                here, there = here + wrecv[c, j, k], there + hrecv[c, j, k]
            own.append(here)
            beyond.append(
                jnp.where(
                    sub < 4,
                    jnp.broadcast_to(there[:1], (8, 128)),
                    jnp.broadcast_to(there[7:], (8, 128)),
                )
            )
        together = jnp.concatenate(own + beyond, axis=0)
        wide = jnp.dot(split(together, 1, 2), wmat[...], preferred_element_type=f32)
        for k in range(2):
            own, beyond = wide[8 * k : 8 * k + 8], wide[16 + 8 * k : 24 + 8 * k]
            wnd[k, 0] = own[:, :128]
            wnd[k, 1] = beyond[:, :128]
            for at in (1, 2):
                here = own[:, 128 * at : 128 * at + 128]
                there = beyond[:, 128 * at : 128 * at + 128]
                below = jnp.where(sub == 0, there, pltpu.roll(here, 1, 0))
                above = jnp.where(sub == 7, there, pltpu.roll(here, 7, 0))
                wnd[k, at + 1] = jnp.where(
                    octet < 3, below, jnp.where(octet >= 13, above, here)
                )
            wnd[k, 4] = beyond[:, 384:]

    def portions(c):
        half = depth // 2
        return [(0, half), (half, depth - half)] if c == 0 else [(0, depth)]

    def send_air(c):
        send(
            band_high,
            air[c].at[:, depth],
            air[c].at[:, 0],
            halo_s.at[4],
            halo_r.at[c % 2, 4],
            device(0, band + 1),
        )
        send(
            band_low,
            air[c].at[:, 1],
            air[c].at[:, depth + 1],
            halo_s.at[5],
            halo_r.at[c % 2, 5],
            device(0, band - 1),
        )
        for piece, (start, count) in enumerate(portions(c)):
            send(
                not_final,
                air[c].at[:, pl.ds(1 + start, count), pl.ds(7, 1), :],
                xh.at[c, 0, :, pl.ds(start, count), pl.ds(7, 1), :],
                halo_s.at[2 * piece],
                halo_r.at[c % 2, 2 * piece],
                device(1, band),
            )
            send(
                not_first,
                air[c].at[:, pl.ds(1 + start, count), pl.ds(0, 1), :],
                xh.at[c, 1, :, pl.ds(start, count), pl.ds(0, 1), :],
                halo_s.at[2 * piece + 1],
                halo_r.at[c % 2, 2 * piece + 1],
                device(-1, band),
            )

    def wait_air(c, piece):
        start, count = portions(c)[piece]
        receive(
            not_first,
            xh.at[c, 0, :, pl.ds(start, count), pl.ds(7, 1), :],
            halo_r.at[c % 2, 2 * piece],
            halo_s.at[2 * piece],
            device(-1, band),
        )
        receive(
            not_final,
            xh.at[c, 1, :, pl.ds(start, count), pl.ds(0, 1), :],
            halo_r.at[c % 2, 2 * piece + 1],
            halo_s.at[2 * piece + 1],
            device(1, band),
        )
        if piece == 0:
            receive(
                band_low, air[c].at[:, 0], halo_r.at[c % 2, 4], halo_s.at[4], device(0, band - 1)
            )
            receive(
                band_high,
                air[c].at[:, depth + 1],
                halo_r.at[c % 2, 5],
                halo_s.at[5],
                device(0, band + 1),
            )

    nothing = jnp.zeros((8, width), f32)
    air_copy.wait()

    def first_air(i, carry):
        weight, total_u, total_v = carry
        total_u = total_u + weight * air[0][2, i + 1]
        total_v = total_v + weight * air[0][3, i + 1]
        return weight * f32(col_ratio), total_u, total_v

    _, total_u, total_v = lax.fori_loop(
        0, depth, first_air, (col_base, nothing, nothing), unroll=4
    )

    expected = (
        bands - 1 + bands * (not_first.astype(jnp.int32) + not_final.astype(jnp.int32))
    )
    pl.semaphore_wait(barrier, expected)

    send_air(0)
    send_wind(0, total_u, total_v)

    def reorder(load):
        return jnp.concatenate(
            [
                jnp.concatenate([load(v, pl.ds(q, 8, stride=REFINE)) for v in range(groups)], axis=1)
                for q in range(REFINE)
            ],
            axis=0,
        )

    for copy in fire_copies:
        copy.wait()
    tables[0].wait()
    kinds = reorder(
        lambda v, at: (turned[0, v, at, :] + 16 * turned[1, v, at, :]).astype(f32)
    ).astype(bf16)
    pieces = split(reorder(lambda v, at: stage[0, v, at, :]), 0, 3)
    found = jnp.dot(
        jnp.concatenate([pieces, kinds], axis=0), gather[...], preferred_element_type=f32
    )
    together = found[:rows] + found[rows : 2 * rows] + found[2 * rows : 3 * rows]
    kinds = found[3 * rows :]
    for q in range(REFINE):
        for p in range(SEG):
            kind = kinds[8 * q : 8 * q + 8, 128 * p : 128 * p + 128]
            when = jnp.floor(kind * (1.0 / 16.0))
            now = together[8 * q : 8 * q + 8, 128 * p : 128 * p + 128]
            ign[q, p] = when
            moist[q, p] = kind - 16.0 * when
            xa[q + 1, p] = jnp.where(when <= 0.0, jnp.minimum(now, -1.0), now)

    def find_rate(q, carry):
        for p in range(SEG):
            kind = moist[q, p]
            value = jnp.full((8, 128), t_rate[0], f32)
            for k in range(1, NFUEL):
                value = jnp.where(kind == float(k), t_rate[k], value)
            rate[q + 1, p] = value
        return carry

    lax.fori_loop(0, REFINE, find_rate, 0, unroll=2)

    def outline(e, ref):
        def edge(q, found):
            x = [ref[q + 1, p] for p in range(SEG)]
            near = pltpu.roll(x[SEG - 1], 1, 1)
            for k in range(1, DEEP):
                near = jnp.where(lane == k, pltpu.roll(x[SEG - 1 - k], k + 1, 1), near)
            for k in range(DEEP):
                near = jnp.where(lane == 127 - k, pltpu.roll(x[k], 127 - k, 1), near)
            return jnp.where(octet == q + 3, pltpu.roll(near, 8 * q + 28, 1), found)

        found = lax.fori_loop(0, REFINE, edge, jnp.zeros((8, 128), f32), unroll=10)
        es[e] = found
        gs[e, SEG] = jnp.where(
            sub < 4,
            jnp.broadcast_to(found[7:8], (8, 128)),
            jnp.broadcast_to(found[0:1], (8, 128)),
        )

        def border(p, carry):
            value = rolled(ref[REFINE, p], 1, 0)
            for k in range(1, DEEP):
                value = jnp.where(sub == k, rolled(ref[REFINE - k, p], k + 1, 0), value)
            for k in range(DEEP):
                value = jnp.where(sub == 4 + k, rolled(ref[DEEP - k, p], 4 + k, 0), value)
            gs[e, p] = value
            return carry

        lax.fori_loop(0, SEG, border, 0, unroll=5)

    def fields(c):
        return pl.ds(0, 2) if c == 0 else pl.ds(1 + c, 1)

    def send_outline(c):
        at = fields(c)
        for way, tile_step, ok in ((0, 1, not_final), (1, -1, not_first)):
            part = pl.ds(4 * way, 4)
            send(
                ok,
                gs.at[at, :, part, :],
                hb.at[at, :, part, :],
                fire_s.at[way],
                fire_r.at[c % 2, way],
                device(tile_step, band),
            )
        for side, band_step, ok in ((0, 1, band_high), (1, -1, band_low)):
            send(
                ok,
                es.at[at],
                er.at[at, side],
                fire_s.at[2 + side],
                fire_r.at[c % 2, 2 + side],
                device(0, band + band_step),
            )
            for way, tile_step, also in ((0, 1, not_final), (1, -1, not_first)):
                send(
                    both(ok, also),
                    es.at[at, pl.ds(7 - 7 * way, 1), :],
                    dg.at[at, side, pl.ds(7 * way, 1), :],
                    fire_s.at[4 + 2 * side + way],
                    fire_r.at[c % 2, 4 + 2 * side + way],
                    device(tile_step, band + band_step),
                )

    def wait_outline(c):
        at = fields(c)
        for way, tile_step, ok in ((0, -1, not_first), (1, 1, not_final)):
            receive(
                ok,
                hb.at[at, :, pl.ds(4 * way, 4), :],
                fire_r.at[c % 2, way],
                fire_s.at[way],
                device(tile_step, band),
            )
        for side, band_step, ok in ((0, -1, band_low), (1, 1, band_high)):
            receive(
                ok,
                er.at[at, side],
                fire_r.at[c % 2, 2 + side],
                fire_s.at[2 + side],
                device(0, band + band_step),
            )
            for way, tile_step, also in ((0, -1, not_first), (1, 1, not_final)):
                receive(
                    both(ok, also),
                    dg.at[at, side, pl.ds(7 * way, 1), :],
                    fire_r.at[c % 2, 4 + 2 * side + way],
                    fire_s.at[4 + 2 * side + way],
                    device(tile_step, band + band_step),
                )

    def surround(e, ref):
        for p in range(SEG):
            ref[12, p] = hb[e, p]
        mine, beyond = es[e], hb[e, SEG]

        def strip(here, there):
            below = jnp.where(sub == 0, there, pltpu.roll(here, 1, 0))
            above = jnp.where(sub == 7, there, pltpu.roll(here, 7, 0))
            return jnp.where(
                octet < 3,
                pltpu.roll(below, 48, 1),
                jnp.where(octet >= 13, pltpu.roll(above, 80, 1), here),
            )

        low = strip(jnp.where(inner, mine, er[e, 0]), jnp.where(inner, beyond, dg[e, 0]))
        high = strip(jnp.where(inner, er[e, 1], mine), jnp.where(inner, dg[e, 1], beyond))
        mixed = jnp.where(inner, high, low)
        corner = mixed
        for k in range(3):
            corner = jnp.where(sub == k, rolled(rolled(mixed, 108 + 8 * k, 1), k, 0), corner)
            corner = jnp.where(sub == 7 - k, rolled(rolled(mixed, 20 - 8 * k, 1), -k, 0), corner)
        ref[13, 0] = low
        ref[13, 1] = high
        ref[13, 2] = corner

    outline(0, rate)
    outline(1, xa)
    send_outline(0)

    @pl.when(jnp.logical_not(not_first))
    def _():
        def zero(i, carry):
            for c in range(STEPS):
                for f in range(4):
                    xh[c, 0, f, i] = jnp.zeros((8, width), f32)
            return carry

        lax.fori_loop(0, depth, zero, 0)
        grecv[:, :, :, 7:] = jnp.zeros((STEPS - 1, bands, 2, 1, 128), f32)

    @pl.when(jnp.logical_not(not_final))
    def _():
        grecv[:, :, :, :1] = jnp.zeros((STEPS - 1, bands, 2, 1, 128), f32)

        def zero(i, carry):
            for c in range(STEPS):
                for f in range(4):
                    xh[c, 1, f, i] = jnp.zeros((8, width), f32)
            return carry

        lax.fori_loop(0, depth, zero, 0)

    @pl.when(jnp.logical_not(band_low))
    def _():
        for c in range(STEPS):
            air[c][:, 0] = jnp.zeros((4, 8, width), f32)

    @pl.when(jnp.logical_not(band_high))
    def _():
        for c in range(STEPS):
            air[c][:, depth + 1] = jnp.zeros((4, 8, width), f32)

    column = iota((16, cols), 1)

    def make_spread(i, carry):
        at = pl.ds(pl.multiple_of(i * 16, 16), 16)
        spread[at, :] = indicator(column == SEG * (line16 + 16 * (i % 8)) + i // 8)
        return carry

    source, place = iota((128, 512), 0), iota((128, 512), 1)
    block, place = place // 128, place % 128
    near = place % 8 < 4
    first = jnp.where(block == 0, 32 + place // 2, jnp.where(near, 32, 31))
    second = jnp.where(
        block == 2, jnp.where(near, 96, 95), jnp.where(place < 64, 31, 96)
    )
    pattern = indicator(source == jnp.where(block < 2, first, second), 0.5)
    wmat[:128, :] = pattern
    wmat[128:, :] = pattern
    source, place = iota((128, 128), 0), iota((128, 128), 1)
    pattern = indicator(place == source // 2 + coarse * (band % 2))
    smat[:128, :] = pattern
    smat[128:, :] = pattern

    for copy in tables[1:]:
        copy.wait()

    def lookup(q, carry):
        for p in range(SEG):
            kind = moist[q, p]
            burn = jnp.full((8, 128), t_burn[0], f32)
            hot = jnp.full((8, 128), t_heat[0], f32)
            wet = jnp.full((8, 128), t_moist[0], f32)
            for k in range(1, NFUEL):
                same = kind == float(k)
                burn = jnp.where(same, t_burn[k], burn)
                hot = jnp.where(same, t_heat[k], hot)
                wet = jnp.where(same, t_moist[k], wet)
            binv[q, p] = 1.0 / burn
            heat[q, p] = hot
            moist[q, p] = wet
            bsum[q, p] = jnp.zeros((8, 128), f32)
        return carry

    lax.fori_loop(0, REFINE, lookup, 0)
    fuel_copy.wait()
    pieces = split(reorder(lambda v, at: stage[1, v, at, :]), 0, 3)
    found = jnp.dot(pieces, gather[...], preferred_element_type=f32)
    together = found[:rows] + found[rows : 2 * rows] + found[2 * rows :]
    for q in range(REFINE):
        for p in range(SEG):
            fuel[q, p] = together[8 * q : 8 * q + 8, 128 * p : 128 * p + 128]
    lax.fori_loop(0, cols // 16, make_spread, 0, unroll=4)

    def uphill(d):
        return jnp.maximum(d, 0.0) * d

    def downhill(d):
        return jnp.minimum(d, 0.0) * d

    def moved(here, dw, de, ds, dn, speed, wu, wv):
        square = (uphill(dw) + downhill(de)) + (uphill(ds) + downhill(dn))
        steep = square * lax.rsqrt(jnp.maximum(square, TINY))
        gx, gy = dw + de, ds + dn
        tail = (wu * gx + wv * gy) * lax.rsqrt(gx * gx + gy * gy + 4.0)
        return here - (speed * (1.0 + jnp.maximum(tail, 0.0))) * steep

    def substep(src, dst, fire_step):
        low, high, corner = src[13, 0], src[13, 1], src[13, 2]
        mixed = jnp.where(inner, high, low)
        top, border, bottom = [], [], []
        for p in range(SEG):
            first, final, beyond = src[1, p], src[REFINE, p], src[12, p]
            border.append(beyond)
            top.append(
                jnp.where(
                    edge_w, first, jnp.where(sub == 0, beyond, pltpu.roll(final, 1, 0))
                )
            )
            src[11, p] = jnp.where(
                edge_e, final, jnp.where(sub == 7, beyond, pltpu.roll(first, 7, 0))
            )

        def across(x, outer):
            south = jnp.where(lane == 0, outer, pltpu.roll(x[SEG - 1], 1, 1))
            north = jnp.where(lane == 127, outer, pltpu.roll(x[0], 127, 1))
            south = jnp.where(edge_s, x[0], south)
            north = jnp.where(edge_n, x[SEG - 1], north)
            line = [south] + x + [north]
            return [line[k + 1] - line[k] for k in range(SEG + 1)]

        wu, wv = wnd[0, 0], wnd[1, 0]

        def line(q, carry):
            x, dw = carry
            after = [src[q + 2, p] for p in range(SEG)]
            dh = across(x, pltpu.roll(mixed, 100 - 8 * q, 1))
            de = []
            for p in range(SEG):
                de.append(after[p] - x[p])
                new = moved(
                    x[p], dw[p], de[p], dh[p], dh[p + 1], fire_step * rate[q + 1, p], wu, wv
                )
                dst[q + 1, p] = new
                bsum[q, p] = bsum[q, p] + jnp.clip(new, -0.5, 0.5)
            return after, de

        x = [src[1, p] for p in range(SEG)]
        lax.fori_loop(0, REFINE, line, (x, [x[p] - top[p] for p in range(SEG)]), unroll=10)

        wu, wv = wnd[0, 1], wnd[1, 1]
        dh = across(border, corner)
        for p in range(SEG):
            here = border[p]
            west = jnp.where(sub == 7, src[REFINE, p], pltpu.roll(here, 7, 0))
            east = jnp.where(sub == 0, src[1, p], pltpu.roll(here, 1, 0))
            dst[12, p] = moved(
                here, here - west, east - here, dh[p], dh[p + 1], fire_step * rate[12, p], wu, wv
            )
        for k, here in enumerate((low, high)):
            west = jnp.where(strip_w, here, pltpu.roll(here, 8, 1))
            east = jnp.where(strip_e, here, pltpu.roll(here, 120, 1))
            south, north = pltpu.roll(here, 127, 1), pltpu.roll(here, 1, 1)
            dst[13, k] = moved(
                here,
                here - west,
                east - here,
                here - south,
                north - here,
                fire_step * rate[13, k],
                wnd[0, 2 + k],
                wnd[1, 2 + k],
            )
        west = jnp.where(sub == 7, pltpu.roll(mixed, 28, 1), pltpu.roll(corner, 7, 0))
        east = jnp.where(sub == 0, pltpu.roll(mixed, 100, 1), pltpu.roll(corner, 1, 0))
        south = jnp.where(lane == 127, border[SEG - 1], pltpu.roll(corner, 127, 1))
        north = jnp.where(lane == 0, border[0], pltpu.roll(corner, 1, 1))
        dst[13, 2] = moved(
            corner,
            corner - west,
            east - corner,
            corner - south,
            north - corner,
            fire_step * rate[13, 2],
            wnd[0, 4],
            wnd[1, 4],
        )

    lane_a = lax.broadcasted_iota(jnp.int32, (8, width), 1)

    def write(c, f, i, value):
        if c == STEPS - 1:
            air_out[f, i] = value
        else:
            air[c + 1][f, i + 1] = value

    def wait_flux(c):
        receive_tile(frecv.at[c, pl.ds(0, bands - 1)], flux_r.at[c % 2], flux_s.at[0])
        return [
            jnp.concatenate(
                [frecv[c, 2 * k, f] + frecv[c, 2 * k + 1, f] for k in range(width // 128)],
                axis=1,
            )
            for f in range(2)
        ]

    def wait_rim(c):
        for way, tile_step, ok in ((0, -1, not_first), (1, 1, not_final)):
            row = pl.ds(7 - 7 * way, 1)
            receive(
                ok,
                grecv.at[c, :, :, row, :],
                rim_r.at[2 + c % 2, way],
                rim_s.at[1, way],
                device(tile_step, 0),
            )
        return [
            jnp.concatenate(
                [grecv[c, 2 * k, f] + grecv[c, 2 * k + 1, f] for k in range(width // 128)],
                axis=1,
            )
            for f in range(2)
        ]

    def force_air(c, flux):
        def force(i, weight):
            for f in range(2):
                now = air_out[f, i] if c == STEPS - 1 else air[c + 1][f, i + 1]
                write(c, f, i, now + weight * flux[f])
            return weight * f32(prof_ratio)

        lax.fori_loop(0, depth, force, prof_base * f32(2.0), unroll=4)

    def move_air(c):
        if c < STEPS - 1:
            drain()
        if c > 0:
            flux = wait_flux(c - 1)
            force_air(c - 1, flux)
        wait_air(c, 0)
        if c > 0:
            low = jnp.where(band_low, prof_base * f32(2.0 / prof_ratio), 0.0)
            high = jnp.where(band_high, prof_base * f32(2.0 * prof_ratio**depth), 0.0)
            for f in range(2):
                air[c][f, 0] = air[c][f, 0] + low * flux[f]
                air[c][f, depth + 1] = air[c][f, depth + 1] + high * flux[f]
        final = c == STEPS - 1

        def update(i, carry):
            weight, total_u, total_v = carry
            u, v = air[c][2, i + 1], air[c][3, i + 1]
            to_w = 0.02 + 0.1 * jnp.maximum(u, 0.0)
            to_e = 0.02 - 0.1 * jnp.minimum(u, 0.0)
            to_s = 0.02 + 0.1 * jnp.maximum(v, 0.0)
            to_n = 0.02 - 0.1 * jnp.minimum(v, 0.0)
            to_here = 0.96 - ((to_w + to_e) + (to_s + to_n))
            to_s = jnp.where(lane_a == 0, 0.0, to_s)
            to_n = jnp.where(lane_a == width - 1, 0.0, to_n)
            lift_x = lift_s = lift_n = None
            for f in range(4):
                here = air[c][f, i + 1]
                west, east = xh[c, 0, f, i], xh[c, 1, f, i]
                west = pltpu.roll(jnp.where(row8 == 7, west, here), 1, 0)
                east = pltpu.roll(jnp.where(row8 == 0, east, here), 7, 0)
                south, north = pltpu.roll(here, 1, 1), pltpu.roll(here, width - 1, 1)
                new = (to_here * here + (to_w * west + to_e * east)) + (
                    (to_s * south + to_n * north) + 0.02 * (air[c][f, i] + air[c][f, i + 2])
                )
                if f == 0:
                    lift_x, lift_s, lift_n = east - west, south, north
                elif f == 1:
                    lift_x = lift_x + 0.6 * (east - west)
                    lift_s = jnp.where(lane_a == 0, 0.0, lift_s + 0.6 * south)
                    lift_n = jnp.where(lane_a == width - 1, 0.0, lift_n + 0.6 * north)
                elif f == 2:
                    new = new + 0.015 * lift_x
                    total_u = total_u + weight * new
                else:
                    new = new + 0.015 * (lift_n - lift_s)
                    total_v = total_v + weight * new
                write(c, f, i, new)
            return weight * f32(col_ratio), total_u, total_v

        carry = (col_base, nothing, nothing)
        for piece, (start, count) in enumerate(portions(c)):
            if piece > 0:
                wait_air(c, piece)
            carry = lax.fori_loop(start, start + count, update, carry, unroll=10)
        _, total_u, total_v = carry
        if c > 0:
            rim = wait_rim(c - 1)
            west = [jnp.where(row8 == 0, pltpu.roll(rim[f], 1, 0), 0.0) for f in range(2)]
            east = [jnp.where(row8 == 7, pltpu.roll(rim[f], 7, 0), 0.0) for f in range(2)]
            push = 0.015 * ((east[0] - west[0]) + 0.6 * (east[1] - west[1]))

            def border(i, carry):
                weight, share, total_u = carry
                u = air[c][2, i + 1]
                to_w = share * (0.02 + 0.1 * jnp.maximum(u, 0.0))
                to_e = share * (0.02 - 0.1 * jnp.minimum(u, 0.0))
                for f in range(2):
                    now = air_out[f, i] if final else air[c + 1][f, i + 1]
                    write(c, f, i, now + (to_w * west[f] + to_e * east[f]))
                more = share * push
                now = air_out[2, i] if final else air[c + 1][2, i + 1]
                write(c, 2, i, now + more)
                return weight * f32(col_ratio), share * f32(prof_ratio), total_u + weight * more

            _, _, total_u = lax.fori_loop(
                0, depth, border, (col_base, prof_base * f32(2.0), total_u), unroll=5
            )
        if not final:
            send_wind(c + 1, total_u, total_v)
            send_air(c + 1)

    def send_rim(c):
        for way, tile_step, ok in ((0, 1, not_final), (1, -1, not_first)):
            row = pl.ds(7 - 7 * way, 1)
            send_group(
                ok,
                [(fsend.at[c, :, row, :], grecv.at[c, band, :, row, :]) for j in range(bands)],
                grecv.at[c, :, :, row, :],
                rim_s.at[1, way],
                rim_r.at[2 + c % 2, way],
                [device(tile_step, j) for j in range(bands)],
            )

    def burn_fire(c, fire_step):
        def burn(q, carry):
            hot, wet = carry
            for p in range(SEG):
                now = fuel[q, p]
                spent = (float(SUBSTEPS) * 0.5 - bsum[q, p]) * binv[q, p]
                remain = now * jnp.exp(-fire_step * spent)
                used = now - remain
                fuel[q, p] = remain
                bsum[q, p] = jnp.zeros((8, 128), f32)
                hot = hot + used * heat[q, p]
                wet = wet + used * moist[q, p]
            return hot, wet

        zero = jnp.zeros((8, 128), f32)
        hot, wet = lax.fori_loop(0, REFINE, burn, (zero, zero), unroll=10)
        flux = jnp.dot(
            split(jnp.concatenate([hot, wet], axis=0), 1, 2),
            smat[...],
            preferred_element_type=f32,
        ) * f32(1.0 / (REFINE * REFINE))
        fsend[c, 0] = flux[:8]
        fsend[c, 1] = flux[8:]
        for j in range(bands):

            @pl.when(band == j)
            def _(j=j):
                frecv[c, j, 0] = flux[:8]
                frecv[c, j, 1] = flux[8:]

        send_tile(
            [(fsend.at[c], frecv.at[c, band]) for j in range(bands)],
            frecv.at[c, pl.ds(0, bands - 1)],
            flux_s.at[0],
            flux_r.at[c % 2],
        )
        if c < STEPS - 1:
            send_rim(c)

    def burn_window(c):
        fire_step = plan[c].astype(f32) * f32(0.15)
        if c == STEPS - 1:
            drain()
        wait_outline(c)
        if c == 0:
            surround(0, rate)
        surround(1 + c, xa)

        def pair(i, carry):
            substep(xa, xb, fire_step)
            substep(xb, xa, fire_step)
            return carry

        lax.fori_loop(0, SUBSTEPS // 2, pair, 0)
        if c != STEPS - 2:
            burn_fire(c, fire_step)
        if c < STEPS - 1:

            def ignite(q, carry):
                for p in range(SEG):
                    now = xa[q + 1, p]
                    xa[q + 1, p] = jnp.where(
                        ign[q, p] <= float(c + 1), jnp.minimum(now, -1.0), now
                    )
                return carry

            lax.fori_loop(0, REFINE, ignite, 0, unroll=10)
            outline(2 + c, xa)
            send_outline(1 + c)
            if c == STEPS - 2:
                burn_fire(c, fire_step)
            wait_wind(c + 1)

    def give(load, array):
        values = jnp.concatenate(
            [
                jnp.concatenate([load(q, p) for p in range(SEG)], axis=1)
                for q in range(REFINE)
            ],
            axis=0,
        )
        found = jnp.dot(split(values, 0, 3), spread[...], preferred_element_type=f32)
        found = found[:rows] + found[rows : 2 * rows] + found[2 * rows :]
        for q in range(REFINE):
            for v in range(groups):
                array[v, pl.ds(q, 8, stride=REFINE), :] = found[
                    8 * q : 8 * q + 8, 128 * v : 128 * v + 128
                ]

    move_air(0)
    wait_wind(0)
    burn_window(0)
    for c in range(1, STEPS - 1):
        move_air(c)
        burn_window(c)
    burn_window(STEPS - 1)
    give(lambda q, p: xa[q + 1, p], level_out)
    move_air(STEPS - 1)
    give(lambda q, p: fuel[q, p], fuel_out)
    drain()
    force_air(STEPS - 1, wait_flux(STEPS - 1))


def release(air, level, fuel, air_out, level_out, fuel_out, sems):
    for f in range(4):
        pltpu.make_async_copy(air.at[f], air_out.at[f], sems.at[0]).start()
    copies = [pltpu.make_async_copy(air, air, sems.at[0])]
    for k, (held, out) in enumerate(((level, level_out), (fuel, fuel_out))):
        for v in range(held.shape[0]):
            pltpu.make_async_copy(
                held.at[v], out.at[:, pl.ds(128 * v, 128)], sems.at[1 + k]
            ).start()
        copies.append(pltpu.make_async_copy(held, held, sems.at[1 + k]))
    for copy in copies:
        copy.wait()


def solution(mesh):
    tiles, sects, subs = (mesh.shape[name] for name in ("tile", "sect", "sub"))
    bands = sects * subs
    air_spec = P(None, ("sect", "sub"), ("group", "tile"), None)
    fire_spec = P(("group", "tile"), ("sect", "sub"))

    def local(air_state, fire_level, *rest):
        depth, width = air_state.shape[1], air_state.shape[3]
        rows, cols = fire_level.shape
        groups = cols // 128
        assert air_state.shape[2] == 8 and cols == 64 * REFINE and rows == 8 * REFINE
        vmem = pl.BlockSpec(memory_space=pltpu.VMEM)
        hbm = pl.BlockSpec(memory_space=pltpu.HBM)
        dma = pltpu.SemaphoreType.DMA

        def blocks(*lead):
            return pltpu.VMEM((*lead, 8, 128), f32)

        held = pl.pallas_call(
            functools.partial(kernel, tiles, sects, subs),
            out_shape=(
                pltpu.VMEM(air_state.shape, f32),
                pltpu.VMEM((groups, rows, 128), f32),
                pltpu.VMEM((groups, rows, 128), f32),
            ),
            in_specs=[hbm] * 10,
            out_specs=(vmem, vmem, vmem),
            scratch_shapes=[
                pltpu.VMEM((4, depth + 2, 8, width), f32),
                pltpu.VMEM((4, depth + 2, 8, width), f32),
                pltpu.VMEM((4, depth + 2, 8, width), f32),
                pltpu.VMEM((4, depth + 2, 8, width), f32),
                pltpu.VMEM((STEPS, 2, 4, depth, 8, width), f32),
                blocks(14, SEG),
                blocks(14, SEG),
                blocks(14, SEG),
                blocks(REFINE, SEG),
                blocks(REFINE, SEG),
                blocks(REFINE, SEG),
                blocks(REFINE, SEG),
                blocks(REFINE, SEG),
                blocks(REFINE, SEG),
                pltpu.VMEM((2, groups, rows, 128), f32),
                pltpu.VMEM((2, groups, rows, 128), jnp.int32),
                pltpu.VMEM((cols, cols), bf16),
                pltpu.VMEM((cols, cols), bf16),
                pltpu.VMEM((256, 512), bf16),
                pltpu.VMEM((256, 128), bf16),
                blocks(2, 5),
                blocks(STEPS + 1),
                blocks(STEPS + 1, SEG + 1),
                blocks(STEPS + 1, SEG + 1),
                blocks(STEPS + 1, 2),
                blocks(STEPS + 1, 2),
                blocks(STEPS, bands, 2),
                blocks(STEPS, bands, 2),
                blocks(STEPS, bands, 2),
                blocks(STEPS, 2),
                blocks(STEPS, bands, 2),
                blocks(STEPS - 1, bands, 2),
                pltpu.SMEM((STEPS,), jnp.int32),
                pltpu.SMEM((NFUEL,), f32),
                pltpu.SMEM((NFUEL,), f32),
                pltpu.SMEM((NFUEL,), f32),
                pltpu.SMEM((NFUEL,), f32),
                dma((5,)),
                dma((5,)),
                dma((8,)),
                dma((2, 8)),
                dma((1,)),
                dma((2,)),
                dma((1,)),
                dma((2,)),
                dma((2, 2)),
                dma((4, 2)),
                dma((6,)),
                dma((2, 6)),
            ],
            compiler_params=pltpu.CompilerParams(
                collective_id=0, has_side_effects=True, vmem_limit_bytes=56 * 1024 * 1024
            ),
        )(air_state, fire_level, *rest)
        held = [pltpu.with_memory_space_constraint(x, pltpu.VMEM) for x in held]
        return pl.pallas_call(
            release,
            out_shape=(
                jax.ShapeDtypeStruct(air_state.shape, f32),
                jax.ShapeDtypeStruct(fire_level.shape, f32),
                jax.ShapeDtypeStruct(fire_level.shape, f32),
            ),
            in_specs=[vmem] * 3,
            out_specs=(hbm, hbm, hbm),
            scratch_shapes=[dma((3,))],
        )(*held)

    return jax.shard_map(
        local,
        mesh=mesh,
        in_specs=(air_spec, fire_spec, fire_spec, fire_spec, fire_spec) + (P(),) * 5,
        out_specs=(air_spec, fire_spec, fire_spec),
        check_vma=False,
    )
```

```python
import functools
import math

import jax
import jax.numpy as jnp
from jax import lax
from jax.experimental import pallas as pl
from jax.experimental.pallas import tpu as pltpu
from jax.sharding import PartitionSpec as P

LEVELS = 80
REFINE = 10
NFUEL = 13
STEPS = 4
SUBSTEPS = 4
DEEP = 4
SEG = REFINE // 2
MESH = pl.DeviceIdType.MESH
TINY = 1.1754944e-38
f32 = jnp.float32
bf16 = jnp.bfloat16


def split(value, axis, pieces):
    parts = []
    for _ in range(pieces):
        parts.append(value.astype(bf16))
        value = value - parts[-1].astype(f32)
    return jnp.concatenate(parts, axis=axis)


def indicator(mask, value=1.0):
    return jnp.where(mask, value, 0.0).astype(bf16)


def kernel(
    tiles,
    sects,
    subs,
    air_in,
    level_in,
    fuel_in,
    class_in,
    ign_in,
    plan_in,
    rate_in,
    burn_in,
    heat_in,
    moist_in,
    air_out,
    level_out,
    fuel_out,
    air_0,
    air_1,
    air_2,
    air_3,
    xh,
    xa,
    xb,
    rate,
    pace,
    fuel,
    binv,
    heat,
    moist,
    ign,
    bsum,
    stage,
    turned,
    gather,
    spread,
    wmat,
    smat,
    wnd,
    es,
    gs,
    hb,
    er,
    dg,
    wsend,
    wrecv,
    hrecv,
    fsend,
    frecv,
    grecv,
    plan,
    t_rate,
    t_burn,
    t_heat,
    t_moist,
    in_s,
    table_s,
    fire_s,
    fire_r,
    wind_s,
    wind_r,
    flux_s,
    flux_r,
    rim_s,
    rim_r,
    halo_s,
    halo_r,
):
    air = (air_0, air_1, air_2, air_3)
    bands = sects * subs
    depth = air_in.shape[1]
    width = air_in.shape[3]
    rows, cols = level_in.shape
    coarse = cols // REFINE
    groups = cols // 128
    tile_at = lax.axis_index("tile")
    sect_at = lax.axis_index("sect")
    sub_at = lax.axis_index("sub")
    band = sect_at * subs + sub_at
    not_first = tile_at > 0
    not_final = tile_at < tiles - 1
    band_low = band > 0
    band_high = band < bands - 1

    def device(tile_step, at_band):
        return {
            "tile": tile_at + tile_step,
            "sect": at_band // subs,
            "sub": at_band % subs,
        }

    def both(a, b):
        return jnp.logical_and(a, b)

    others = [
        (sect_at + a) % sects * subs + (sub_at + b) % subs
        for a in [*range(1, sects), 0]
        for b in range(subs)
        if a or b
    ]
    pending = []

    def send(condition, src, dst, send_sem, recv_sem, where):
        def make():
            return pltpu.make_async_remote_copy(
                src_ref=src,
                dst_ref=dst,
                send_sem=send_sem,
                recv_sem=recv_sem,
                device_id=where,
                device_id_type=MESH,
            )

        @pl.when(condition)
        def _():
            make().start()

        pending.append((condition, make))

    def drain():
        for condition, make in pending:
            if condition is None:
                make().wait_send()
                continue

            @pl.when(condition)
            def _(make=make):
                make().wait_send()

        pending.clear()

    def send_group(condition, parts, whole, send_sem, recv_sem, wheres):
        def make(src, dst, where):
            return pltpu.make_async_remote_copy(
                src_ref=src,
                dst_ref=dst,
                send_sem=send_sem,
                recv_sem=recv_sem,
                device_id=where,
                device_id_type=MESH,
            )

        @pl.when(condition)
        def _():
            for (src, dst), where in zip(parts, wheres):
                make(src, dst, where).start()

        pending.append((condition, lambda: make(whole, whole, wheres[0])))

    def send_tile(parts, whole, send_sem, recv_sem):
        def make(src, dst, j):
            return pltpu.make_async_remote_copy(
                src_ref=src,
                dst_ref=dst,
                send_sem=send_sem,
                recv_sem=recv_sem,
                device_id=device(0, j),
                device_id_type=MESH,
            )

        for j in others:
            make(*parts(j), j).start()

        pending.append((None, lambda: make(whole, whole, 0)))

    def receive_tile(whole, recv_sem, send_sem):
        pltpu.make_async_remote_copy(
            src_ref=whole,
            dst_ref=whole,
            send_sem=send_sem,
            recv_sem=recv_sem,
            device_id=device(0, 0),
            device_id_type=MESH,
        ).wait_recv()

    def receive(condition, dst, recv_sem, send_sem, where):
        @pl.when(condition)
        def _():
            pltpu.make_async_remote_copy(
                src_ref=dst,
                dst_ref=dst,
                send_sem=send_sem,
                recv_sem=recv_sem,
                device_id=where,
                device_id_type=MESH,
            ).wait_recv()

    def iota(shape, dim):
        return lax.broadcasted_iota(jnp.int32, shape, dim)

    barrier = pltpu.get_barrier_semaphore()
    for tile_step, condition in ((0, None), (-1, not_first), (1, not_final)):
        for j in range(bands):
            ok = (band != j) if condition is None else condition

            @pl.when(ok)
            def _(tile_step=tile_step, j=j):
                pl.semaphore_signal(
                    barrier, inc=1, device_id=device(tile_step, j), device_id_type=MESH
                )

    def fetch(array, held, slot):
        for v in range(groups):
            pltpu.make_async_copy(
                array.at[:, pl.ds(128 * v, 128)], held.at[v], in_s.at[slot]
            ).start()
        return pltpu.make_async_copy(held, held, in_s.at[slot])

    air_copy = pltpu.make_async_copy(air_in, air[0].at[:, pl.ds(1, depth)], in_s.at[3])
    air_copy.start()
    fire_copies = [
        fetch(class_in, turned.at[0], 0),
        fetch(ign_in, turned.at[1], 1),
        fetch(level_in, stage.at[0], 2),
    ]
    tables = [
        pltpu.make_async_copy(src, dst, table_s.at[k])
        for k, (src, dst) in enumerate(
            (
                (rate_in, t_rate),
                (plan_in, plan),
                (burn_in, t_burn),
                (heat_in, t_heat),
                (moist_in, t_moist),
            )
        )
    ]
    for copy in tables:
        copy.start()
    fuel_copy = fetch(fuel_in, stage.at[1], 4)

    spot = iota((16, cols), 1)
    spot = SEG * (spot % 128) + spot // 128
    line16 = iota((16, cols), 0)

    def make_gather(i, carry):
        at = pl.ds(pl.multiple_of(i * 16, 16), 16)
        gather[at, :] = indicator(spot == line16 + 16 * i)
        return carry

    lax.fori_loop(0, cols // 16, make_gather, 0, unroll=4)

    sub = iota((8, 128), 0)
    lane = iota((8, 128), 1)
    octet = lane // 8
    inner = lane % 8 < 4
    edge_w = sub == jnp.where(not_first, -1, 0)
    edge_e = sub == jnp.where(not_final, -1, 7)
    edge_s = lane == jnp.where(band_low, -1, 0)
    edge_n = lane == jnp.where(band_high, -1, 127)
    strip_w = both(edge_w, octet == 3)
    strip_e = both(edge_e, octet == 12)

    def rolled(value, shift, axis):
        shift = shift % value.shape[axis]
        return pltpu.roll(value, shift, axis) if shift else value

    row8 = iota((8, width), 0)
    total_col = sum(math.exp(-k / LEVELS) for k in range(LEVELS))
    total_prof = sum(math.exp(-2.0 * k / LEVELS) for k in range(LEVELS))
    col_base = f32(0.0)
    prof_base = f32(0.0)
    for j in range(bands):
        here = band == j
        col_base = jnp.where(here, f32(math.exp(-j * depth / LEVELS) / total_col), col_base)
        prof_base = jnp.where(
            here, f32(LEVELS * math.exp(-2.0 * j * depth / LEVELS) / total_prof), prof_base
        )
    col_ratio = math.exp(-1.0 / LEVELS)
    prof_ratio = math.exp(-2.0 / LEVELS)

    def send_wind(c, total_u, total_v):
        stacked = jnp.concatenate([total_u, total_v], axis=0)
        for j in range(bands):
            shift = (128 // 4 - coarse * j) % width
            window = (pltpu.roll(stacked, shift, 1) if shift else stacked)[:, :128]
            wsend[c, j, 0] = window[:8]
            wsend[c, j, 1] = window[8:]

            @pl.when(band == j)
            def _(window=window, j=j):
                wrecv[c, j, 0] = window[:8]
                wrecv[c, j, 1] = window[8:]

        send_tile(
            lambda j: (wsend.at[c, j], wrecv.at[c, band]),
            wsend.at[c, pl.ds(0, bands - 1)],
            wind_s.at[0],
            wind_r.at[c % 2],
        )
        for way, tile_step, ok in ((0, 1, not_final), (1, -1, not_first)):
            row, there = pl.ds(7 - 7 * way, 1), pl.ds(7 * way, 1)
            send_group(
                ok,
                [
                    (wsend.at[c, j, :, row, :], hrecv.at[c, band, :, there, :])
                    for j in range(bands)
                ],
                hrecv.at[c, :, :, there, :],
                rim_s.at[0, way],
                rim_r.at[c % 2, way],
                [device(tile_step, j) for j in range(bands)],
            )

    def wait_wind(c):
        receive_tile(wrecv.at[c, pl.ds(0, bands - 1)], wind_r.at[c % 2], wind_s.at[0])
        for way, tile_step, ok in ((0, -1, not_first), (1, 1, not_final)):
            receive(
                ok,
                hrecv.at[c, :, :, pl.ds(7 * way, 1), :],
                rim_r.at[c % 2, way],
                rim_s.at[0, way],
                device(tile_step, 0),
            )
        own, beyond = [], []
        for k in range(2):
            here, there = wrecv[c, 0, k], hrecv[c, 0, k]
            for j in range(1, bands):
                here, there = here + wrecv[c, j, k], there + hrecv[c, j, k]
            own.append(here)
            beyond.append(
                jnp.where(
                    sub < 4,
                    jnp.broadcast_to(there[:1], (8, 128)),
                    jnp.broadcast_to(there[7:], (8, 128)),
                )
            )
        together = jnp.concatenate(own + beyond, axis=0)
        wide = jnp.dot(split(together, 1, 2), wmat[...], preferred_element_type=f32)
        for k in range(2):
            own, beyond = wide[8 * k : 8 * k + 8], wide[16 + 8 * k : 24 + 8 * k]
            wnd[k, 0] = own[:, :128]
            wnd[k, 1] = beyond[:, :128]
            for at in (1, 2):
                here = own[:, 128 * at : 128 * at + 128]
                there = beyond[:, 128 * at : 128 * at + 128]
                below = jnp.where(sub == 0, there, pltpu.roll(here, 1, 0))
                above = jnp.where(sub == 7, there, pltpu.roll(here, 7, 0))
                wnd[k, at + 1] = jnp.where(
                    octet < 3, below, jnp.where(octet >= 13, above, here)
                )
            wnd[k, 4] = beyond[:, 384:]

    def portions(c):
        half = depth // 2
        return [(0, half), (half, depth - half)] if c == 0 else [(0, depth)]

    def send_air(c):
        send(
            band_high,
            air[c].at[:, depth],
            air[c].at[:, 0],
            halo_s.at[4],
            halo_r.at[c % 2, 4],
            device(0, band + 1),
        )
        send(
            band_low,
            air[c].at[:, 1],
            air[c].at[:, depth + 1],
            halo_s.at[5],
            halo_r.at[c % 2, 5],
            device(0, band - 1),
        )
        for piece, (start, count) in enumerate(portions(c)):
            send(
                not_final,
                air[c].at[:, pl.ds(1 + start, count), pl.ds(7, 1), :],
                xh.at[c, 0, :, pl.ds(start, count), pl.ds(7, 1), :],
                halo_s.at[2 * piece],
                halo_r.at[c % 2, 2 * piece],
                device(1, band),
            )
            send(
                not_first,
                air[c].at[:, pl.ds(1 + start, count), pl.ds(0, 1), :],
                xh.at[c, 1, :, pl.ds(start, count), pl.ds(0, 1), :],
                halo_s.at[2 * piece + 1],
                halo_r.at[c % 2, 2 * piece + 1],
                device(-1, band),
            )

    def wait_air(c, piece):
        start, count = portions(c)[piece]
        receive(
            not_first,
            xh.at[c, 0, :, pl.ds(start, count), pl.ds(7, 1), :],
            halo_r.at[c % 2, 2 * piece],
            halo_s.at[2 * piece],
            device(-1, band),
        )
        receive(
            not_final,
            xh.at[c, 1, :, pl.ds(start, count), pl.ds(0, 1), :],
            halo_r.at[c % 2, 2 * piece + 1],
            halo_s.at[2 * piece + 1],
            device(1, band),
        )
        if piece == 0:
            receive(
                band_low, air[c].at[:, 0], halo_r.at[c % 2, 4], halo_s.at[4], device(0, band - 1)
            )
            receive(
                band_high,
                air[c].at[:, depth + 1],
                halo_r.at[c % 2, 5],
                halo_s.at[5],
                device(0, band + 1),
            )

    nothing = jnp.zeros((8, width), f32)
    air_copy.wait()

    def first_air(i, carry):
        weight, total_u, total_v = carry
        total_u = total_u + weight * air[0][2, i + 1]
        total_v = total_v + weight * air[0][3, i + 1]
        return weight * f32(col_ratio), total_u, total_v

    _, total_u, total_v = lax.fori_loop(
        0, depth, first_air, (col_base, nothing, nothing), unroll=4
    )

    expected = (
        bands - 1 + bands * (not_first.astype(jnp.int32) + not_final.astype(jnp.int32))
    )
    pl.semaphore_wait(barrier, expected)

    send_air(0)
    send_wind(0, total_u, total_v)

    def reorder(load):
        return jnp.concatenate(
            [
                jnp.concatenate([load(v, pl.ds(q, 8, stride=REFINE)) for v in range(groups)], axis=1)
                for q in range(REFINE)
            ],
            axis=0,
        )

    for copy in fire_copies:
        copy.wait()
    tables[0].wait()
    kinds = reorder(
        lambda v, at: (turned[0, v, at, :] + 16 * turned[1, v, at, :]).astype(f32)
    ).astype(bf16)
    pieces = split(reorder(lambda v, at: stage[0, v, at, :]), 0, 3)
    found = jnp.dot(
        jnp.concatenate([pieces, kinds], axis=0), gather[...], preferred_element_type=f32
    )
    together = found[:rows] + found[rows : 2 * rows] + found[2 * rows : 3 * rows]
    kinds = found[3 * rows :]
    for q in range(REFINE):
        for p in range(SEG):
            kind = kinds[8 * q : 8 * q + 8, 128 * p : 128 * p + 128]
            when = jnp.floor(kind * (1.0 / 16.0))
            now = together[8 * q : 8 * q + 8, 128 * p : 128 * p + 128]
            ign[q, p] = when
            moist[q, p] = kind - 16.0 * when
            xa[q + 1, p] = jnp.where(when <= 0.0, jnp.minimum(now, -1.0), now)

    def find_rate(q, carry):
        for p in range(SEG):
            kind = moist[q, p]
            value = jnp.full((8, 128), t_rate[0], f32)
            for k in range(1, NFUEL):
                value = jnp.where(kind == float(k), t_rate[k], value)
            rate[q + 1, p] = value
        return carry

    lax.fori_loop(0, REFINE, find_rate, 0, unroll=2)

    def outline(e, ref):
        def edge(q, found):
            x = [ref[q + 1, p] for p in range(SEG)]
            near = pltpu.roll(x[SEG - 1], 1, 1)
            for k in range(1, DEEP):
                near = jnp.where(lane == k, pltpu.roll(x[SEG - 1 - k], k + 1, 1), near)
            for k in range(DEEP):
                near = jnp.where(lane == 127 - k, pltpu.roll(x[k], 127 - k, 1), near)
            return jnp.where(octet == q + 3, pltpu.roll(near, 8 * q + 28, 1), found)

        found = lax.fori_loop(0, REFINE, edge, jnp.zeros((8, 128), f32), unroll=10)
        es[e] = found
        gs[e, SEG] = jnp.where(
            sub < 4,
            jnp.broadcast_to(found[7:8], (8, 128)),
            jnp.broadcast_to(found[0:1], (8, 128)),
        )

        def border(p, carry):
            value = rolled(ref[REFINE, p], 1, 0)
            for k in range(1, DEEP):
                value = jnp.where(sub == k, rolled(ref[REFINE - k, p], k + 1, 0), value)
            for k in range(DEEP):
                value = jnp.where(sub == 4 + k, rolled(ref[DEEP - k, p], 4 + k, 0), value)
            gs[e, p] = value
            return carry

        lax.fori_loop(0, SEG, border, 0, unroll=5)

    def fields(c):
        return pl.ds(0, 2) if c == 0 else pl.ds(1 + c, 1)

    def send_outline(c):
        at = fields(c)
        for way, tile_step, ok in ((0, 1, not_final), (1, -1, not_first)):
            part = pl.ds(4 * way, 4)
            send(
                ok,
                gs.at[at, :, part, :],
                hb.at[at, :, part, :],
                fire_s.at[way],
                fire_r.at[c % 2, way],
                device(tile_step, band),
            )
        for side, band_step, ok in ((0, 1, band_high), (1, -1, band_low)):
            send(
                ok,
                es.at[at],
                er.at[at, side],
                fire_s.at[2 + side],
                fire_r.at[c % 2, 2 + side],
                device(0, band + band_step),
            )
            for way, tile_step, also in ((0, 1, not_final), (1, -1, not_first)):
                send(
                    both(ok, also),
                    es.at[at, pl.ds(7 - 7 * way, 1), :],
                    dg.at[at, side, pl.ds(7 * way, 1), :],
                    fire_s.at[4 + 2 * side + way],
                    fire_r.at[c % 2, 4 + 2 * side + way],
                    device(tile_step, band + band_step),
                )

    def wait_outline(c):
        at = fields(c)
        for way, tile_step, ok in ((0, -1, not_first), (1, 1, not_final)):
            receive(
                ok,
                hb.at[at, :, pl.ds(4 * way, 4), :],
                fire_r.at[c % 2, way],
                fire_s.at[way],
                device(tile_step, band),
            )
        for side, band_step, ok in ((0, -1, band_low), (1, 1, band_high)):
            receive(
                ok,
                er.at[at, side],
                fire_r.at[c % 2, 2 + side],
                fire_s.at[2 + side],
                device(0, band + band_step),
            )
            for way, tile_step, also in ((0, -1, not_first), (1, 1, not_final)):
                receive(
                    both(ok, also),
                    dg.at[at, side, pl.ds(7 * way, 1), :],
                    fire_r.at[c % 2, 4 + 2 * side + way],
                    fire_s.at[4 + 2 * side + way],
                    device(tile_step, band + band_step),
                )

    def surround(e, ref):
        for p in range(SEG):
            ref[12, p] = hb[e, p]
        mine, beyond = es[e], hb[e, SEG]

        def strip(here, there):
            below = jnp.where(sub == 0, there, pltpu.roll(here, 1, 0))
            above = jnp.where(sub == 7, there, pltpu.roll(here, 7, 0))
            return jnp.where(
                octet < 3,
                pltpu.roll(below, 48, 1),
                jnp.where(octet >= 13, pltpu.roll(above, 80, 1), here),
            )

        low = strip(jnp.where(inner, mine, er[e, 0]), jnp.where(inner, beyond, dg[e, 0]))
        high = strip(jnp.where(inner, er[e, 1], mine), jnp.where(inner, dg[e, 1], beyond))
        mixed = jnp.where(inner, high, low)
        corner = mixed
        for k in range(3):
            corner = jnp.where(sub == k, rolled(rolled(mixed, 108 + 8 * k, 1), k, 0), corner)
            corner = jnp.where(sub == 7 - k, rolled(rolled(mixed, 20 - 8 * k, 1), -k, 0), corner)
        ref[13, 0] = low
        ref[13, 1] = high
        ref[13, 2] = corner

    outline(0, rate)
    outline(1, xa)
    send_outline(0)

    @pl.when(jnp.logical_not(not_first))
    def _():
        def zero(i, carry):
            for c in range(STEPS):
                for f in range(4):
                    xh[c, 0, f, i] = jnp.zeros((8, width), f32)
            return carry

        lax.fori_loop(0, depth, zero, 0)
        grecv[:, :, :, 7:] = jnp.zeros((STEPS - 1, bands, 2, 1, 128), f32)

    @pl.when(jnp.logical_not(not_final))
    def _():
        grecv[:, :, :, :1] = jnp.zeros((STEPS - 1, bands, 2, 1, 128), f32)

        def zero(i, carry):
            for c in range(STEPS):
                for f in range(4):
                    xh[c, 1, f, i] = jnp.zeros((8, width), f32)
            return carry

        lax.fori_loop(0, depth, zero, 0)

    @pl.when(jnp.logical_not(band_low))
    def _():
        for c in range(STEPS):
            air[c][:, 0] = jnp.zeros((4, 8, width), f32)

    @pl.when(jnp.logical_not(band_high))
    def _():
        for c in range(STEPS):
            air[c][:, depth + 1] = jnp.zeros((4, 8, width), f32)

    column = iota((16, cols), 1)

    def make_spread(i, carry):
        at = pl.ds(pl.multiple_of(i * 16, 16), 16)
        spread[at, :] = indicator(column == SEG * (line16 + 16 * (i % 8)) + i // 8)
        return carry

    source, place = iota((128, 512), 0), iota((128, 512), 1)
    block, place = place // 128, place % 128
    near = place % 8 < 4
    first = jnp.where(block == 0, 32 + place // 2, jnp.where(near, 32, 31))
    second = jnp.where(
        block == 2, jnp.where(near, 96, 95), jnp.where(place < 64, 31, 96)
    )
    pattern = indicator(source == jnp.where(block < 2, first, second), 0.5)
    wmat[:128, :] = pattern
    wmat[128:, :] = pattern
    source, place = iota((128, 128), 0), iota((128, 128), 1)
    pattern = indicator(place == source // 2 + coarse * (band % 2))
    smat[:128, :] = pattern
    smat[128:, :] = pattern

    for copy in tables[1:]:
        copy.wait()

    def lookup(q, carry):
        for p in range(SEG):
            kind = moist[q, p]
            burn = jnp.full((8, 128), t_burn[0], f32)
            hot = jnp.full((8, 128), t_heat[0], f32)
            wet = jnp.full((8, 128), t_moist[0], f32)
            for k in range(1, NFUEL):
                same = kind == float(k)
                burn = jnp.where(same, t_burn[k], burn)
                hot = jnp.where(same, t_heat[k], hot)
                wet = jnp.where(same, t_moist[k], wet)
            binv[q, p] = 1.0 / burn
            heat[q, p] = hot
            moist[q, p] = wet
            bsum[q, p] = jnp.zeros((8, 128), f32)
        return carry

    lax.fori_loop(0, REFINE, lookup, 0)
    fuel_copy.wait()
    pieces = split(reorder(lambda v, at: stage[1, v, at, :]), 0, 3)
    found = jnp.dot(pieces, gather[...], preferred_element_type=f32)
    together = found[:rows] + found[rows : 2 * rows] + found[2 * rows :]
    for q in range(REFINE):
        for p in range(SEG):
            fuel[q, p] = together[8 * q : 8 * q + 8, 128 * p : 128 * p + 128]
    lax.fori_loop(0, cols // 16, make_spread, 0, unroll=4)

    def uphill(d):
        return jnp.maximum(d, 0.0) * d

    def downhill(d):
        return jnp.minimum(d, 0.0) * d

    def moved(here, dw, de, ds, dn, speed, wu, wv):
        square = (uphill(dw) + downhill(de)) + (uphill(ds) + downhill(dn))
        steep = square * lax.rsqrt(jnp.maximum(square, TINY))
        gx, gy = dw + de, ds + dn
        tail = (wu * gx + wv * gy) * lax.rsqrt(gx * gx + gy * gy + 4.0)
        return here - (speed * (1.0 + jnp.maximum(tail, 0.0))) * steep

    def substep(src, dst, fire_step):
        low, high, corner = src[13, 0], src[13, 1], src[13, 2]
        mixed = jnp.where(inner, high, low)
        top, border, bottom = [], [], []
        for p in range(SEG):
            first, final, beyond = src[1, p], src[REFINE, p], src[12, p]
            border.append(beyond)
            top.append(
                jnp.where(
                    edge_w, first, jnp.where(sub == 0, beyond, pltpu.roll(final, 1, 0))
                )
            )
            src[11, p] = jnp.where(
                edge_e, final, jnp.where(sub == 7, beyond, pltpu.roll(first, 7, 0))
            )

        def across(x, outer):
            south = jnp.where(lane == 0, outer, pltpu.roll(x[SEG - 1], 1, 1))
            north = jnp.where(lane == 127, outer, pltpu.roll(x[0], 127, 1))
            south = jnp.where(edge_s, x[0], south)
            north = jnp.where(edge_n, x[SEG - 1], north)
            line = [south] + x + [north]
            return [line[k + 1] - line[k] for k in range(SEG + 1)]

        wu, wv = wnd[0, 0], wnd[1, 0]

        def line(q, carry):
            x, dw = carry
            after = [src[q + 2, p] for p in range(SEG)]
            dh = across(x, pltpu.roll(mixed, 100 - 8 * q, 1))
            de = []
            for p in range(SEG):
                de.append(after[p] - x[p])
                new = moved(
                    x[p], dw[p], de[p], dh[p], dh[p + 1], pace[q + 1, p], wu, wv
                )
                dst[q + 1, p] = new
                bsum[q, p] = bsum[q, p] + jnp.clip(new, -0.5, 0.5)
            return after, de

        x = [src[1, p] for p in range(SEG)]
        lax.fori_loop(0, REFINE, line, (x, [x[p] - top[p] for p in range(SEG)]), unroll=10)

        wu, wv = wnd[0, 1], wnd[1, 1]
        dh = across(border, corner)
        for p in range(SEG):
            here = border[p]
            west = jnp.where(sub == 7, src[REFINE, p], pltpu.roll(here, 7, 0))
            east = jnp.where(sub == 0, src[1, p], pltpu.roll(here, 1, 0))
            dst[12, p] = moved(
                here, here - west, east - here, dh[p], dh[p + 1], pace[12, p], wu, wv
            )
        for k, here in enumerate((low, high)):
            west = jnp.where(strip_w, here, pltpu.roll(here, 8, 1))
            east = jnp.where(strip_e, here, pltpu.roll(here, 120, 1))
            south, north = pltpu.roll(here, 127, 1), pltpu.roll(here, 1, 1)
            dst[13, k] = moved(
                here,
                here - west,
                east - here,
                here - south,
                north - here,
                pace[13, k],
                wnd[0, 2 + k],
                wnd[1, 2 + k],
            )
        west = jnp.where(sub == 7, pltpu.roll(mixed, 28, 1), pltpu.roll(corner, 7, 0))
        east = jnp.where(sub == 0, pltpu.roll(mixed, 100, 1), pltpu.roll(corner, 1, 0))
        south = jnp.where(lane == 127, border[SEG - 1], pltpu.roll(corner, 127, 1))
        north = jnp.where(lane == 0, border[0], pltpu.roll(corner, 1, 1))
        dst[13, 2] = moved(
            corner,
            corner - west,
            east - corner,
            corner - south,
            north - corner,
            pace[13, 2],
            wnd[0, 4],
            wnd[1, 4],
        )

    lane_a = lax.broadcasted_iota(jnp.int32, (8, width), 1)

    def write(c, f, i, value):
        if c == STEPS - 1:
            air_out[f, i] = value
        else:
            air[c + 1][f, i + 1] = value

    def wait_flux(c):
        receive_tile(frecv.at[c, pl.ds(0, bands - 1)], flux_r.at[c % 2], flux_s.at[0])
        return [
            jnp.concatenate(
                [frecv[c, 2 * k, f] + frecv[c, 2 * k + 1, f] for k in range(width // 128)],
                axis=1,
            )
            for f in range(2)
        ]

    def wait_rim(c):
        for way, tile_step, ok in ((0, -1, not_first), (1, 1, not_final)):
            row = pl.ds(7 - 7 * way, 1)
            receive(
                ok,
                grecv.at[c, :, :, row, :],
                rim_r.at[2 + c % 2, way],
                rim_s.at[1, way],
                device(tile_step, 0),
            )
        return [
            jnp.concatenate(
                [grecv[c, 2 * k, f] + grecv[c, 2 * k + 1, f] for k in range(width // 128)],
                axis=1,
            )
            for f in range(2)
        ]

    def force_air(c, flux):
        def force(i, weight):
            for f in range(2):
                now = air_out[f, i] if c == STEPS - 1 else air[c + 1][f, i + 1]
                write(c, f, i, now + weight * flux[f])
            return weight * f32(prof_ratio)

        lax.fori_loop(0, depth, force, prof_base * f32(2.0), unroll=4)

    def move_air(c):
        if c < STEPS - 1:
            drain()
        if c > 0:
            flux = wait_flux(c - 1)
            force_air(c - 1, flux)
        wait_air(c, 0)
        if c > 0:
            low = jnp.where(band_low, prof_base * f32(2.0 / prof_ratio), 0.0)
            high = jnp.where(band_high, prof_base * f32(2.0 * prof_ratio**depth), 0.0)
            for f in range(2):
                air[c][f, 0] = air[c][f, 0] + low * flux[f]
                air[c][f, depth + 1] = air[c][f, depth + 1] + high * flux[f]
        final = c == STEPS - 1

        def update(i, carry):
            weight, total_u, total_v = carry
            u, v = air[c][2, i + 1], air[c][3, i + 1]
            to_w = 0.02 + 0.1 * jnp.maximum(u, 0.0)
            to_e = 0.02 - 0.1 * jnp.minimum(u, 0.0)
            to_s = 0.02 + 0.1 * jnp.maximum(v, 0.0)
            to_n = 0.02 - 0.1 * jnp.minimum(v, 0.0)
            to_here = 0.96 - ((to_w + to_e) + (to_s + to_n))
            to_s = jnp.where(lane_a == 0, 0.0, to_s)
            to_n = jnp.where(lane_a == width - 1, 0.0, to_n)
            lift_x = lift_s = lift_n = None
            for f in range(4):
                here = air[c][f, i + 1]
                west, east = xh[c, 0, f, i], xh[c, 1, f, i]
                west = pltpu.roll(jnp.where(row8 == 7, west, here), 1, 0)
                east = pltpu.roll(jnp.where(row8 == 0, east, here), 7, 0)
                south, north = pltpu.roll(here, 1, 1), pltpu.roll(here, width - 1, 1)
                new = (to_here * here + (to_w * west + to_e * east)) + (
                    (to_s * south + to_n * north) + 0.02 * (air[c][f, i] + air[c][f, i + 2])
                )
                if f == 0:
                    lift_x, lift_s, lift_n = east - west, south, north
                elif f == 1:
                    lift_x = lift_x + 0.6 * (east - west)
                    lift_s = jnp.where(lane_a == 0, 0.0, lift_s + 0.6 * south)
                    lift_n = jnp.where(lane_a == width - 1, 0.0, lift_n + 0.6 * north)
                elif f == 2:
                    new = new + 0.015 * lift_x
                    total_u = total_u + weight * new
                else:
                    new = new + 0.015 * (lift_n - lift_s)
                    total_v = total_v + weight * new
                write(c, f, i, new)
            return weight * f32(col_ratio), total_u, total_v

        carry = (col_base, nothing, nothing)
        for piece, (start, count) in enumerate(portions(c)):
            if piece > 0:
                wait_air(c, piece)
            carry = lax.fori_loop(start, start + count, update, carry, unroll=10)
        _, total_u, total_v = carry
        if c > 0:
            rim = wait_rim(c - 1)
            west = [jnp.where(row8 == 0, pltpu.roll(rim[f], 1, 0), 0.0) for f in range(2)]
            east = [jnp.where(row8 == 7, pltpu.roll(rim[f], 7, 0), 0.0) for f in range(2)]
            push = 0.015 * ((east[0] - west[0]) + 0.6 * (east[1] - west[1]))

            def border(i, carry):
                weight, share, total_u = carry
                u = air[c][2, i + 1]
                to_w = share * (0.02 + 0.1 * jnp.maximum(u, 0.0))
                to_e = share * (0.02 - 0.1 * jnp.minimum(u, 0.0))
                for f in range(2):
                    now = air_out[f, i] if final else air[c + 1][f, i + 1]
                    write(c, f, i, now + (to_w * west[f] + to_e * east[f]))
                more = share * push
                now = air_out[2, i] if final else air[c + 1][2, i + 1]
                write(c, 2, i, now + more)
                return weight * f32(col_ratio), share * f32(prof_ratio), total_u + weight * more

            _, _, total_u = lax.fori_loop(
                0, depth, border, (col_base, prof_base * f32(2.0), total_u), unroll=5
            )
        if not final:
            send_wind(c + 1, total_u, total_v)
            send_air(c + 1)

    def send_rim(c):
        for way, tile_step, ok in ((0, 1, not_final), (1, -1, not_first)):
            row = pl.ds(7 - 7 * way, 1)
            send_group(
                ok,
                [(fsend.at[c, :, row, :], grecv.at[c, band, :, row, :]) for j in range(bands)],
                grecv.at[c, :, :, row, :],
                rim_s.at[1, way],
                rim_r.at[2 + c % 2, way],
                [device(tile_step, j) for j in range(bands)],
            )

    def burn_fire(c, fire_step):
        def burn(q, carry):
            hot, wet = carry
            for p in range(SEG):
                now = fuel[q, p]
                spent = (float(SUBSTEPS) * 0.5 - bsum[q, p]) * binv[q, p]
                remain = now * jnp.exp(-fire_step * spent)
                used = now - remain
                fuel[q, p] = remain
                bsum[q, p] = jnp.zeros((8, 128), f32)
                hot = hot + used * heat[q, p]
                wet = wet + used * moist[q, p]
            return hot, wet

        zero = jnp.zeros((8, 128), f32)
        hot, wet = lax.fori_loop(0, REFINE, burn, (zero, zero), unroll=10)
        flux = jnp.dot(
            split(jnp.concatenate([hot, wet], axis=0), 1, 2),
            smat[...],
            preferred_element_type=f32,
        ) * f32(1.0 / (REFINE * REFINE))
        fsend[c, 0] = flux[:8]
        fsend[c, 1] = flux[8:]
        for j in range(bands):

            @pl.when(band == j)
            def _(j=j):
                frecv[c, j, 0] = flux[:8]
                frecv[c, j, 1] = flux[8:]

        send_tile(
            lambda j: (fsend.at[c], frecv.at[c, band]),
            frecv.at[c, pl.ds(0, bands - 1)],
            flux_s.at[0],
            flux_r.at[c % 2],
        )
        if c < STEPS - 1:
            send_rim(c)

    def burn_window(c):
        fire_step = plan[c].astype(f32) * f32(0.15)
        if c == STEPS - 1:
            drain()
        wait_outline(c)
        if c == 0:
            surround(0, rate)
        surround(1 + c, xa)

        for q in range(1, REFINE + 1):
            for p in range(SEG):
                pace[q, p] = fire_step * rate[q, p]
        for p in range(SEG):
            pace[12, p] = fire_step * rate[12, p]
        for k in range(3):
            pace[13, k] = fire_step * rate[13, k]

        def pair(i, carry):
            substep(xa, xb, fire_step)
            substep(xb, xa, fire_step)
            return carry

        lax.fori_loop(0, SUBSTEPS // 2, pair, 0)
        if c != STEPS - 2:
            burn_fire(c, fire_step)
        if c < STEPS - 1:

            def ignite(q, carry):
                for p in range(SEG):
                    now = xa[q + 1, p]
                    xa[q + 1, p] = jnp.where(
                        ign[q, p] <= float(c + 1), jnp.minimum(now, -1.0), now
                    )
                return carry

            lax.fori_loop(0, REFINE, ignite, 0, unroll=10)
            outline(2 + c, xa)
            send_outline(1 + c)
            if c == STEPS - 2:
                burn_fire(c, fire_step)
            wait_wind(c + 1)

    def give(load, array):
        values = jnp.concatenate(
            [
                jnp.concatenate([load(q, p) for p in range(SEG)], axis=1)
                for q in range(REFINE)
            ],
            axis=0,
        )
        found = jnp.dot(split(values, 0, 3), spread[...], preferred_element_type=f32)
        found = found[:rows] + found[rows : 2 * rows] + found[2 * rows :]
        for q in range(REFINE):
            for v in range(groups):
                array[v, pl.ds(q, 8, stride=REFINE), :] = found[
                    8 * q : 8 * q + 8, 128 * v : 128 * v + 128
                ]

    move_air(0)
    wait_wind(0)
    burn_window(0)
    for c in range(1, STEPS - 1):
        move_air(c)
        burn_window(c)
    burn_window(STEPS - 1)
    give(lambda q, p: xa[q + 1, p], level_out)
    move_air(STEPS - 1)
    give(lambda q, p: fuel[q, p], fuel_out)
    drain()
    force_air(STEPS - 1, wait_flux(STEPS - 1))


def release(air, level, fuel, air_out, level_out, fuel_out, sems):
    for f in range(4):
        pltpu.make_async_copy(air.at[f], air_out.at[f], sems.at[0]).start()
    copies = [pltpu.make_async_copy(air, air, sems.at[0])]
    for k, (held, out) in enumerate(((level, level_out), (fuel, fuel_out))):
        for v in range(held.shape[0]):
            pltpu.make_async_copy(
                held.at[v], out.at[:, pl.ds(128 * v, 128)], sems.at[1 + k]
            ).start()
        copies.append(pltpu.make_async_copy(held, held, sems.at[1 + k]))
    for copy in copies:
        copy.wait()


def solution(mesh):
    tiles, sects, subs = (mesh.shape[name] for name in ("tile", "sect", "sub"))
    bands = sects * subs
    air_spec = P(None, ("sect", "sub"), ("group", "tile"), None)
    fire_spec = P(("group", "tile"), ("sect", "sub"))

    def local(air_state, fire_level, *rest):
        depth, width = air_state.shape[1], air_state.shape[3]
        rows, cols = fire_level.shape
        groups = cols // 128
        assert air_state.shape[2] == 8 and cols == 64 * REFINE and rows == 8 * REFINE
        vmem = pl.BlockSpec(memory_space=pltpu.VMEM)
        hbm = pl.BlockSpec(memory_space=pltpu.HBM)
        dma = pltpu.SemaphoreType.DMA

        def blocks(*lead):
            return pltpu.VMEM((*lead, 8, 128), f32)

        held = pl.pallas_call(
            functools.partial(kernel, tiles, sects, subs),
            out_shape=(
                pltpu.VMEM(air_state.shape, f32),
                pltpu.VMEM((groups, rows, 128), f32),
                pltpu.VMEM((groups, rows, 128), f32),
            ),
            in_specs=[hbm] * 10,
            out_specs=(vmem, vmem, vmem),
            scratch_shapes=[
                pltpu.VMEM((4, depth + 2, 8, width), f32),
                pltpu.VMEM((4, depth + 2, 8, width), f32),
                pltpu.VMEM((4, depth + 2, 8, width), f32),
                pltpu.VMEM((4, depth + 2, 8, width), f32),
                pltpu.VMEM((STEPS, 2, 4, depth, 8, width), f32),
                blocks(14, SEG),
                blocks(14, SEG),
                blocks(14, SEG),
                blocks(14, SEG),
                blocks(REFINE, SEG),
                blocks(REFINE, SEG),
                blocks(REFINE, SEG),
                blocks(REFINE, SEG),
                blocks(REFINE, SEG),
                blocks(REFINE, SEG),
                pltpu.VMEM((2, groups, rows, 128), f32),
                pltpu.VMEM((2, groups, rows, 128), jnp.int32),
                pltpu.VMEM((cols, cols), bf16),
                pltpu.VMEM((cols, cols), bf16),
                pltpu.VMEM((256, 512), bf16),
                pltpu.VMEM((256, 128), bf16),
                blocks(2, 5),
                blocks(STEPS + 1),
                blocks(STEPS + 1, SEG + 1),
                blocks(STEPS + 1, SEG + 1),
                blocks(STEPS + 1, 2),
                blocks(STEPS + 1, 2),
                blocks(STEPS, bands, 2),
                blocks(STEPS, bands, 2),
                blocks(STEPS, bands, 2),
                blocks(STEPS, 2),
                blocks(STEPS, bands, 2),
                blocks(STEPS - 1, bands, 2),
                pltpu.SMEM((STEPS,), jnp.int32),
                pltpu.SMEM((NFUEL,), f32),
                pltpu.SMEM((NFUEL,), f32),
                pltpu.SMEM((NFUEL,), f32),
                pltpu.SMEM((NFUEL,), f32),
                dma((5,)),
                dma((5,)),
                dma((8,)),
                dma((2, 8)),
                dma((1,)),
                dma((2,)),
                dma((1,)),
                dma((2,)),
                dma((2, 2)),
                dma((4, 2)),
                dma((6,)),
                dma((2, 6)),
            ],
            compiler_params=pltpu.CompilerParams(
                collective_id=0, has_side_effects=True, vmem_limit_bytes=56 * 1024 * 1024
            ),
        )(air_state, fire_level, *rest)
        held = [pltpu.with_memory_space_constraint(x, pltpu.VMEM) for x in held]
        return pl.pallas_call(
            release,
            out_shape=(
                jax.ShapeDtypeStruct(air_state.shape, f32),
                jax.ShapeDtypeStruct(fire_level.shape, f32),
                jax.ShapeDtypeStruct(fire_level.shape, f32),
            ),
            in_specs=[vmem] * 3,
            out_specs=(hbm, hbm, hbm),
            scratch_shapes=[dma((3,))],
        )(*held)

    return jax.shard_map(
        local,
        mesh=mesh,
        in_specs=(air_spec, fire_spec, fire_spec, fire_spec, fire_spec) + (P(),) * 5,
        out_specs=(air_spec, fire_spec, fire_spec),
        check_vma=False,
    )
```

```python
import functools
import math

import jax
import jax.numpy as jnp
from jax import lax
from jax.experimental import pallas as pl
from jax.experimental.pallas import tpu as pltpu
from jax.sharding import PartitionSpec as P

LEVELS = 80
REFINE = 10
NFUEL = 13
STEPS = 4
SUBSTEPS = 4
DEEP = 4
SEG = REFINE // 2
MESH = pl.DeviceIdType.MESH
TINY = 1.1754944e-38
f32 = jnp.float32
bf16 = jnp.bfloat16


def split(value, axis, pieces):
    parts = []
    for _ in range(pieces):
        parts.append(value.astype(bf16))
        value = value - parts[-1].astype(f32)
    return jnp.concatenate(parts, axis=axis)


def indicator(mask, value=1.0):
    return jnp.where(mask, value, 0.0).astype(bf16)


def kernel(
    tiles,
    sects,
    subs,
    air_in,
    level_in,
    fuel_in,
    class_in,
    ign_in,
    plan_in,
    rate_in,
    burn_in,
    heat_in,
    moist_in,
    air_out,
    level_out,
    fuel_out,
    air_0,
    air_1,
    air_2,
    air_3,
    xh,
    xa,
    xb,
    rate,
    pace,
    fuel,
    binv,
    heat,
    moist,
    ign,
    bsum,
    stage,
    turned,
    gather,
    spread,
    wmat,
    smat,
    wnd,
    es,
    gs,
    hb,
    er,
    dg,
    wsend,
    wrecv,
    hrecv,
    fsend,
    frecv,
    grecv,
    plan,
    t_rate,
    t_burn,
    t_heat,
    t_moist,
    in_s,
    table_s,
    fire_s,
    fire_r,
    wind_s,
    wind_r,
    flux_s,
    flux_r,
    rim_s,
    rim_r,
    halo_s,
    halo_r,
):
    air = (air_0, air_1, air_2, air_3)
    bands = sects * subs
    depth = air_in.shape[1]
    width = air_in.shape[3]
    rows, cols = level_in.shape
    coarse = cols // REFINE
    groups = cols // 128
    tile_at = lax.axis_index("tile")
    sect_at = lax.axis_index("sect")
    sub_at = lax.axis_index("sub")
    band = sect_at * subs + sub_at
    not_first = tile_at > 0
    not_final = tile_at < tiles - 1
    band_low = band > 0
    band_high = band < bands - 1

    def device(tile_step, at_band):
        return {
            "tile": tile_at + tile_step,
            "sect": at_band // subs,
            "sub": at_band % subs,
        }

    def both(a, b):
        return jnp.logical_and(a, b)

    others = [
        (sect_at + a) % sects * subs + (sub_at + b) % subs
        for a in [*range(1, sects), 0]
        for b in range(subs)
        if a or b
    ]
    pending = []

    def send(condition, src, dst, send_sem, recv_sem, where):
        def make():
            return pltpu.make_async_remote_copy(
                src_ref=src,
                dst_ref=dst,
                send_sem=send_sem,
                recv_sem=recv_sem,
                device_id=where,
                device_id_type=MESH,
            )

        @pl.when(condition)
        def _():
            make().start()

        pending.append((condition, make))

    def drain():
        for condition, make in pending:
            if condition is None:
                make().wait_send()
                continue

            @pl.when(condition)
            def _(make=make):
                make().wait_send()

        pending.clear()

    def send_group(condition, parts, whole, send_sem, recv_sem, wheres):
        def make(src, dst, where):
            return pltpu.make_async_remote_copy(
                src_ref=src,
                dst_ref=dst,
                send_sem=send_sem,
                recv_sem=recv_sem,
                device_id=where,
                device_id_type=MESH,
            )

        @pl.when(condition)
        def _():
            for (src, dst), where in zip(parts, wheres):
                make(src, dst, where).start()

        pending.append((condition, lambda: make(whole, whole, wheres[0])))

    def send_tile(parts, whole, send_sem, recv_sem):
        def make(src, dst, j):
            return pltpu.make_async_remote_copy(
                src_ref=src,
                dst_ref=dst,
                send_sem=send_sem,
                recv_sem=recv_sem,
                device_id=device(0, j),
                device_id_type=MESH,
            )

        for j in others:
            make(*parts(j), j).start()

        pending.append((None, lambda: make(whole, whole, 0)))

    def receive_tile(whole, recv_sem, send_sem):
        pltpu.make_async_remote_copy(
            src_ref=whole,
            dst_ref=whole,
            send_sem=send_sem,
            recv_sem=recv_sem,
            device_id=device(0, 0),
            device_id_type=MESH,
        ).wait_recv()

    def receive(condition, dst, recv_sem, send_sem, where):
        @pl.when(condition)
        def _():
            pltpu.make_async_remote_copy(
                src_ref=dst,
                dst_ref=dst,
                send_sem=send_sem,
                recv_sem=recv_sem,
                device_id=where,
                device_id_type=MESH,
            ).wait_recv()

    def iota(shape, dim):
        return lax.broadcasted_iota(jnp.int32, shape, dim)

    barrier = pltpu.get_barrier_semaphore()
    for tile_step, condition in ((0, None), (-1, not_first), (1, not_final)):
        for j in range(bands):
            ok = (band != j) if condition is None else condition

            @pl.when(ok)
            def _(tile_step=tile_step, j=j):
                pl.semaphore_signal(
                    barrier, inc=1, device_id=device(tile_step, j), device_id_type=MESH
                )

    def fetch(array, held, slot):
        for v in range(groups):
            pltpu.make_async_copy(
                array.at[:, pl.ds(128 * v, 128)], held.at[v], in_s.at[slot]
            ).start()
        return pltpu.make_async_copy(held, held, in_s.at[slot])

    air_copy = pltpu.make_async_copy(air_in, air[0].at[:, pl.ds(1, depth)], in_s.at[3])
    air_copy.start()
    fire_copies = [
        fetch(class_in, turned.at[0], 0),
        fetch(ign_in, turned.at[1], 1),
        fetch(level_in, stage.at[0], 2),
    ]
    tables = [
        pltpu.make_async_copy(src, dst, table_s.at[k])
        for k, (src, dst) in enumerate(
            (
                (rate_in, t_rate),
                (plan_in, plan),
                (burn_in, t_burn),
                (heat_in, t_heat),
                (moist_in, t_moist),
            )
        )
    ]
    for copy in tables:
        copy.start()
    fuel_copy = fetch(fuel_in, stage.at[1], 4)

    spot = iota((16, cols), 1)
    spot = SEG * (spot % 128) + spot // 128
    line16 = iota((16, cols), 0)

    def make_gather(i, carry):
        at = pl.ds(pl.multiple_of(i * 16, 16), 16)
        gather[at, :] = indicator(spot == line16 + 16 * i)
        return carry

    lax.fori_loop(0, cols // 16, make_gather, 0, unroll=4)

    sub = iota((8, 128), 0)
    lane = iota((8, 128), 1)
    octet = lane // 8
    inner = lane % 8 < 4
    edge_w = sub == jnp.where(not_first, -1, 0)
    edge_e = sub == jnp.where(not_final, -1, 7)
    edge_s = lane == jnp.where(band_low, -1, 0)
    edge_n = lane == jnp.where(band_high, -1, 127)
    strip_w = both(edge_w, octet == 3)
    strip_e = both(edge_e, octet == 12)

    def rolled(value, shift, axis):
        shift = shift % value.shape[axis]
        return pltpu.roll(value, shift, axis) if shift else value

    row8 = iota((8, width), 0)
    total_col = sum(math.exp(-k / LEVELS) for k in range(LEVELS))
    total_prof = sum(math.exp(-2.0 * k / LEVELS) for k in range(LEVELS))
    col_base = f32(0.0)
    prof_base = f32(0.0)
    for j in range(bands):
        here = band == j
        col_base = jnp.where(here, f32(math.exp(-j * depth / LEVELS) / total_col), col_base)
        prof_base = jnp.where(
            here, f32(LEVELS * math.exp(-2.0 * j * depth / LEVELS) / total_prof), prof_base
        )
    col_ratio = math.exp(-1.0 / LEVELS)
    prof_ratio = math.exp(-2.0 / LEVELS)

    def send_wind(c, total_u, total_v):
        stacked = jnp.concatenate([total_u, total_v], axis=0)
        for j in range(bands):
            shift = (128 // 4 - coarse * j) % width
            window = (pltpu.roll(stacked, shift, 1) if shift else stacked)[:, :128]
            wsend[c, j, 0] = window[:8]
            wsend[c, j, 1] = window[8:]

            @pl.when(band == j)
            def _(window=window, j=j):
                wrecv[c, j, 0] = window[:8]
                wrecv[c, j, 1] = window[8:]

        send_tile(
            lambda j: (wsend.at[c, j], wrecv.at[c, band]),
            wsend.at[c, pl.ds(0, bands - 1)],
            wind_s.at[0],
            wind_r.at[c % 2],
        )
        for way, tile_step, ok in ((0, 1, not_final), (1, -1, not_first)):
            row, there = pl.ds(7 - 7 * way, 1), pl.ds(7 * way, 1)
            send_group(
                ok,
                [
                    (wsend.at[c, j, :, row, :], hrecv.at[c, band, :, there, :])
                    for j in range(bands)
                ],
                hrecv.at[c, :, :, there, :],
                rim_s.at[0, way],
                rim_r.at[c % 2, way],
                [device(tile_step, j) for j in range(bands)],
            )

    def wait_wind(c):
        receive_tile(wrecv.at[c, pl.ds(0, bands - 1)], wind_r.at[c % 2], wind_s.at[0])
        for way, tile_step, ok in ((0, -1, not_first), (1, 1, not_final)):
            receive(
                ok,
                hrecv.at[c, :, :, pl.ds(7 * way, 1), :],
                rim_r.at[c % 2, way],
                rim_s.at[0, way],
                device(tile_step, 0),
            )
        own, beyond = [], []
        for k in range(2):
            here, there = wrecv[c, 0, k], hrecv[c, 0, k]
            for j in range(1, bands):
                here, there = here + wrecv[c, j, k], there + hrecv[c, j, k]
            own.append(here)
            beyond.append(
                jnp.where(
                    sub < 4,
                    jnp.broadcast_to(there[:1], (8, 128)),
                    jnp.broadcast_to(there[7:], (8, 128)),
                )
            )
        together = jnp.concatenate(own + beyond, axis=0)
        wide = jnp.dot(split(together, 1, 2), wmat[...], preferred_element_type=f32)
        for k in range(2):
            own, beyond = wide[8 * k : 8 * k + 8], wide[16 + 8 * k : 24 + 8 * k]
            wnd[k, 0] = own[:, :128]
            wnd[k, 1] = beyond[:, :128]
            for at in (1, 2):
                here = own[:, 128 * at : 128 * at + 128]
                there = beyond[:, 128 * at : 128 * at + 128]
                below = jnp.where(sub == 0, there, pltpu.roll(here, 1, 0))
                above = jnp.where(sub == 7, there, pltpu.roll(here, 7, 0))
                wnd[k, at + 1] = jnp.where(
                    octet < 3, below, jnp.where(octet >= 13, above, here)
                )
            wnd[k, 4] = beyond[:, 384:]

    def portions(c):
        half = depth // 2
        return [(0, half), (half, depth - half)] if c == 0 else [(0, depth)]

    def send_air(c):
        send(
            band_high,
            air[c].at[:, depth],
            air[c].at[:, 0],
            halo_s.at[4],
            halo_r.at[c % 2, 4],
            device(0, band + 1),
        )
        send(
            band_low,
            air[c].at[:, 1],
            air[c].at[:, depth + 1],
            halo_s.at[5],
            halo_r.at[c % 2, 5],
            device(0, band - 1),
        )
        for piece, (start, count) in enumerate(portions(c)):
            send(
                not_final,
                air[c].at[:, pl.ds(1 + start, count), pl.ds(7, 1), :],
                xh.at[c, 0, :, pl.ds(start, count), pl.ds(7, 1), :],
                halo_s.at[2 * piece],
                halo_r.at[c % 2, 2 * piece],
                device(1, band),
            )
            send(
                not_first,
                air[c].at[:, pl.ds(1 + start, count), pl.ds(0, 1), :],
                xh.at[c, 1, :, pl.ds(start, count), pl.ds(0, 1), :],
                halo_s.at[2 * piece + 1],
                halo_r.at[c % 2, 2 * piece + 1],
                device(-1, band),
            )

    def wait_air(c, piece):
        start, count = portions(c)[piece]
        receive(
            not_first,
            xh.at[c, 0, :, pl.ds(start, count), pl.ds(7, 1), :],
            halo_r.at[c % 2, 2 * piece],
            halo_s.at[2 * piece],
            device(-1, band),
        )
        receive(
            not_final,
            xh.at[c, 1, :, pl.ds(start, count), pl.ds(0, 1), :],
            halo_r.at[c % 2, 2 * piece + 1],
            halo_s.at[2 * piece + 1],
            device(1, band),
        )
        if piece == 0:
            receive(
                band_low, air[c].at[:, 0], halo_r.at[c % 2, 4], halo_s.at[4], device(0, band - 1)
            )
            receive(
                band_high,
                air[c].at[:, depth + 1],
                halo_r.at[c % 2, 5],
                halo_s.at[5],
                device(0, band + 1),
            )

    nothing = jnp.zeros((8, width), f32)
    air_copy.wait()

    def first_air(i, carry):
        weight, total_u, total_v = carry
        total_u = total_u + weight * air[0][2, i + 1]
        total_v = total_v + weight * air[0][3, i + 1]
        return weight * f32(col_ratio), total_u, total_v

    _, total_u, total_v = lax.fori_loop(
        0, depth, first_air, (col_base, nothing, nothing), unroll=4
    )

    expected = (
        bands - 1 + bands * (not_first.astype(jnp.int32) + not_final.astype(jnp.int32))
    )
    pl.semaphore_wait(barrier, expected)

    send_air(0)
    send_wind(0, total_u, total_v)

    def reorder(load):
        return jnp.concatenate(
            [
                jnp.concatenate([load(v, pl.ds(q, 8, stride=REFINE)) for v in range(groups)], axis=1)
                for q in range(REFINE)
            ],
            axis=0,
        )

    for copy in fire_copies:
        copy.wait()
    tables[0].wait()
    kinds = reorder(
        lambda v, at: (turned[0, v, at, :] + 16 * turned[1, v, at, :]).astype(f32)
    ).astype(bf16)
    pieces = split(reorder(lambda v, at: stage[0, v, at, :]), 0, 3)
    found = jnp.dot(
        jnp.concatenate([pieces, kinds], axis=0), gather[...], preferred_element_type=f32
    )
    together = found[:rows] + found[rows : 2 * rows] + found[2 * rows : 3 * rows]
    kinds = found[3 * rows :]
    for q in range(REFINE):
        for p in range(SEG):
            kind = kinds[8 * q : 8 * q + 8, 128 * p : 128 * p + 128]
            when = jnp.floor(kind * (1.0 / 16.0))
            now = together[8 * q : 8 * q + 8, 128 * p : 128 * p + 128]
            ign[q, p] = when
            moist[q, p] = kind - 16.0 * when
            xa[q + 1, p] = jnp.where(when <= 0.0, jnp.minimum(now, -1.0), now)

    def find_rate(q, carry):
        for p in range(SEG):
            kind = moist[q, p]
            value = jnp.full((8, 128), t_rate[0], f32)
            for k in range(1, NFUEL):
                value = jnp.where(kind == float(k), t_rate[k], value)
            rate[q + 1, p] = value
        return carry

    lax.fori_loop(0, REFINE, find_rate, 0, unroll=2)

    def outline(e, ref):
        def edge(q, found):
            x = [ref[q + 1, p] for p in range(SEG)]
            near = pltpu.roll(x[SEG - 1], 1, 1)
            for k in range(1, DEEP):
                near = jnp.where(lane == k, pltpu.roll(x[SEG - 1 - k], k + 1, 1), near)
            for k in range(DEEP):
                near = jnp.where(lane == 127 - k, pltpu.roll(x[k], 127 - k, 1), near)
            return jnp.where(octet == q + 3, pltpu.roll(near, 8 * q + 28, 1), found)

        found = lax.fori_loop(0, REFINE, edge, jnp.zeros((8, 128), f32), unroll=10)
        es[e] = found
        gs[e, SEG] = jnp.where(
            sub < 4,
            jnp.broadcast_to(found[7:8], (8, 128)),
            jnp.broadcast_to(found[0:1], (8, 128)),
        )

        def border(p, carry):
            value = rolled(ref[REFINE, p], 1, 0)
            for k in range(1, DEEP):
                value = jnp.where(sub == k, rolled(ref[REFINE - k, p], k + 1, 0), value)
            for k in range(DEEP):
                value = jnp.where(sub == 4 + k, rolled(ref[DEEP - k, p], 4 + k, 0), value)
            gs[e, p] = value
            return carry

        lax.fori_loop(0, SEG, border, 0, unroll=5)

    def fields(c):
        return pl.ds(0, 2) if c == 0 else pl.ds(1 + c, 1)

    def send_outline(c):
        at = fields(c)
        for way, tile_step, ok in ((0, 1, not_final), (1, -1, not_first)):
            part = pl.ds(4 * way, 4)
            send(
                ok,
                gs.at[at, :, part, :],
                hb.at[at, :, part, :],
                fire_s.at[way],
                fire_r.at[c % 2, way],
                device(tile_step, band),
            )
        for side, band_step, ok in ((0, 1, band_high), (1, -1, band_low)):
            send(
                ok,
                es.at[at],
                er.at[at, side],
                fire_s.at[2 + side],
                fire_r.at[c % 2, 2 + side],
                device(0, band + band_step),
            )
            for way, tile_step, also in ((0, 1, not_final), (1, -1, not_first)):
                send(
                    both(ok, also),
                    es.at[at, pl.ds(7 - 7 * way, 1), :],
                    dg.at[at, side, pl.ds(7 * way, 1), :],
                    fire_s.at[4 + 2 * side + way],
                    fire_r.at[c % 2, 4 + 2 * side + way],
                    device(tile_step, band + band_step),
                )

    def wait_outline(c):
        at = fields(c)
        for way, tile_step, ok in ((0, -1, not_first), (1, 1, not_final)):
            receive(
                ok,
                hb.at[at, :, pl.ds(4 * way, 4), :],
                fire_r.at[c % 2, way],
                fire_s.at[way],
                device(tile_step, band),
            )
        for side, band_step, ok in ((0, -1, band_low), (1, 1, band_high)):
            receive(
                ok,
                er.at[at, side],
                fire_r.at[c % 2, 2 + side],
                fire_s.at[2 + side],
                device(0, band + band_step),
            )
            for way, tile_step, also in ((0, -1, not_first), (1, 1, not_final)):
                receive(
                    both(ok, also),
                    dg.at[at, side, pl.ds(7 * way, 1), :],
                    fire_r.at[c % 2, 4 + 2 * side + way],
                    fire_s.at[4 + 2 * side + way],
                    device(tile_step, band + band_step),
                )

    def surround(e, ref):
        for p in range(SEG):
            ref[12, p] = hb[e, p]
        mine, beyond = es[e], hb[e, SEG]

        def strip(here, there):
            below = jnp.where(sub == 0, there, pltpu.roll(here, 1, 0))
            above = jnp.where(sub == 7, there, pltpu.roll(here, 7, 0))
            return jnp.where(
                octet < 3,
                pltpu.roll(below, 48, 1),
                jnp.where(octet >= 13, pltpu.roll(above, 80, 1), here),
            )

        low = strip(jnp.where(inner, mine, er[e, 0]), jnp.where(inner, beyond, dg[e, 0]))
        high = strip(jnp.where(inner, er[e, 1], mine), jnp.where(inner, dg[e, 1], beyond))
        mixed = jnp.where(inner, high, low)
        corner = mixed
        for k in range(3):
            corner = jnp.where(sub == k, rolled(rolled(mixed, 108 + 8 * k, 1), k, 0), corner)
            corner = jnp.where(sub == 7 - k, rolled(rolled(mixed, 20 - 8 * k, 1), -k, 0), corner)
        ref[13, 0] = low
        ref[13, 1] = high
        ref[13, 2] = corner

    outline(0, rate)
    outline(1, xa)
    send_outline(0)

    @pl.when(jnp.logical_not(not_first))
    def _():
        def zero(i, carry):
            for c in range(STEPS):
                for f in range(4):
                    xh[c, 0, f, i] = jnp.zeros((8, width), f32)
            return carry

        lax.fori_loop(0, depth, zero, 0)
        grecv[:, :, :, 7:] = jnp.zeros((STEPS - 1, bands, 2, 1, 128), f32)

    @pl.when(jnp.logical_not(not_final))
    def _():
        grecv[:, :, :, :1] = jnp.zeros((STEPS - 1, bands, 2, 1, 128), f32)

        def zero(i, carry):
            for c in range(STEPS):
                for f in range(4):
                    xh[c, 1, f, i] = jnp.zeros((8, width), f32)
            return carry

        lax.fori_loop(0, depth, zero, 0)

    @pl.when(jnp.logical_not(band_low))
    def _():
        for c in range(STEPS):
            air[c][:, 0] = jnp.zeros((4, 8, width), f32)

    @pl.when(jnp.logical_not(band_high))
    def _():
        for c in range(STEPS):
            air[c][:, depth + 1] = jnp.zeros((4, 8, width), f32)

    column = iota((16, cols), 1)

    def make_spread(i, carry):
        at = pl.ds(pl.multiple_of(i * 16, 16), 16)
        spread[at, :] = indicator(column == SEG * (line16 + 16 * (i % 8)) + i // 8)
        return carry

    source, place = iota((128, 512), 0), iota((128, 512), 1)
    block, place = place // 128, place % 128
    near = place % 8 < 4
    first = jnp.where(block == 0, 32 + place // 2, jnp.where(near, 32, 31))
    second = jnp.where(
        block == 2, jnp.where(near, 96, 95), jnp.where(place < 64, 31, 96)
    )
    pattern = indicator(source == jnp.where(block < 2, first, second), 0.5)
    wmat[:128, :] = pattern
    wmat[128:, :] = pattern
    source, place = iota((128, 128), 0), iota((128, 128), 1)
    pattern = indicator(place == source // 2 + coarse * (band % 2))
    smat[:128, :] = pattern
    smat[128:, :] = pattern

    for copy in tables[1:]:
        copy.wait()

    def lookup(q, carry):
        for p in range(SEG):
            kind = moist[q, p]
            burn = jnp.full((8, 128), t_burn[0], f32)
            hot = jnp.full((8, 128), t_heat[0], f32)
            wet = jnp.full((8, 128), t_moist[0], f32)
            for k in range(1, NFUEL):
                same = kind == float(k)
                burn = jnp.where(same, t_burn[k], burn)
                hot = jnp.where(same, t_heat[k], hot)
                wet = jnp.where(same, t_moist[k], wet)
            binv[q, p] = 1.0 / burn
            heat[q, p] = hot
            moist[q, p] = wet
            bsum[q, p] = jnp.zeros((8, 128), f32)
        return carry

    lax.fori_loop(0, REFINE, lookup, 0)
    fuel_copy.wait()
    pieces = split(reorder(lambda v, at: stage[1, v, at, :]), 0, 3)
    found = jnp.dot(pieces, gather[...], preferred_element_type=f32)
    together = found[:rows] + found[rows : 2 * rows] + found[2 * rows :]
    for q in range(REFINE):
        for p in range(SEG):
            fuel[q, p] = together[8 * q : 8 * q + 8, 128 * p : 128 * p + 128]
    lax.fori_loop(0, cols // 16, make_spread, 0, unroll=4)

    def uphill(d):
        return jnp.maximum(d, 0.0) * d

    def downhill(d):
        return jnp.minimum(d, 0.0) * d

    def moved(here, dw, de, ds, dn, speed, wu, wv):
        square = (uphill(dw) + downhill(de)) + (uphill(ds) + downhill(dn))
        steep = square * lax.rsqrt(jnp.maximum(square, TINY))
        gx, gy = dw + de, ds + dn
        tail = (wu * gx + wv * gy) * lax.rsqrt(gx * gx + gy * gy + 4.0)
        return here - (speed * (1.0 + jnp.maximum(tail, 0.0))) * steep

    def substep(src, dst, fire_step):
        low, high, corner = src[13, 0], src[13, 1], src[13, 2]
        mixed = jnp.where(inner, high, low)
        top, border, bottom = [], [], []
        for p in range(SEG):
            first, final, beyond = src[1, p], src[REFINE, p], src[12, p]
            border.append(beyond)
            top.append(
                jnp.where(
                    edge_w, first, jnp.where(sub == 0, beyond, pltpu.roll(final, 1, 0))
                )
            )
            src[11, p] = jnp.where(
                edge_e, final, jnp.where(sub == 7, beyond, pltpu.roll(first, 7, 0))
            )

        def across(x, outer):
            south = jnp.where(lane == 0, outer, pltpu.roll(x[SEG - 1], 1, 1))
            north = jnp.where(lane == 127, outer, pltpu.roll(x[0], 127, 1))
            south = jnp.where(edge_s, x[0], south)
            north = jnp.where(edge_n, x[SEG - 1], north)
            line = [south] + x + [north]
            return [line[k + 1] - line[k] for k in range(SEG + 1)]

        wu, wv = wnd[0, 0], wnd[1, 0]

        def line(q, carry):
            x, dw = carry
            after = [src[q + 2, p] for p in range(SEG)]
            dh = across(x, pltpu.roll(mixed, 100 - 8 * q, 1))
            de = []
            for p in range(SEG):
                de.append(after[p] - x[p])
                new = moved(
                    x[p], dw[p], de[p], dh[p], dh[p + 1], pace[q + 1, p], wu, wv
                )
                dst[q + 1, p] = new
                bsum[q, p] = bsum[q, p] + jnp.clip(new, -0.5, 0.5)
            return after, de

        x = [src[1, p] for p in range(SEG)]
        lax.fori_loop(0, REFINE, line, (x, [x[p] - top[p] for p in range(SEG)]), unroll=10)

        wu, wv = wnd[0, 1], wnd[1, 1]
        dh = across(border, corner)
        for p in range(SEG):
            here = border[p]
            west = jnp.where(sub == 7, src[REFINE, p], pltpu.roll(here, 7, 0))
            east = jnp.where(sub == 0, src[1, p], pltpu.roll(here, 1, 0))
            dst[12, p] = moved(
                here, here - west, east - here, dh[p], dh[p + 1], pace[12, p], wu, wv
            )
        for k, here in enumerate((low, high)):
            west = jnp.where(strip_w, here, pltpu.roll(here, 8, 1))
            east = jnp.where(strip_e, here, pltpu.roll(here, 120, 1))
            south, north = pltpu.roll(here, 127, 1), pltpu.roll(here, 1, 1)
            dst[13, k] = moved(
                here,
                here - west,
                east - here,
                here - south,
                north - here,
                pace[13, k],
                wnd[0, 2 + k],
                wnd[1, 2 + k],
            )
        west = jnp.where(sub == 7, pltpu.roll(mixed, 28, 1), pltpu.roll(corner, 7, 0))
        east = jnp.where(sub == 0, pltpu.roll(mixed, 100, 1), pltpu.roll(corner, 1, 0))
        south = jnp.where(lane == 127, border[SEG - 1], pltpu.roll(corner, 127, 1))
        north = jnp.where(lane == 0, border[0], pltpu.roll(corner, 1, 1))
        dst[13, 2] = moved(
            corner,
            corner - west,
            east - corner,
            corner - south,
            north - corner,
            pace[13, 2],
            wnd[0, 4],
            wnd[1, 4],
        )

    lane_a = lax.broadcasted_iota(jnp.int32, (8, width), 1)

    def write(c, f, i, value):
        if c == STEPS - 1:
            air_out[f, i] = value
        else:
            air[c + 1][f, i + 1] = value

    def wait_flux(c):
        receive_tile(frecv.at[c, pl.ds(0, bands - 1)], flux_r.at[c % 2], flux_s.at[0])
        return [
            jnp.concatenate(
                [frecv[c, 2 * k, f] + frecv[c, 2 * k + 1, f] for k in range(width // 128)],
                axis=1,
            )
            for f in range(2)
        ]

    def wait_rim(c):
        for way, tile_step, ok in ((0, -1, not_first), (1, 1, not_final)):
            row = pl.ds(7 - 7 * way, 1)
            receive(
                ok,
                grecv.at[c, :, :, row, :],
                rim_r.at[2 + c % 2, way],
                rim_s.at[1, way],
                device(tile_step, 0),
            )
        return [
            jnp.concatenate(
                [grecv[c, 2 * k, f] + grecv[c, 2 * k + 1, f] for k in range(width // 128)],
                axis=1,
            )
            for f in range(2)
        ]

    def force_air(c, flux):
        def force(i, weight):
            for f in range(2):
                now = air_out[f, i] if c == STEPS - 1 else air[c + 1][f, i + 1]
                write(c, f, i, now + weight * flux[f])
            return weight * f32(prof_ratio)

        lax.fori_loop(0, depth, force, prof_base * f32(2.0), unroll=20)

    def move_air(c):
        if c < STEPS - 1:
            drain()
        if c > 0:
            flux = wait_flux(c - 1)
            force_air(c - 1, flux)
        wait_air(c, 0)
        if c > 0:
            low = jnp.where(band_low, prof_base * f32(2.0 / prof_ratio), 0.0)
            high = jnp.where(band_high, prof_base * f32(2.0 * prof_ratio**depth), 0.0)
            for f in range(2):
                air[c][f, 0] = air[c][f, 0] + low * flux[f]
                air[c][f, depth + 1] = air[c][f, depth + 1] + high * flux[f]
        final = c == STEPS - 1

        def update(i, carry):
            weight, total_u, total_v = carry
            u, v = air[c][2, i + 1], air[c][3, i + 1]
            to_w = 0.02 + 0.1 * jnp.maximum(u, 0.0)
            to_e = 0.02 - 0.1 * jnp.minimum(u, 0.0)
            to_s = 0.02 + 0.1 * jnp.maximum(v, 0.0)
            to_n = 0.02 - 0.1 * jnp.minimum(v, 0.0)
            to_here = 0.96 - ((to_w + to_e) + (to_s + to_n))
            to_s = jnp.where(lane_a == 0, 0.0, to_s)
            to_n = jnp.where(lane_a == width - 1, 0.0, to_n)
            lift_x = lift_s = lift_n = None
            for f in range(4):
                here = air[c][f, i + 1]
                west, east = xh[c, 0, f, i], xh[c, 1, f, i]
                west = pltpu.roll(jnp.where(row8 == 7, west, here), 1, 0)
                east = pltpu.roll(jnp.where(row8 == 0, east, here), 7, 0)
                south, north = pltpu.roll(here, 1, 1), pltpu.roll(here, width - 1, 1)
                new = (to_here * here + (to_w * west + to_e * east)) + (
                    (to_s * south + to_n * north) + 0.02 * (air[c][f, i] + air[c][f, i + 2])
                )
                if f == 0:
                    lift_x, lift_s, lift_n = east - west, south, north
                elif f == 1:
                    lift_x = lift_x + 0.6 * (east - west)
                    lift_s = jnp.where(lane_a == 0, 0.0, lift_s + 0.6 * south)
                    lift_n = jnp.where(lane_a == width - 1, 0.0, lift_n + 0.6 * north)
                elif f == 2:
                    new = new + 0.015 * lift_x
                    total_u = total_u + weight * new
                else:
                    new = new + 0.015 * (lift_n - lift_s)
                    total_v = total_v + weight * new
                write(c, f, i, new)
            return weight * f32(col_ratio), total_u, total_v

        carry = (col_base, nothing, nothing)
        for piece, (start, count) in enumerate(portions(c)):
            if piece > 0:
                wait_air(c, piece)
            carry = lax.fori_loop(start, start + count, update, carry, unroll=count)
        _, total_u, total_v = carry
        if c > 0:
            rim = wait_rim(c - 1)
            west = [jnp.where(row8 == 0, pltpu.roll(rim[f], 1, 0), 0.0) for f in range(2)]
            east = [jnp.where(row8 == 7, pltpu.roll(rim[f], 7, 0), 0.0) for f in range(2)]
            push = 0.015 * ((east[0] - west[0]) + 0.6 * (east[1] - west[1]))

            def border(i, carry):
                weight, share, total_u = carry
                u = air[c][2, i + 1]
                to_w = share * (0.02 + 0.1 * jnp.maximum(u, 0.0))
                to_e = share * (0.02 - 0.1 * jnp.minimum(u, 0.0))
                for f in range(2):
                    now = air_out[f, i] if final else air[c + 1][f, i + 1]
                    write(c, f, i, now + (to_w * west[f] + to_e * east[f]))
                more = share * push
                now = air_out[2, i] if final else air[c + 1][2, i + 1]
                write(c, 2, i, now + more)
                return weight * f32(col_ratio), share * f32(prof_ratio), total_u + weight * more

            _, _, total_u = lax.fori_loop(
                0, depth, border, (col_base, prof_base * f32(2.0), total_u), unroll=20
            )
        if not final:
            send_wind(c + 1, total_u, total_v)
            send_air(c + 1)

    def send_rim(c):
        for way, tile_step, ok in ((0, 1, not_final), (1, -1, not_first)):
            row = pl.ds(7 - 7 * way, 1)
            send_group(
                ok,
                [(fsend.at[c, :, row, :], grecv.at[c, band, :, row, :]) for j in range(bands)],
                grecv.at[c, :, :, row, :],
                rim_s.at[1, way],
                rim_r.at[2 + c % 2, way],
                [device(tile_step, j) for j in range(bands)],
            )

    def burn_fire(c, fire_step):
        def burn(q, carry):
            hot, wet = carry
            for p in range(SEG):
                now = fuel[q, p]
                spent = (float(SUBSTEPS) * 0.5 - bsum[q, p]) * binv[q, p]
                remain = now * jnp.exp(-fire_step * spent)
                used = now - remain
                fuel[q, p] = remain
                bsum[q, p] = jnp.zeros((8, 128), f32)
                hot = hot + used * heat[q, p]
                wet = wet + used * moist[q, p]
            return hot, wet

        zero = jnp.zeros((8, 128), f32)
        hot, wet = lax.fori_loop(0, REFINE, burn, (zero, zero), unroll=10)
        flux = jnp.dot(
            split(jnp.concatenate([hot, wet], axis=0), 1, 2),
            smat[...],
            preferred_element_type=f32,
        ) * f32(1.0 / (REFINE * REFINE))
        fsend[c, 0] = flux[:8]
        fsend[c, 1] = flux[8:]
        for j in range(bands):

            @pl.when(band == j)
            def _(j=j):
                frecv[c, j, 0] = flux[:8]
                frecv[c, j, 1] = flux[8:]

        send_tile(
            lambda j: (fsend.at[c], frecv.at[c, band]),
            frecv.at[c, pl.ds(0, bands - 1)],
            flux_s.at[0],
            flux_r.at[c % 2],
        )
        if c < STEPS - 1:
            send_rim(c)

    def burn_window(c):
        fire_step = plan[c].astype(f32) * f32(0.15)
        if c == STEPS - 1:
            drain()
        wait_outline(c)
        if c == 0:
            surround(0, rate)
        surround(1 + c, xa)

        for q in range(1, REFINE + 1):
            for p in range(SEG):
                pace[q, p] = fire_step * rate[q, p]
        for p in range(SEG):
            pace[12, p] = fire_step * rate[12, p]
        for k in range(3):
            pace[13, k] = fire_step * rate[13, k]

        def pair(i, carry):
            substep(xa, xb, fire_step)
            substep(xb, xa, fire_step)
            return carry

        lax.fori_loop(0, SUBSTEPS // 2, pair, 0)
        if c != STEPS - 2:
            burn_fire(c, fire_step)
        if c < STEPS - 1:

            def ignite(q, carry):
                for p in range(SEG):
                    now = xa[q + 1, p]
                    xa[q + 1, p] = jnp.where(
                        ign[q, p] <= float(c + 1), jnp.minimum(now, -1.0), now
                    )
                return carry

            lax.fori_loop(0, REFINE, ignite, 0, unroll=10)
            outline(2 + c, xa)
            send_outline(1 + c)
            if c == STEPS - 2:
                burn_fire(c, fire_step)
            wait_wind(c + 1)

    def give(load, array):
        values = jnp.concatenate(
            [
                jnp.concatenate([load(q, p) for p in range(SEG)], axis=1)
                for q in range(REFINE)
            ],
            axis=0,
        )
        found = jnp.dot(split(values, 0, 3), spread[...], preferred_element_type=f32)
        found = found[:rows] + found[rows : 2 * rows] + found[2 * rows :]
        for q in range(REFINE):
            for v in range(groups):
                array[v, pl.ds(q, 8, stride=REFINE), :] = found[
                    8 * q : 8 * q + 8, 128 * v : 128 * v + 128
                ]

    move_air(0)
    wait_wind(0)
    burn_window(0)
    for c in range(1, STEPS - 1):
        move_air(c)
        burn_window(c)
    burn_window(STEPS - 1)
    give(lambda q, p: xa[q + 1, p], level_out)
    move_air(STEPS - 1)
    give(lambda q, p: fuel[q, p], fuel_out)
    drain()
    force_air(STEPS - 1, wait_flux(STEPS - 1))


def release(air, level, fuel, air_out, level_out, fuel_out, sems):
    for f in range(4):
        pltpu.make_async_copy(air.at[f], air_out.at[f], sems.at[0]).start()
    copies = [pltpu.make_async_copy(air, air, sems.at[0])]
    for k, (held, out) in enumerate(((level, level_out), (fuel, fuel_out))):
        for v in range(held.shape[0]):
            pltpu.make_async_copy(
                held.at[v], out.at[:, pl.ds(128 * v, 128)], sems.at[1 + k]
            ).start()
        copies.append(pltpu.make_async_copy(held, held, sems.at[1 + k]))
    for copy in copies:
        copy.wait()


def solution(mesh):
    tiles, sects, subs = (mesh.shape[name] for name in ("tile", "sect", "sub"))
    bands = sects * subs
    air_spec = P(None, ("sect", "sub"), ("group", "tile"), None)
    fire_spec = P(("group", "tile"), ("sect", "sub"))

    def local(air_state, fire_level, *rest):
        depth, width = air_state.shape[1], air_state.shape[3]
        rows, cols = fire_level.shape
        groups = cols // 128
        assert air_state.shape[2] == 8 and cols == 64 * REFINE and rows == 8 * REFINE
        vmem = pl.BlockSpec(memory_space=pltpu.VMEM)
        hbm = pl.BlockSpec(memory_space=pltpu.HBM)
        dma = pltpu.SemaphoreType.DMA

        def blocks(*lead):
            return pltpu.VMEM((*lead, 8, 128), f32)

        held = pl.pallas_call(
            functools.partial(kernel, tiles, sects, subs),
            out_shape=(
                pltpu.VMEM(air_state.shape, f32),
                pltpu.VMEM((groups, rows, 128), f32),
                pltpu.VMEM((groups, rows, 128), f32),
            ),
            in_specs=[hbm] * 10,
            out_specs=(vmem, vmem, vmem),
            scratch_shapes=[
                pltpu.VMEM((4, depth + 2, 8, width), f32),
                pltpu.VMEM((4, depth + 2, 8, width), f32),
                pltpu.VMEM((4, depth + 2, 8, width), f32),
                pltpu.VMEM((4, depth + 2, 8, width), f32),
                pltpu.VMEM((STEPS, 2, 4, depth, 8, width), f32),
                blocks(14, SEG),
                blocks(14, SEG),
                blocks(14, SEG),
                blocks(14, SEG),
                blocks(REFINE, SEG),
                blocks(REFINE, SEG),
                blocks(REFINE, SEG),
                blocks(REFINE, SEG),
                blocks(REFINE, SEG),
                blocks(REFINE, SEG),
                pltpu.VMEM((2, groups, rows, 128), f32),
                pltpu.VMEM((2, groups, rows, 128), jnp.int32),
                pltpu.VMEM((cols, cols), bf16),
                pltpu.VMEM((cols, cols), bf16),
                pltpu.VMEM((256, 512), bf16),
                pltpu.VMEM((256, 128), bf16),
                blocks(2, 5),
                blocks(STEPS + 1),
                blocks(STEPS + 1, SEG + 1),
                blocks(STEPS + 1, SEG + 1),
                blocks(STEPS + 1, 2),
                blocks(STEPS + 1, 2),
                blocks(STEPS, bands, 2),
                blocks(STEPS, bands, 2),
                blocks(STEPS, bands, 2),
                blocks(STEPS, 2),
                blocks(STEPS, bands, 2),
                blocks(STEPS - 1, bands, 2),
                pltpu.SMEM((STEPS,), jnp.int32),
                pltpu.SMEM((NFUEL,), f32),
                pltpu.SMEM((NFUEL,), f32),
                pltpu.SMEM((NFUEL,), f32),
                pltpu.SMEM((NFUEL,), f32),
                dma((5,)),
                dma((5,)),
                dma((8,)),
                dma((2, 8)),
                dma((1,)),
                dma((2,)),
                dma((1,)),
                dma((2,)),
                dma((2, 2)),
                dma((4, 2)),
                dma((6,)),
                dma((2, 6)),
            ],
            compiler_params=pltpu.CompilerParams(
                collective_id=0, has_side_effects=True, vmem_limit_bytes=56 * 1024 * 1024
            ),
        )(air_state, fire_level, *rest)
        held = [pltpu.with_memory_space_constraint(x, pltpu.VMEM) for x in held]
        return pl.pallas_call(
            release,
            out_shape=(
                jax.ShapeDtypeStruct(air_state.shape, f32),
                jax.ShapeDtypeStruct(fire_level.shape, f32),
                jax.ShapeDtypeStruct(fire_level.shape, f32),
            ),
            in_specs=[vmem] * 3,
            out_specs=(hbm, hbm, hbm),
            scratch_shapes=[dma((3,))],
        )(*held)

    return jax.shard_map(
        local,
        mesh=mesh,
        in_specs=(air_spec, fire_spec, fire_spec, fire_spec, fire_spec) + (P(),) * 5,
        out_specs=(air_spec, fire_spec, fire_spec),
        check_vma=False,
    )
```

```python
import functools
import math

import jax
import jax.numpy as jnp
from jax import lax
from jax.experimental import pallas as pl
from jax.experimental.pallas import tpu as pltpu
from jax.sharding import PartitionSpec as P

LEVELS = 80
REFINE = 10
NFUEL = 13
STEPS = 4
SUBSTEPS = 4
DEEP = 4
SEG = REFINE // 2
MESH = pl.DeviceIdType.MESH
TINY = 1.1754944e-38
f32 = jnp.float32
bf16 = jnp.bfloat16


def split(value, axis, pieces):
    parts = []
    for _ in range(pieces):
        parts.append(value.astype(bf16))
        value = value - parts[-1].astype(f32)
    return jnp.concatenate(parts, axis=axis)


def indicator(mask, value=1.0):
    return jnp.where(mask, value, 0.0).astype(bf16)


def kernel(
    tiles,
    sects,
    subs,
    air_in,
    level_in,
    fuel_in,
    class_in,
    ign_in,
    plan_in,
    rate_in,
    burn_in,
    heat_in,
    moist_in,
    air_out,
    level_out,
    fuel_out,
    air_0,
    air_1,
    air_2,
    air_3,
    xh,
    xa,
    xb,
    rate,
    pace,
    fuel,
    binv,
    heat,
    moist,
    ign,
    bsum,
    stage,
    turned,
    gather,
    spread,
    wmat,
    smat,
    wnd,
    es,
    gs,
    hb,
    er,
    dg,
    wsend,
    wrecv,
    hrecv,
    fsend,
    frecv,
    grecv,
    plan,
    t_rate,
    t_burn,
    t_heat,
    t_moist,
    in_s,
    table_s,
    fire_s,
    fire_r,
    wind_s,
    wind_r,
    flux_s,
    flux_r,
    rim_s,
    rim_r,
    halo_s,
    halo_r,
):
    air = (air_0, air_1, air_2, air_3)
    bands = sects * subs
    depth = air_in.shape[1]
    width = air_in.shape[3]
    rows, cols = level_in.shape
    coarse = cols // REFINE
    groups = cols // 128
    tile_at = lax.axis_index("tile")
    sect_at = lax.axis_index("sect")
    sub_at = lax.axis_index("sub")
    band = sect_at * subs + sub_at
    not_first = tile_at > 0
    not_final = tile_at < tiles - 1
    band_low = band > 0
    band_high = band < bands - 1

    def device(tile_step, at_band):
        return {
            "tile": tile_at + tile_step,
            "sect": at_band // subs,
            "sub": at_band % subs,
        }

    def both(a, b):
        return jnp.logical_and(a, b)

    others = [
        (sect_at + a) % sects * subs + (sub_at + b) % subs
        for a in [*range(1, sects), 0]
        for b in range(subs)
        if a or b
    ]
    pending = []

    def send(condition, src, dst, send_sem, recv_sem, where):
        def make():
            return pltpu.make_async_remote_copy(
                src_ref=src,
                dst_ref=dst,
                send_sem=send_sem,
                recv_sem=recv_sem,
                device_id=where,
                device_id_type=MESH,
            )

        @pl.when(condition)
        def _():
            make().start()

        pending.append((condition, make))

    def drain():
        for condition, make in pending:
            if condition is None:
                make().wait_send()
                continue

            @pl.when(condition)
            def _(make=make):
                make().wait_send()

        pending.clear()

    def send_group(condition, parts, whole, send_sem, recv_sem, wheres):
        def make(src, dst, where):
            return pltpu.make_async_remote_copy(
                src_ref=src,
                dst_ref=dst,
                send_sem=send_sem,
                recv_sem=recv_sem,
                device_id=where,
                device_id_type=MESH,
            )

        @pl.when(condition)
        def _():
            for (src, dst), where in zip(parts, wheres):
                make(src, dst, where).start()

        pending.append((condition, lambda: make(whole, whole, wheres[0])))

    def send_tile(parts, whole, send_sem, recv_sem):
        def make(src, dst, j):
            return pltpu.make_async_remote_copy(
                src_ref=src,
                dst_ref=dst,
                send_sem=send_sem,
                recv_sem=recv_sem,
                device_id=device(0, j),
                device_id_type=MESH,
            )

        for j in others:
            make(*parts(j), j).start()

        pending.append((None, lambda: make(whole, whole, 0)))

    def receive_tile(whole, recv_sem, send_sem):
        pltpu.make_async_remote_copy(
            src_ref=whole,
            dst_ref=whole,
            send_sem=send_sem,
            recv_sem=recv_sem,
            device_id=device(0, 0),
            device_id_type=MESH,
        ).wait_recv()

    def receive(condition, dst, recv_sem, send_sem, where):
        @pl.when(condition)
        def _():
            pltpu.make_async_remote_copy(
                src_ref=dst,
                dst_ref=dst,
                send_sem=send_sem,
                recv_sem=recv_sem,
                device_id=where,
                device_id_type=MESH,
            ).wait_recv()

    def iota(shape, dim):
        return lax.broadcasted_iota(jnp.int32, shape, dim)

    barrier = pltpu.get_barrier_semaphore()
    for tile_step, condition in ((0, None), (-1, not_first), (1, not_final)):
        for j in range(bands):
            ok = (band != j) if condition is None else condition

            @pl.when(ok)
            def _(tile_step=tile_step, j=j):
                pl.semaphore_signal(
                    barrier, inc=1, device_id=device(tile_step, j), device_id_type=MESH
                )

    def fetch(array, held, slot):
        for v in range(groups):
            pltpu.make_async_copy(
                array.at[:, pl.ds(128 * v, 128)], held.at[v], in_s.at[slot]
            ).start()
        return pltpu.make_async_copy(held, held, in_s.at[slot])

    air_copy = pltpu.make_async_copy(air_in, air[0].at[:, pl.ds(1, depth)], in_s.at[3])
    air_copy.start()
    fire_copies = [
        fetch(class_in, turned.at[0], 0),
        fetch(ign_in, turned.at[1], 1),
        fetch(level_in, stage.at[0], 2),
    ]
    tables = [
        pltpu.make_async_copy(src, dst, table_s.at[k])
        for k, (src, dst) in enumerate(
            (
                (rate_in, t_rate),
                (plan_in, plan),
                (burn_in, t_burn),
                (heat_in, t_heat),
                (moist_in, t_moist),
            )
        )
    ]
    for copy in tables:
        copy.start()
    fuel_copy = fetch(fuel_in, stage.at[1], 4)

    spot = iota((16, cols), 1)
    spot = SEG * (spot % 128) + spot // 128
    line16 = iota((16, cols), 0)

    def make_gather(i, carry):
        at = pl.ds(pl.multiple_of(i * 16, 16), 16)
        gather[at, :] = indicator(spot == line16 + 16 * i)
        return carry

    lax.fori_loop(0, cols // 16, make_gather, 0, unroll=4)

    sub = iota((8, 128), 0)
    lane = iota((8, 128), 1)
    octet = lane // 8
    inner = lane % 8 < 4
    edge_w = sub == jnp.where(not_first, -1, 0)
    edge_e = sub == jnp.where(not_final, -1, 7)
    edge_s = lane == jnp.where(band_low, -1, 0)
    edge_n = lane == jnp.where(band_high, -1, 127)
    strip_w = both(edge_w, octet == 3)
    strip_e = both(edge_e, octet == 12)

    def rolled(value, shift, axis):
        shift = shift % value.shape[axis]
        return pltpu.roll(value, shift, axis) if shift else value

    row8 = iota((8, width), 0)
    total_col = sum(math.exp(-k / LEVELS) for k in range(LEVELS))
    total_prof = sum(math.exp(-2.0 * k / LEVELS) for k in range(LEVELS))
    col_base = f32(0.0)
    prof_base = f32(0.0)
    for j in range(bands):
        here = band == j
        col_base = jnp.where(here, f32(math.exp(-j * depth / LEVELS) / total_col), col_base)
        prof_base = jnp.where(
            here, f32(LEVELS * math.exp(-2.0 * j * depth / LEVELS) / total_prof), prof_base
        )
    col_ratio = math.exp(-1.0 / LEVELS)
    prof_ratio = math.exp(-2.0 / LEVELS)

    def send_wind(c, total_u, total_v):
        stacked = jnp.concatenate([total_u, total_v], axis=0)
        for j in range(bands):
            shift = (128 // 4 - coarse * j) % width
            window = (pltpu.roll(stacked, shift, 1) if shift else stacked)[:, :128]
            wsend[c, j, 0] = window[:8]
            wsend[c, j, 1] = window[8:]

            @pl.when(band == j)
            def _(window=window, j=j):
                wrecv[c, j, 0] = window[:8]
                wrecv[c, j, 1] = window[8:]

        send_tile(
            lambda j: (wsend.at[c, j], wrecv.at[c, band]),
            wsend.at[c, pl.ds(0, bands - 1)],
            wind_s.at[0],
            wind_r.at[c % 2],
        )
        for way, tile_step, ok in ((0, 1, not_final), (1, -1, not_first)):
            row, there = pl.ds(7 - 7 * way, 1), pl.ds(7 * way, 1)
            send_group(
                ok,
                [
                    (wsend.at[c, j, :, row, :], hrecv.at[c, band, :, there, :])
                    for j in range(bands)
                ],
                hrecv.at[c, :, :, there, :],
                rim_s.at[0, way],
                rim_r.at[c % 2, way],
                [device(tile_step, j) for j in range(bands)],
            )

    def wait_wind(c):
        receive_tile(wrecv.at[c, pl.ds(0, bands - 1)], wind_r.at[c % 2], wind_s.at[0])
        for way, tile_step, ok in ((0, -1, not_first), (1, 1, not_final)):
            receive(
                ok,
                hrecv.at[c, :, :, pl.ds(7 * way, 1), :],
                rim_r.at[c % 2, way],
                rim_s.at[0, way],
                device(tile_step, 0),
            )
        own, beyond = [], []
        for k in range(2):
            here, there = wrecv[c, 0, k], hrecv[c, 0, k]
            for j in range(1, bands):
                here, there = here + wrecv[c, j, k], there + hrecv[c, j, k]
            own.append(here)
            beyond.append(
                jnp.where(
                    sub < 4,
                    jnp.broadcast_to(there[:1], (8, 128)),
                    jnp.broadcast_to(there[7:], (8, 128)),
                )
            )
        together = jnp.concatenate(own + beyond, axis=0)
        wide = jnp.dot(split(together, 1, 2), wmat[...], preferred_element_type=f32)
        for k in range(2):
            own, beyond = wide[8 * k : 8 * k + 8], wide[16 + 8 * k : 24 + 8 * k]
            wnd[k, 0] = own[:, :128]
            wnd[k, 1] = beyond[:, :128]
            for at in (1, 2):
                here = own[:, 128 * at : 128 * at + 128]
                there = beyond[:, 128 * at : 128 * at + 128]
                below = jnp.where(sub == 0, there, pltpu.roll(here, 1, 0))
                above = jnp.where(sub == 7, there, pltpu.roll(here, 7, 0))
                wnd[k, at + 1] = jnp.where(
                    octet < 3, below, jnp.where(octet >= 13, above, here)
                )
            wnd[k, 4] = beyond[:, 384:]

    def portions(c):
        half = depth // 2
        return [(0, half), (half, depth - half)] if c == 0 else [(0, depth)]

    def send_air(c):
        send(
            band_high,
            air[c].at[:, depth],
            air[c].at[:, 0],
            halo_s.at[4],
            halo_r.at[c % 2, 4],
            device(0, band + 1),
        )
        send(
            band_low,
            air[c].at[:, 1],
            air[c].at[:, depth + 1],
            halo_s.at[5],
            halo_r.at[c % 2, 5],
            device(0, band - 1),
        )
        for piece, (start, count) in enumerate(portions(c)):
            send(
                not_final,
                air[c].at[:, pl.ds(1 + start, count), pl.ds(7, 1), :],
                xh.at[c, 0, :, pl.ds(start, count), pl.ds(7, 1), :],
                halo_s.at[2 * piece],
                halo_r.at[c % 2, 2 * piece],
                device(1, band),
            )
            send(
                not_first,
                air[c].at[:, pl.ds(1 + start, count), pl.ds(0, 1), :],
                xh.at[c, 1, :, pl.ds(start, count), pl.ds(0, 1), :],
                halo_s.at[2 * piece + 1],
                halo_r.at[c % 2, 2 * piece + 1],
                device(-1, band),
            )

    def wait_air(c, piece):
        start, count = portions(c)[piece]
        receive(
            not_first,
            xh.at[c, 0, :, pl.ds(start, count), pl.ds(7, 1), :],
            halo_r.at[c % 2, 2 * piece],
            halo_s.at[2 * piece],
            device(-1, band),
        )
        receive(
            not_final,
            xh.at[c, 1, :, pl.ds(start, count), pl.ds(0, 1), :],
            halo_r.at[c % 2, 2 * piece + 1],
            halo_s.at[2 * piece + 1],
            device(1, band),
        )
        if piece == 0:
            receive(
                band_low, air[c].at[:, 0], halo_r.at[c % 2, 4], halo_s.at[4], device(0, band - 1)
            )
            receive(
                band_high,
                air[c].at[:, depth + 1],
                halo_r.at[c % 2, 5],
                halo_s.at[5],
                device(0, band + 1),
            )

    nothing = jnp.zeros((8, width), f32)
    air_copy.wait()

    def first_air(i, carry):
        weight, total_u, total_v = carry
        total_u = total_u + weight * air[0][2, i + 1]
        total_v = total_v + weight * air[0][3, i + 1]
        return weight * f32(col_ratio), total_u, total_v

    _, total_u, total_v = lax.fori_loop(
        0, depth, first_air, (col_base, nothing, nothing), unroll=20
    )

    expected = (
        bands - 1 + bands * (not_first.astype(jnp.int32) + not_final.astype(jnp.int32))
    )
    pl.semaphore_wait(barrier, expected)

    send_air(0)
    send_wind(0, total_u, total_v)

    def reorder(load):
        return jnp.concatenate(
            [
                jnp.concatenate([load(v, pl.ds(q, 8, stride=REFINE)) for v in range(groups)], axis=1)
                for q in range(REFINE)
            ],
            axis=0,
        )

    for copy in fire_copies:
        copy.wait()
    tables[0].wait()
    kinds = reorder(
        lambda v, at: (turned[0, v, at, :] + 16 * turned[1, v, at, :]).astype(f32)
    ).astype(bf16)
    pieces = split(reorder(lambda v, at: stage[0, v, at, :]), 0, 3)
    found = jnp.dot(
        jnp.concatenate([pieces, kinds], axis=0), gather[...], preferred_element_type=f32
    )
    together = found[:rows] + found[rows : 2 * rows] + found[2 * rows : 3 * rows]
    kinds = found[3 * rows :]
    for q in range(REFINE):
        for p in range(SEG):
            kind = kinds[8 * q : 8 * q + 8, 128 * p : 128 * p + 128]
            when = jnp.floor(kind * (1.0 / 16.0))
            now = together[8 * q : 8 * q + 8, 128 * p : 128 * p + 128]
            ign[q, p] = when
            moist[q, p] = kind - 16.0 * when
            xa[q + 1, p] = jnp.where(when <= 0.0, jnp.minimum(now, -1.0), now)

    def find_rate(q, carry):
        for p in range(SEG):
            kind = moist[q, p]
            value = jnp.full((8, 128), t_rate[0], f32)
            for k in range(1, NFUEL):
                value = jnp.where(kind == float(k), t_rate[k], value)
            rate[q + 1, p] = value
        return carry

    lax.fori_loop(0, REFINE, find_rate, 0, unroll=10)

    def outline(e, ref):
        def edge(q, found):
            x = [ref[q + 1, p] for p in range(SEG)]
            near = pltpu.roll(x[SEG - 1], 1, 1)
            for k in range(1, DEEP):
                near = jnp.where(lane == k, pltpu.roll(x[SEG - 1 - k], k + 1, 1), near)
            for k in range(DEEP):
                near = jnp.where(lane == 127 - k, pltpu.roll(x[k], 127 - k, 1), near)
            return jnp.where(octet == q + 3, pltpu.roll(near, 8 * q + 28, 1), found)

        found = lax.fori_loop(0, REFINE, edge, jnp.zeros((8, 128), f32), unroll=10)
        es[e] = found
        gs[e, SEG] = jnp.where(
            sub < 4,
            jnp.broadcast_to(found[7:8], (8, 128)),
            jnp.broadcast_to(found[0:1], (8, 128)),
        )

        def border(p, carry):
            value = rolled(ref[REFINE, p], 1, 0)
            for k in range(1, DEEP):
                value = jnp.where(sub == k, rolled(ref[REFINE - k, p], k + 1, 0), value)
            for k in range(DEEP):
                value = jnp.where(sub == 4 + k, rolled(ref[DEEP - k, p], 4 + k, 0), value)
            gs[e, p] = value
            return carry

        lax.fori_loop(0, SEG, border, 0, unroll=5)

    def fields(c):
        return pl.ds(0, 2) if c == 0 else pl.ds(1 + c, 1)

    def send_outline(c):
        at = fields(c)
        for way, tile_step, ok in ((0, 1, not_final), (1, -1, not_first)):
            part = pl.ds(4 * way, 4)
            send(
                ok,
                gs.at[at, :, part, :],
                hb.at[at, :, part, :],
                fire_s.at[way],
                fire_r.at[c % 2, way],
                device(tile_step, band),
            )
        for side, band_step, ok in ((0, 1, band_high), (1, -1, band_low)):
            send(
                ok,
                es.at[at],
                er.at[at, side],
                fire_s.at[2 + side],
                fire_r.at[c % 2, 2 + side],
                device(0, band + band_step),
            )
            for way, tile_step, also in ((0, 1, not_final), (1, -1, not_first)):
                send(
                    both(ok, also),
                    es.at[at, pl.ds(7 - 7 * way, 1), :],
                    dg.at[at, side, pl.ds(7 * way, 1), :],
                    fire_s.at[4 + 2 * side + way],
                    fire_r.at[c % 2, 4 + 2 * side + way],
                    device(tile_step, band + band_step),
                )

    def wait_outline(c):
        at = fields(c)
        for way, tile_step, ok in ((0, -1, not_first), (1, 1, not_final)):
            receive(
                ok,
                hb.at[at, :, pl.ds(4 * way, 4), :],
                fire_r.at[c % 2, way],
                fire_s.at[way],
                device(tile_step, band),
            )
        for side, band_step, ok in ((0, -1, band_low), (1, 1, band_high)):
            receive(
                ok,
                er.at[at, side],
                fire_r.at[c % 2, 2 + side],
                fire_s.at[2 + side],
                device(0, band + band_step),
            )
            for way, tile_step, also in ((0, -1, not_first), (1, 1, not_final)):
                receive(
                    both(ok, also),
                    dg.at[at, side, pl.ds(7 * way, 1), :],
                    fire_r.at[c % 2, 4 + 2 * side + way],
                    fire_s.at[4 + 2 * side + way],
                    device(tile_step, band + band_step),
                )

    def surround(e, ref):
        for p in range(SEG):
            ref[12, p] = hb[e, p]
        mine, beyond = es[e], hb[e, SEG]

        def strip(here, there):
            below = jnp.where(sub == 0, there, pltpu.roll(here, 1, 0))
            above = jnp.where(sub == 7, there, pltpu.roll(here, 7, 0))
            return jnp.where(
                octet < 3,
                pltpu.roll(below, 48, 1),
                jnp.where(octet >= 13, pltpu.roll(above, 80, 1), here),
            )

        low = strip(jnp.where(inner, mine, er[e, 0]), jnp.where(inner, beyond, dg[e, 0]))
        high = strip(jnp.where(inner, er[e, 1], mine), jnp.where(inner, dg[e, 1], beyond))
        mixed = jnp.where(inner, high, low)
        corner = mixed
        for k in range(3):
            corner = jnp.where(sub == k, rolled(rolled(mixed, 108 + 8 * k, 1), k, 0), corner)
            corner = jnp.where(sub == 7 - k, rolled(rolled(mixed, 20 - 8 * k, 1), -k, 0), corner)
        ref[13, 0] = low
        ref[13, 1] = high
        ref[13, 2] = corner

    outline(0, rate)
    outline(1, xa)
    send_outline(0)

    @pl.when(jnp.logical_not(not_first))
    def _():
        def zero(i, carry):
            for c in range(STEPS):
                for f in range(4):
                    xh[c, 0, f, i] = jnp.zeros((8, width), f32)
            return carry

        lax.fori_loop(0, depth, zero, 0)
        grecv[:, :, :, 7:] = jnp.zeros((STEPS - 1, bands, 2, 1, 128), f32)

    @pl.when(jnp.logical_not(not_final))
    def _():
        grecv[:, :, :, :1] = jnp.zeros((STEPS - 1, bands, 2, 1, 128), f32)

        def zero(i, carry):
            for c in range(STEPS):
                for f in range(4):
                    xh[c, 1, f, i] = jnp.zeros((8, width), f32)
            return carry

        lax.fori_loop(0, depth, zero, 0)

    @pl.when(jnp.logical_not(band_low))
    def _():
        for c in range(STEPS):
            air[c][:, 0] = jnp.zeros((4, 8, width), f32)

    @pl.when(jnp.logical_not(band_high))
    def _():
        for c in range(STEPS):
            air[c][:, depth + 1] = jnp.zeros((4, 8, width), f32)

    column = iota((16, cols), 1)

    def make_spread(i, carry):
        at = pl.ds(pl.multiple_of(i * 16, 16), 16)
        spread[at, :] = indicator(column == SEG * (line16 + 16 * (i % 8)) + i // 8)
        return carry

    source, place = iota((128, 512), 0), iota((128, 512), 1)
    block, place = place // 128, place % 128
    near = place % 8 < 4
    first = jnp.where(block == 0, 32 + place // 2, jnp.where(near, 32, 31))
    second = jnp.where(
        block == 2, jnp.where(near, 96, 95), jnp.where(place < 64, 31, 96)
    )
    pattern = indicator(source == jnp.where(block < 2, first, second), 0.5)
    wmat[:128, :] = pattern
    wmat[128:, :] = pattern
    source, place = iota((128, 128), 0), iota((128, 128), 1)
    pattern = indicator(place == source // 2 + coarse * (band % 2))
    smat[:128, :] = pattern
    smat[128:, :] = pattern

    for copy in tables[1:]:
        copy.wait()

    def lookup(q, carry):
        for p in range(SEG):
            kind = moist[q, p]
            burn = jnp.full((8, 128), t_burn[0], f32)
            hot = jnp.full((8, 128), t_heat[0], f32)
            wet = jnp.full((8, 128), t_moist[0], f32)
            for k in range(1, NFUEL):
                same = kind == float(k)
                burn = jnp.where(same, t_burn[k], burn)
                hot = jnp.where(same, t_heat[k], hot)
                wet = jnp.where(same, t_moist[k], wet)
            binv[q, p] = 1.0 / burn
            heat[q, p] = hot
            moist[q, p] = wet
            bsum[q, p] = jnp.zeros((8, 128), f32)
        return carry

    lax.fori_loop(0, REFINE, lookup, 0)
    fuel_copy.wait()
    pieces = split(reorder(lambda v, at: stage[1, v, at, :]), 0, 3)
    found = jnp.dot(pieces, gather[...], preferred_element_type=f32)
    together = found[:rows] + found[rows : 2 * rows] + found[2 * rows :]
    for q in range(REFINE):
        for p in range(SEG):
            fuel[q, p] = together[8 * q : 8 * q + 8, 128 * p : 128 * p + 128]
    lax.fori_loop(0, cols // 16, make_spread, 0, unroll=4)

    def uphill(d):
        return jnp.maximum(d, 0.0) * d

    def downhill(d):
        return jnp.minimum(d, 0.0) * d

    def moved(here, dw, de, ds, dn, speed, wu, wv):
        square = (uphill(dw) + downhill(de)) + (uphill(ds) + downhill(dn))
        steep = square * lax.rsqrt(jnp.maximum(square, TINY))
        gx, gy = dw + de, ds + dn
        tail = (wu * gx + wv * gy) * lax.rsqrt(gx * gx + gy * gy + 4.0)
        return here - (speed * (1.0 + jnp.maximum(tail, 0.0))) * steep

    def substep(src, dst, fire_step):
        low, high, corner = src[13, 0], src[13, 1], src[13, 2]
        mixed = jnp.where(inner, high, low)
        top, border, bottom = [], [], []
        for p in range(SEG):
            first, final, beyond = src[1, p], src[REFINE, p], src[12, p]
            border.append(beyond)
            top.append(
                jnp.where(
                    edge_w, first, jnp.where(sub == 0, beyond, pltpu.roll(final, 1, 0))
                )
            )
            src[11, p] = jnp.where(
                edge_e, final, jnp.where(sub == 7, beyond, pltpu.roll(first, 7, 0))
            )

        def across(x, outer):
            south = jnp.where(lane == 0, outer, pltpu.roll(x[SEG - 1], 1, 1))
            north = jnp.where(lane == 127, outer, pltpu.roll(x[0], 127, 1))
            south = jnp.where(edge_s, x[0], south)
            north = jnp.where(edge_n, x[SEG - 1], north)
            line = [south] + x + [north]
            return [line[k + 1] - line[k] for k in range(SEG + 1)]

        wu, wv = wnd[0, 0], wnd[1, 0]

        def line(q, carry):
            x, dw = carry
            after = [src[q + 2, p] for p in range(SEG)]
            dh = across(x, pltpu.roll(mixed, 100 - 8 * q, 1))
            de = []
            for p in range(SEG):
                de.append(after[p] - x[p])
                new = moved(
                    x[p], dw[p], de[p], dh[p], dh[p + 1], pace[q + 1, p], wu, wv
                )
                dst[q + 1, p] = new
                bsum[q, p] = bsum[q, p] + jnp.clip(new, -0.5, 0.5)
            return after, de

        x = [src[1, p] for p in range(SEG)]
        lax.fori_loop(0, REFINE, line, (x, [x[p] - top[p] for p in range(SEG)]), unroll=10)

        wu, wv = wnd[0, 1], wnd[1, 1]
        dh = across(border, corner)
        for p in range(SEG):
            here = border[p]
            west = jnp.where(sub == 7, src[REFINE, p], pltpu.roll(here, 7, 0))
            east = jnp.where(sub == 0, src[1, p], pltpu.roll(here, 1, 0))
            dst[12, p] = moved(
                here, here - west, east - here, dh[p], dh[p + 1], pace[12, p], wu, wv
            )
        for k, here in enumerate((low, high)):
            west = jnp.where(strip_w, here, pltpu.roll(here, 8, 1))
            east = jnp.where(strip_e, here, pltpu.roll(here, 120, 1))
            south, north = pltpu.roll(here, 127, 1), pltpu.roll(here, 1, 1)
            dst[13, k] = moved(
                here,
                here - west,
                east - here,
                here - south,
                north - here,
                pace[13, k],
                wnd[0, 2 + k],
                wnd[1, 2 + k],
            )
        west = jnp.where(sub == 7, pltpu.roll(mixed, 28, 1), pltpu.roll(corner, 7, 0))
        east = jnp.where(sub == 0, pltpu.roll(mixed, 100, 1), pltpu.roll(corner, 1, 0))
        south = jnp.where(lane == 127, border[SEG - 1], pltpu.roll(corner, 127, 1))
        north = jnp.where(lane == 0, border[0], pltpu.roll(corner, 1, 1))
        dst[13, 2] = moved(
            corner,
            corner - west,
            east - corner,
            corner - south,
            north - corner,
            pace[13, 2],
            wnd[0, 4],
            wnd[1, 4],
        )

    lane_a = lax.broadcasted_iota(jnp.int32, (8, width), 1)

    def write(c, f, i, value):
        if c == STEPS - 1:
            air_out[f, i] = value
        else:
            air[c + 1][f, i + 1] = value

    def wait_flux(c):
        receive_tile(frecv.at[c, pl.ds(0, bands - 1)], flux_r.at[c % 2], flux_s.at[0])
        return [
            jnp.concatenate(
                [frecv[c, 2 * k, f] + frecv[c, 2 * k + 1, f] for k in range(width // 128)],
                axis=1,
            )
            for f in range(2)
        ]

    def wait_rim(c):
        for way, tile_step, ok in ((0, -1, not_first), (1, 1, not_final)):
            row = pl.ds(7 - 7 * way, 1)
            receive(
                ok,
                grecv.at[c, :, :, row, :],
                rim_r.at[2 + c % 2, way],
                rim_s.at[1, way],
                device(tile_step, 0),
            )
        return [
            jnp.concatenate(
                [grecv[c, 2 * k, f] + grecv[c, 2 * k + 1, f] for k in range(width // 128)],
                axis=1,
            )
            for f in range(2)
        ]

    def force_air(c, flux):
        def force(i, weight):
            for f in range(2):
                now = air_out[f, i] if c == STEPS - 1 else air[c + 1][f, i + 1]
                write(c, f, i, now + weight * flux[f])
            return weight * f32(prof_ratio)

        lax.fori_loop(0, depth, force, prof_base * f32(2.0), unroll=20)

    def move_air(c):
        if c < STEPS - 1:
            drain()
        if c > 0:
            flux = wait_flux(c - 1)
            force_air(c - 1, flux)
        wait_air(c, 0)
        if c > 0:
            low = jnp.where(band_low, prof_base * f32(2.0 / prof_ratio), 0.0)
            high = jnp.where(band_high, prof_base * f32(2.0 * prof_ratio**depth), 0.0)
            for f in range(2):
                air[c][f, 0] = air[c][f, 0] + low * flux[f]
                air[c][f, depth + 1] = air[c][f, depth + 1] + high * flux[f]
        final = c == STEPS - 1

        def update(i, carry):
            weight, total_u, total_v = carry
            u, v = air[c][2, i + 1], air[c][3, i + 1]
            to_w = 0.02 + 0.1 * jnp.maximum(u, 0.0)
            to_e = 0.02 - 0.1 * jnp.minimum(u, 0.0)
            to_s = 0.02 + 0.1 * jnp.maximum(v, 0.0)
            to_n = 0.02 - 0.1 * jnp.minimum(v, 0.0)
            to_here = 0.96 - ((to_w + to_e) + (to_s + to_n))
            to_s = jnp.where(lane_a == 0, 0.0, to_s)
            to_n = jnp.where(lane_a == width - 1, 0.0, to_n)
            lift_x = lift_s = lift_n = None
            for f in range(4):
                here = air[c][f, i + 1]
                west, east = xh[c, 0, f, i], xh[c, 1, f, i]
                west = pltpu.roll(jnp.where(row8 == 7, west, here), 1, 0)
                east = pltpu.roll(jnp.where(row8 == 0, east, here), 7, 0)
                south, north = pltpu.roll(here, 1, 1), pltpu.roll(here, width - 1, 1)
                new = (to_here * here + (to_w * west + to_e * east)) + (
                    (to_s * south + to_n * north) + 0.02 * (air[c][f, i] + air[c][f, i + 2])
                )
                if f == 0:
                    lift_x, lift_s, lift_n = east - west, south, north
                elif f == 1:
                    lift_x = lift_x + 0.6 * (east - west)
                    lift_s = jnp.where(lane_a == 0, 0.0, lift_s + 0.6 * south)
                    lift_n = jnp.where(lane_a == width - 1, 0.0, lift_n + 0.6 * north)
                elif f == 2:
                    new = new + 0.015 * lift_x
                    total_u = total_u + weight * new
                else:
                    new = new + 0.015 * (lift_n - lift_s)
                    total_v = total_v + weight * new
                write(c, f, i, new)
            return weight * f32(col_ratio), total_u, total_v

        carry = (col_base, nothing, nothing)
        for piece, (start, count) in enumerate(portions(c)):
            if piece > 0:
                wait_air(c, piece)
            carry = lax.fori_loop(start, start + count, update, carry, unroll=count)
        _, total_u, total_v = carry
        if c > 0:
            rim = wait_rim(c - 1)
            west = [jnp.where(row8 == 0, pltpu.roll(rim[f], 1, 0), 0.0) for f in range(2)]
            east = [jnp.where(row8 == 7, pltpu.roll(rim[f], 7, 0), 0.0) for f in range(2)]
            push = 0.015 * ((east[0] - west[0]) + 0.6 * (east[1] - west[1]))

            def border(i, carry):
                weight, share, total_u = carry
                u = air[c][2, i + 1]
                to_w = share * (0.02 + 0.1 * jnp.maximum(u, 0.0))
                to_e = share * (0.02 - 0.1 * jnp.minimum(u, 0.0))
                for f in range(2):
                    now = air_out[f, i] if final else air[c + 1][f, i + 1]
                    write(c, f, i, now + (to_w * west[f] + to_e * east[f]))
                more = share * push
                now = air_out[2, i] if final else air[c + 1][2, i + 1]
                write(c, 2, i, now + more)
                return weight * f32(col_ratio), share * f32(prof_ratio), total_u + weight * more

            _, _, total_u = lax.fori_loop(
                0, depth, border, (col_base, prof_base * f32(2.0), total_u), unroll=20
            )
        if not final:
            send_wind(c + 1, total_u, total_v)
            send_air(c + 1)

    def send_rim(c):
        for way, tile_step, ok in ((0, 1, not_final), (1, -1, not_first)):
            row = pl.ds(7 - 7 * way, 1)
            send_group(
                ok,
                [(fsend.at[c, :, row, :], grecv.at[c, band, :, row, :]) for j in range(bands)],
                grecv.at[c, :, :, row, :],
                rim_s.at[1, way],
                rim_r.at[2 + c % 2, way],
                [device(tile_step, j) for j in range(bands)],
            )

    def burn_fire(c, fire_step):
        def burn(q, carry):
            hot, wet = carry
            for p in range(SEG):
                now = fuel[q, p]
                spent = (float(SUBSTEPS) * 0.5 - bsum[q, p]) * binv[q, p]
                remain = now * jnp.exp(-fire_step * spent)
                used = now - remain
                fuel[q, p] = remain
                bsum[q, p] = jnp.zeros((8, 128), f32)
                hot = hot + used * heat[q, p]
                wet = wet + used * moist[q, p]
            return hot, wet

        zero = jnp.zeros((8, 128), f32)
        hot, wet = lax.fori_loop(0, REFINE, burn, (zero, zero), unroll=10)
        flux = jnp.dot(
            split(jnp.concatenate([hot, wet], axis=0), 1, 2),
            smat[...],
            preferred_element_type=f32,
        ) * f32(1.0 / (REFINE * REFINE))
        fsend[c, 0] = flux[:8]
        fsend[c, 1] = flux[8:]
        for j in range(bands):

            @pl.when(band == j)
            def _(j=j):
                frecv[c, j, 0] = flux[:8]
                frecv[c, j, 1] = flux[8:]

        send_tile(
            lambda j: (fsend.at[c], frecv.at[c, band]),
            frecv.at[c, pl.ds(0, bands - 1)],
            flux_s.at[0],
            flux_r.at[c % 2],
        )
        if c < STEPS - 1:
            send_rim(c)

    def burn_window(c):
        fire_step = plan[c].astype(f32) * f32(0.15)
        if c == STEPS - 1:
            drain()
        wait_outline(c)
        if c == 0:
            surround(0, rate)
        surround(1 + c, xa)

        for q in range(1, REFINE + 1):
            for p in range(SEG):
                pace[q, p] = fire_step * rate[q, p]
        for p in range(SEG):
            pace[12, p] = fire_step * rate[12, p]
        for k in range(3):
            pace[13, k] = fire_step * rate[13, k]

        def pair(i, carry):
            substep(xa, xb, fire_step)
            substep(xb, xa, fire_step)
            return carry

        lax.fori_loop(0, SUBSTEPS // 2, pair, 0)
        if c != STEPS - 2:
            burn_fire(c, fire_step)
        if c < STEPS - 1:

            def ignite(q, carry):
                for p in range(SEG):
                    now = xa[q + 1, p]
                    xa[q + 1, p] = jnp.where(
                        ign[q, p] <= float(c + 1), jnp.minimum(now, -1.0), now
                    )
                return carry

            lax.fori_loop(0, REFINE, ignite, 0, unroll=10)
            outline(2 + c, xa)
            send_outline(1 + c)
            if c == STEPS - 2:
                burn_fire(c, fire_step)
            wait_wind(c + 1)

    def give(load, array):
        values = jnp.concatenate(
            [
                jnp.concatenate([load(q, p) for p in range(SEG)], axis=1)
                for q in range(REFINE)
            ],
            axis=0,
        )
        found = jnp.dot(split(values, 0, 3), spread[...], preferred_element_type=f32)
        found = found[:rows] + found[rows : 2 * rows] + found[2 * rows :]
        for q in range(REFINE):
            for v in range(groups):
                array[v, pl.ds(q, 8, stride=REFINE), :] = found[
                    8 * q : 8 * q + 8, 128 * v : 128 * v + 128
                ]

    move_air(0)
    wait_wind(0)
    burn_window(0)
    for c in range(1, STEPS - 1):
        move_air(c)
        burn_window(c)
    burn_window(STEPS - 1)
    give(lambda q, p: xa[q + 1, p], level_out)
    move_air(STEPS - 1)
    give(lambda q, p: fuel[q, p], fuel_out)
    drain()
    force_air(STEPS - 1, wait_flux(STEPS - 1))


def release(air, level, fuel, air_out, level_out, fuel_out, sems):
    for f in range(4):
        pltpu.make_async_copy(air.at[f], air_out.at[f], sems.at[0]).start()
    copies = [pltpu.make_async_copy(air, air, sems.at[0])]
    for k, (held, out) in enumerate(((level, level_out), (fuel, fuel_out))):
        for v in range(held.shape[0]):
            pltpu.make_async_copy(
                held.at[v], out.at[:, pl.ds(128 * v, 128)], sems.at[1 + k]
            ).start()
        copies.append(pltpu.make_async_copy(held, held, sems.at[1 + k]))
    for copy in copies:
        copy.wait()


def solution(mesh):
    tiles, sects, subs = (mesh.shape[name] for name in ("tile", "sect", "sub"))
    bands = sects * subs
    air_spec = P(None, ("sect", "sub"), ("group", "tile"), None)
    fire_spec = P(("group", "tile"), ("sect", "sub"))

    def local(air_state, fire_level, *rest):
        depth, width = air_state.shape[1], air_state.shape[3]
        rows, cols = fire_level.shape
        groups = cols // 128
        assert air_state.shape[2] == 8 and cols == 64 * REFINE and rows == 8 * REFINE
        vmem = pl.BlockSpec(memory_space=pltpu.VMEM)
        hbm = pl.BlockSpec(memory_space=pltpu.HBM)
        dma = pltpu.SemaphoreType.DMA

        def blocks(*lead):
            return pltpu.VMEM((*lead, 8, 128), f32)

        held = pl.pallas_call(
            functools.partial(kernel, tiles, sects, subs),
            out_shape=(
                pltpu.VMEM(air_state.shape, f32),
                pltpu.VMEM((groups, rows, 128), f32),
                pltpu.VMEM((groups, rows, 128), f32),
            ),
            in_specs=[hbm] * 10,
            out_specs=(vmem, vmem, vmem),
            scratch_shapes=[
                pltpu.VMEM((4, depth + 2, 8, width), f32),
                pltpu.VMEM((4, depth + 2, 8, width), f32),
                pltpu.VMEM((4, depth + 2, 8, width), f32),
                pltpu.VMEM((4, depth + 2, 8, width), f32),
                pltpu.VMEM((STEPS, 2, 4, depth, 8, width), f32),
                blocks(14, SEG),
                blocks(14, SEG),
                blocks(14, SEG),
                blocks(14, SEG),
                blocks(REFINE, SEG),
                blocks(REFINE, SEG),
                blocks(REFINE, SEG),
                blocks(REFINE, SEG),
                blocks(REFINE, SEG),
                blocks(REFINE, SEG),
                pltpu.VMEM((2, groups, rows, 128), f32),
                pltpu.VMEM((2, groups, rows, 128), jnp.int32),
                pltpu.VMEM((cols, cols), bf16),
                pltpu.VMEM((cols, cols), bf16),
                pltpu.VMEM((256, 512), bf16),
                pltpu.VMEM((256, 128), bf16),
                blocks(2, 5),
                blocks(STEPS + 1),
                blocks(STEPS + 1, SEG + 1),
                blocks(STEPS + 1, SEG + 1),
                blocks(STEPS + 1, 2),
                blocks(STEPS + 1, 2),
                blocks(STEPS, bands, 2),
                blocks(STEPS, bands, 2),
                blocks(STEPS, bands, 2),
                blocks(STEPS, 2),
                blocks(STEPS, bands, 2),
                blocks(STEPS - 1, bands, 2),
                pltpu.SMEM((STEPS,), jnp.int32),
                pltpu.SMEM((NFUEL,), f32),
                pltpu.SMEM((NFUEL,), f32),
                pltpu.SMEM((NFUEL,), f32),
                pltpu.SMEM((NFUEL,), f32),
                dma((5,)),
                dma((5,)),
                dma((8,)),
                dma((2, 8)),
                dma((1,)),
                dma((2,)),
                dma((1,)),
                dma((2,)),
                dma((2, 2)),
                dma((4, 2)),
                dma((6,)),
                dma((2, 6)),
            ],
            compiler_params=pltpu.CompilerParams(
                collective_id=0, has_side_effects=True, vmem_limit_bytes=56 * 1024 * 1024
            ),
        )(air_state, fire_level, *rest)
        held = [pltpu.with_memory_space_constraint(x, pltpu.VMEM) for x in held]
        return pl.pallas_call(
            release,
            out_shape=(
                jax.ShapeDtypeStruct(air_state.shape, f32),
                jax.ShapeDtypeStruct(fire_level.shape, f32),
                jax.ShapeDtypeStruct(fire_level.shape, f32),
            ),
            in_specs=[vmem] * 3,
            out_specs=(hbm, hbm, hbm),
            scratch_shapes=[dma((3,))],
        )(*held)

    return jax.shard_map(
        local,
        mesh=mesh,
        in_specs=(air_spec, fire_spec, fire_spec, fire_spec, fire_spec) + (P(),) * 5,
        out_specs=(air_spec, fire_spec, fire_spec),
        check_vma=False,
    )
```
